32 devices in a mesh: row: 8 (over z, y), col: 4 (over x, core).
Axes of the slice: x: 2, y: 2, z: 4, core: 2. Of those that a mesh axis runs over, the one named last changes fastest.
Arguments:
- matrix_blocks: bfloat16 [16, 24, 256, 256], P('row', 'col'), may hold values from 0 to 10, as said below
- matrix_rows: int32 [16, 24], P('row', 'col'), may hold values from 0 to 7, as said below
- matrix_counts: int32 [16, 4], P('row', 'col'), may hold values from 0 to 6, as said below
- slab_blocks: bfloat16 [16, 16, 256, 256], P('row', 'col'), may hold values from 0.099609375 to 1
- slab_inner: int32 [16, 16], P('row', 'col'), may hold values from 0 to 15, as said below
- slab_counts: int32 [16], P('row'), may hold values from 8 to 16
Outputs:
- inflated: bfloat16 [16, 32, 256, 256], P('row', 'col')
The draws below stay inside these ranges and needn't reach their ends.
Inputs may be any that keep to these rules, and one draw needn't show every extreme that they name: `matrix_blocks`: entries are positive. `matrix_rows`: the 6 slots of one matrix block column within one index of col name distinct block rows. `matrix_counts`: each row sums to 16; every matrix block column has an index of col where all 6 slots are live. `slab_inner`: the 16 entries of a row are distinct.
All inputs are finite; a program needn't handle non-finite values.
Results may differ from the reference program's by a relative error of at most 0.001.
Values may be sent and summed in bfloat16 or wider, within the bound.
A program may use at most 192 MiB of HBM per device.

```python
import math
import jax
import jax.numpy as jnp
from jax import lax

BS = 256
KB = 16
CAPA = 6
RB_DEV = 8
KW = 16
WB = 16
NBW = 32
N_COL = 4


def draw_matrix_blocks(key, part):
    first, second = jax.random.split(key)
    slots = N_COL * CAPA
    ranges = (jnp.arange(slots) // CAPA).astype(jnp.float32).reshape(1, slots, 1, 1)
    spread = ranges / max(N_COL - 1, 1)
    values = jax.random.uniform(first, (KW, slots, BS, BS), jnp.float32, 0.1, 1.0)
    rising = jnp.sqrt(1.0 + 2.0 * spread)
    row_scale = jnp.exp(jax.random.uniform(second, (KW, slots, BS, 1), jnp.float32, 0.0, math.log(3.2)))
    return (values * row_scale * rising).astype(jnp.bfloat16)


def draw_matrix_rows(key, part):
    starting = jax.random.randint(key, (KW, N_COL, 1), 0, RB_DEV)
    offset = jnp.arange(CAPA, dtype=jnp.int32)[None, None, :]
    placed = (starting + offset) % RB_DEV
    return placed.reshape(KW, N_COL * CAPA).astype(jnp.int32)


def draw_matrix_counts(key, part):
    first, second = jax.random.split(key)
    full_range = jax.random.randint(first, (KW, 1, 1), 0, N_COL)
    scores = jax.random.randint(second, (KW, N_COL, CAPA), 0, 1 << 20)
    sections = jnp.arange(N_COL, dtype=jnp.int32)[None, :, None]
    scores = scores + jnp.where(sections == full_range, 1 << 21, 0)
    flat = scores.reshape(KW, N_COL * CAPA) * (N_COL * CAPA) + jnp.arange(N_COL * CAPA, dtype=jnp.int32)[None, :]
    unused, chosen = jax.lax.top_k(flat, KB)
    owners = chosen // CAPA
    tallies = jnp.sum((owners[:, :, None] == jnp.arange(N_COL, dtype=jnp.int32)[None, None, :]).astype(jnp.int32), axis=1)
    return tallies.astype(jnp.int32)


def permute_one(subkey):
    return jax.random.permutation(subkey, KW)


def draw_slab_inner(key, part):
    subkeys = jax.random.split(key, WB)
    orders = jax.vmap(permute_one)(subkeys)
    return orders[:, :KB].astype(jnp.int32)


def draw_slab_counts(key, part):
    first, second = jax.random.split(key)
    tallies = jax.random.randint(first, (WB,), KB // 2, KB + 1)
    picked = jax.random.randint(second, (), 0, WB)
    return jnp.where(jnp.arange(WB, dtype=jnp.int32) == picked, KB, tallies).astype(jnp.int32)


def shard_levels(rng, extent, shards, low, high):
    loudness = 1.0
    for axis_at, shards_of in shards:
        heights = jax.random.uniform(jax.random.fold_in(jax.random.fold_in(rng, 6), axis_at), (shards_of,), jnp.float32, low / len(shards), high / len(shards))
        loudness = loudness * jnp.repeat(jnp.exp(heights), extent[axis_at] // shards_of).reshape((-1,) + (1,) * (len(extent) - 1 - axis_at))
    return loudness


def setup_inputs(seed: int = 0) -> dict:
    seeds = jax.random.split(jax.random.key(seed), 7)
    matrix_blocks = draw_matrix_blocks(jax.random.fold_in(seeds[6], 71), 0)
    matrix_rows = draw_matrix_rows(jax.random.fold_in(seeds[6], 71), 0)
    matrix_counts = draw_matrix_counts(jax.random.fold_in(seeds[6], 71), 0)
    slab_blocks = jnp.clip(0.099609375 + 0.9003906 * jax.random.uniform(seeds[3], (WB, KB, BS, BS), jnp.float32) ** shard_levels(seeds[3], (WB, KB, BS, BS), ((0, 8), (1, 4)), -0.2, 0.2), 0.099609375, 1.0).astype(jnp.bfloat16)
    slab_inner = draw_slab_inner(jax.random.fold_in(seeds[6], 71), 0)
    slab_counts = draw_slab_counts(jax.random.fold_in(seeds[6], 71), 0)
    return dict(matrix_blocks=matrix_blocks, matrix_rows=matrix_rows, matrix_counts=matrix_counts, slab_blocks=slab_blocks, slab_inner=slab_inner, slab_counts=slab_counts)


def reference(matrix_blocks, matrix_rows, matrix_counts, slab_blocks, slab_inner, slab_counts):
    blocks = matrix_blocks.reshape(KW, N_COL, CAPA, BS, BS)
    block_rows = matrix_rows.reshape(KW, N_COL, CAPA)
    window_index = jnp.arange(RB_DEV, dtype=jnp.int32)
    slot_index = jnp.arange(CAPA, dtype=jnp.int32)
    slab_index = jnp.arange(KB, dtype=jnp.int32)

    def one_column(column):
        inner = slab_inner[column]
        used = slab_index < slab_counts[column]
        right = slab_blocks[column].astype(jnp.float32)

        def one_range(section):
            selected = blocks[inner, section].astype(jnp.float32)
            chosen_rows = block_rows[inner, section]
            chosen_counts = matrix_counts[inner, section]
            active = (slot_index[None, :] < chosen_counts[:, None]) & used[:, None]
            weight = ((chosen_rows[:, :, None] == window_index) & active[:, :, None]).astype(jnp.float32)
            products = jnp.einsum("qtxz,qzy->qtxy", selected, right, precision=lax.Precision.HIGHEST)
            return jnp.einsum("qti,qtxy->ixy", weight, products, precision=lax.Precision.HIGHEST)

        expanded = lax.map(one_range, jnp.arange(N_COL, dtype=jnp.int32))
        squared = expanded * expanded
        sums = jnp.sum(squared, axis=(0, 1, 2))
        factor = (NBW * BS) / sums
        result = (squared * factor[None, None, None, :]).astype(jnp.bfloat16)
        return result.reshape(NBW, BS, BS)

    return lax.map(one_column, jnp.arange(WB, dtype=jnp.int32))
```

```python
import functools

import jax
import jax.numpy as jnp
from jax import lax
from jax.experimental import pallas as pl
from jax.experimental.pallas import tpu as pltpu
from jax.sharding import PartitionSpec as P

RB_DEV = 8
MESH = pl.DeviceIdType.MESH
CHUNKS = 6
PLAIN = CHUNKS - 1
UP, DOWN, SIDE = 0, 1, 2


def step_kernel(n_row, n_col, shape, a_ref, b_ref, rows_ref, counts_ref, inner_ref, slab_counts, out_ref,
                a_all, b_all, rows_all, counts_all, inner_all, rows_s, counts_s, inner_s,
                slot_s, source_s, stage, right, acc, sums_all, result,
                send, recv, b_send, b_recv, m_send, m_recv, s_send, s_recv, local, done):
    columns, slots, per_rank, capacity, block = shape
    each = CHUNKS // per_rank
    size = capacity // each
    n_z = n_row // 2
    r = lax.axis_index("row")
    c = lax.axis_index("col")
    z = lax.div(r, 2)
    y = lax.rem(r, 2)
    other = 1 - y
    beside = 2 * z + other
    has_up = z < n_z - 1
    has_down = z > 0

    barrier = pltpu.get_barrier_semaphore()
    for d in range(1, n_row):
        pl.semaphore_signal(barrier, inc=1, device_id={"row": lax.rem(r + d, n_row)}, device_id_type=MESH)
    for d in range(1, n_col):
        pl.semaphore_signal(barrier, inc=1, device_id={"col": lax.rem(c + d, n_col)}, device_id_type=MESH)
    pl.semaphore_wait(barrier, n_row + n_col - 2)

    def chunk(way, rank, ch, own=False):
        target = {UP: r + 2, DOWN: r - 2, SIDE: beside}[way]
        src = a_ref.at[ch] if own else a_all.at[rank, ch]
        return pltpu.make_async_remote_copy(
            src_ref=src, dst_ref=a_all.at[rank, ch], send_sem=send.at[way, rank, ch],
            recv_sem=recv.at[rank, ch], device_id={"row": target}, device_id_type=MESH)

    def arrived(rank, ch):
        pltpu.make_async_remote_copy(
            src_ref=a_all.at[rank, ch], dst_ref=a_all.at[rank, ch], send_sem=send.at[SIDE, rank, ch],
            recv_sem=recv.at[rank, ch], device_id={"row": beside}, device_id_type=MESH).wait_recv()

    def small(d):
        target = {"row": lax.rem(r + d, n_row)}
        return [
            pltpu.make_async_remote_copy(
                src_ref=src, dst_ref=dst.at[r], send_sem=m_send.at[n, d], recv_sem=m_recv.at[n, d],
                device_id=target, device_id_type=MESH)
            for n, (src, dst) in enumerate(((rows_ref, rows_all), (counts_ref, counts_all)))
        ]

    def slab(d):
        target = {"col": lax.rem(c + d, n_col)}
        return [
            pltpu.make_async_remote_copy(
                src_ref=inner_ref, dst_ref=inner_all.at[c], send_sem=b_send.at[1, d], recv_sem=b_recv.at[1, d],
                device_id=target, device_id_type=MESH),
            pltpu.make_async_remote_copy(
                src_ref=b_ref, dst_ref=b_all.at[c], send_sem=b_send.at[0, d], recv_sem=b_recv.at[0, d],
                device_id=target, device_id_type=MESH),
        ]

    def share(d):
        return pltpu.make_async_remote_copy(
            src_ref=sums_all.at[c], dst_ref=sums_all.at[c], send_sem=s_send.at[d], recv_sem=s_recv.at[d],
            device_id={"col": lax.rem(c + d, n_col)}, device_id_type=MESH)

    for ch in [PLAIN] + list(range(PLAIN)):
        chunk(SIDE, r, ch, True).start()
    for ch in range(CHUNKS):
        @pl.when(has_up)
        def _():
            chunk(UP, r, ch, True).start()

        @pl.when(has_down)
        def _():
            chunk(DOWN, r, ch, True).start()

    for d in range(1, n_row):
        for copy in small(d):
            copy.start()
    for d in range(1, n_col):
        for copy in slab(d):
            copy.start()
    mine = (
        pltpu.make_async_copy(a_ref, a_all.at[r], local.at[0]),
        pltpu.make_async_copy(b_ref, b_all.at[c], local.at[1]),
        pltpu.make_async_copy(rows_ref, rows_all.at[r], local.at[2]),
        pltpu.make_async_copy(counts_ref, counts_all.at[r], local.at[3]),
        pltpu.make_async_copy(inner_ref, inner_all.at[c], local.at[4]),
    )
    for copy in mine:
        copy.start()
    acc[...] = jnp.zeros_like(acc)

    arrived(beside, PLAIN)

    @pl.when(has_up)
    def _():
        chunk(UP, beside, PLAIN).start()

    @pl.when(has_down)
    def _():
        chunk(DOWN, beside, PLAIN).start()

    steps = [(0, ch, True) for ch in range(PLAIN)] + [(0, PLAIN, False), (1, PLAIN, False)]

    def sides(d, work):
        def one(side, carry):
            at = z + d * (2 * side - 1)

            @pl.when((at >= 0) & (at < n_z))
            def _():
                work(at)
            return carry

        lax.fori_loop(0, 2, one, 0)

    def relay(d, extra):
        for n, (flip, ch, cross) in enumerate(steps):
            column = other if flip else y

            @pl.when(z >= d)
            def _():
                rank = 2 * (z - d) + column
                arrived(rank, ch)

                @pl.when(has_up)
                def _():
                    chunk(UP, rank, ch).start()

                if cross:
                    chunk(SIDE, rank, ch).start()

            @pl.when(z + d < n_z)
            def _():
                rank = 2 * (z + d) + column
                arrived(rank, ch)

                @pl.when(has_down)
                def _():
                    chunk(DOWN, rank, ch).start()

                if cross:
                    chunk(SIDE, rank, ch).start()

            for work in extra.get(n, ()):
                work()

    def half(rank, kk):
        k = rank * per_rank + kk
        copy = pltpu.make_async_copy(a_all.at[rank, pl.ds(kk * each, each)], stage, local.at[0])
        copy.start()
        for j in range(columns):
            q = source_s[k, j]
            at = jnp.maximum(q, 0)
            value = b_all[lax.div(at, slots), j * slots + lax.rem(at, slots)]
            right[:, j * block:(j + 1) * block] = jnp.where(q >= 0, value, jnp.zeros_like(value))
        copy.wait()

        def block_row(i, carry):
            t = slot_s[k, i]
            at = jnp.maximum(t, 0)
            value = stage[lax.div(at, size), lax.rem(at, size)]
            left = jnp.where(t >= 0, value, jnp.zeros_like(value))
            rows = pl.ds(pl.multiple_of(i * block, block), block)
            acc[rows, :] += jnp.dot(left, right[...], preferred_element_type=jnp.float32)
            return carry

        lax.fori_loop(0, RB_DEV, block_row, 0, unroll=2)

    def whole(rank):
        def one(kk, carry):
            half(rank, kk)
            return carry

        lax.fori_loop(0, per_rank, one, 0)

    def await_side(rank, first, end):
        for ch in range(first, end):
            arrived(rank, ch)

    def own_whole(at):
        whole(2 * at + y)

    def side_whole(at):
        await_side(2 * at + other, 0, PLAIN)
        whole(2 * at + other)

    def own_half(kk):
        def work(at):
            half(2 * at + y, kk)
        return work

    def side_half(kk):
        def work(at):
            await_side(2 * at + other, kk * each, min(kk * each + each, PLAIN))
            half(2 * at + other, kk)
        return work

    relay(1, {})

    def complete():
        for copy in mine:
            copy.wait()
        for d in range(1, n_row):
            for copy in small(d):
                copy.wait()
        for d in range(1, n_col):
            for copy in slab(d):
                copy.wait()
        for n, (src, dst) in enumerate(((rows_all, rows_s), (counts_all, counts_s), (inner_all, inner_s))):
            copy = pltpu.make_async_copy(src, dst, local.at[5 + n])
            copy.start()
            copy.wait()
        lax.fori_loop(0, n_row, table, 0)

    def table(rank, carry):
        for kk in range(per_rank):
            k = rank * per_rank + kk
            for j in range(columns):
                q = jnp.int32(-1)
                for n in range(n_col * slots):
                    found = (inner_s[n // slots, j, n % slots] == k) & (n < slab_counts[j])
                    q = jnp.where(found, n, q)
                source_s[k, j] = q
            for i in range(RB_DEV):
                t = jnp.int32(-1)
                for n in range(capacity):
                    found = (rows_s[rank, kk, n] == i) & (n < counts_s[rank, 0, kk])
                    t = jnp.where(found, n, t)
                slot_s[k, i] = t
        return carry

    def side_here():
        await_side(beside, 0, PLAIN)
        whole(beside)

    relay(2, {
        0: (complete,),
        1: (lambda: whole(r),),
        2: (side_here,),
        3: (lambda: sides(1, own_whole),),
    })
    sides(1, side_whole)
    sides(2, own_whole)

    def later(d, carry):
        relay(d, {})
        sides(d - 1, side_whole)
        sides(d, own_whole)
        return carry

    lax.fori_loop(3, n_z - 1, later, 0)
    far = n_z - 1

    def side_halves(at):
        side_half(0)(at)
        side_half(1)(at)

    relay(far, {
        each - 1: (lambda: sides(far, own_half(0)), lambda: sides(far - 1, side_halves)),
        CHUNKS - 1: (lambda: sides(far, own_half(1)), lambda: sides(far, side_half(0))),
        CHUNKS: (lambda: sides(far, side_half(1)),),
    })

    def square(i, total):
        rows = pl.ds(pl.multiple_of(i * block, block), block)
        value = acc[rows, :]
        value = value * value
        return total + jnp.sum(value.reshape(block // 8, 8, columns * block), axis=0)

    total = lax.fori_loop(0, RB_DEV, square, jnp.zeros((8, columns * block), jnp.float32))
    sums_all[c] = total
    for d in range(1, n_col):
        share(d).start()

    for ch in range(CHUNKS):
        chunk(SIDE, r, ch, True).wait_send()

        @pl.when(has_up)
        def _():
            chunk(UP, r, ch, True).wait_send()

        @pl.when(has_down)
        def _():
            chunk(DOWN, r, ch, True).wait_send()

    @pl.when(has_up)
    def _():
        chunk(UP, beside, PLAIN).wait_send()

    @pl.when(has_down)
    def _():
        chunk(DOWN, beside, PLAIN).wait_send()

    def drain(d, carry):
        for flip, ch, cross in steps:
            column = other if flip else y

            @pl.when(z >= d)
            def _():
                rank = 2 * (z - d) + column

                @pl.when(has_up)
                def _():
                    chunk(UP, rank, ch).wait_send()

                if cross:
                    chunk(SIDE, rank, ch).wait_send()

            @pl.when(z + d < n_z)
            def _():
                rank = 2 * (z + d) + column

                @pl.when(has_down)
                def _():
                    chunk(DOWN, rank, ch).wait_send()

                if cross:
                    chunk(SIDE, rank, ch).wait_send()
        return carry

    lax.fori_loop(1, n_z, drain, 0)

    for d in range(1, n_col):
        share(d).wait()
    sums = jnp.sum(jnp.sum(sums_all[...], axis=0), axis=0, keepdims=True)
    factor = float(RB_DEV * n_col * block) / sums

    def scale(i, carry):
        rows = pl.ds(pl.multiple_of(i * block, block), block)
        value = acc[rows, :]
        value = (value * value * factor).astype(jnp.bfloat16)
        for j in range(columns):
            result[j, i] = value[:, j * block:(j + 1) * block]
            pltpu.make_async_copy(result.at[j, i], out_ref.at[j, i], done.at[j, i]).start()
        return carry

    lax.fori_loop(0, RB_DEV, scale, 0)

    def finish(i, carry):
        for j in range(columns):
            pltpu.make_async_copy(result.at[j, i], out_ref.at[j, i], done.at[j, i]).wait()
        return carry

    lax.fori_loop(0, RB_DEV, finish, 0)


def on_device(n_row, n_col, matrix_blocks, matrix_rows, matrix_counts, slab_blocks, slab_inner, slab_counts):
    per_rank, capacity, block = matrix_blocks.shape[0], matrix_blocks.shape[1], matrix_blocks.shape[2]
    columns, slots = slab_blocks.shape[0], slab_blocks.shape[1]
    held = per_rank * capacity
    size = held // CHUNKS
    a = matrix_blocks.reshape(CHUNKS, size, block, block)
    b = slab_blocks.reshape(columns * slots, block, block)
    matrix_counts = matrix_counts.reshape(1, per_rank)
    hbm = pl.BlockSpec(memory_space=pltpu.HBM)
    dma = pltpu.SemaphoreType.DMA
    rows_shape, counts_shape, inner_shape = (
        (n_row,) + matrix_rows.shape, (n_row,) + matrix_counts.shape, (n_col,) + slab_inner.shape)
    return pl.pallas_call(
        functools.partial(step_kernel, n_row, n_col, (columns, slots, per_rank, capacity, block)),
        out_shape=jax.ShapeDtypeStruct((columns, RB_DEV, block, block), jnp.bfloat16),
        in_specs=[hbm, hbm, hbm, hbm, hbm, pl.BlockSpec(memory_space=pltpu.SMEM)],
        out_specs=hbm,
        scratch_shapes=[
            pltpu.VMEM((n_row,) + a.shape, a.dtype),
            pltpu.VMEM((n_col,) + b.shape, b.dtype),
            pltpu.VMEM(rows_shape, jnp.int32),
            pltpu.VMEM(counts_shape, jnp.int32),
            pltpu.VMEM(inner_shape, jnp.int32),
            pltpu.SMEM(rows_shape, jnp.int32),
            pltpu.SMEM(counts_shape, jnp.int32),
            pltpu.SMEM(inner_shape, jnp.int32),
            pltpu.SMEM((n_row * per_rank, RB_DEV), jnp.int32),
            pltpu.SMEM((n_row * per_rank, columns), jnp.int32),
            pltpu.VMEM((CHUNKS // per_rank, size, block, block), a.dtype),
            pltpu.VMEM((block, columns * block), b.dtype),
            pltpu.VMEM((RB_DEV * block, columns * block), jnp.float32),
            pltpu.VMEM((n_col, 8, columns * block), jnp.float32),
            pltpu.VMEM((columns, RB_DEV, block, block), jnp.bfloat16),
            dma((3, n_row, CHUNKS)), dma((n_row, CHUNKS)),
            dma((2, n_col)), dma((2, n_col)), dma((2, n_row)), dma((2, n_row)), dma((n_col,)), dma((n_col,)),
            dma((8,)), dma((columns, RB_DEV)),
        ],
        compiler_params=pltpu.CompilerParams(
            collective_id=0, has_side_effects=True, vmem_limit_bytes=63 << 20),
        name="gather_multiply_normalize",
    )(a, b, matrix_rows, matrix_counts, slab_inner, slab_counts)


LIST = 9
OVER = 3
FIRST = LIST - OVER
SLOTS = LIST + OVER
PARTS = 4
LEVELS = 65535.0


def pair_kernel(n_z, shape, a_ref, b_ref, rows_ref, counts_ref, inner_ref, used_ref, counts_in, used_in, out_ref,
                cand, over, over_in, y_out, a_all, a_par, b_all, right, stage, lhs, acc, result,
                sums_acc, sums_all, c_out, c_in, top_out, top_in,
                rows_all, counts_all, counts_par, counts_near, inner_all, used_all,
                rows_s, counts_s, counts_par_s, near_s, inner_s, used_s, slot_s, source_s,
                local, ready, near_send, near_recv, z_send, z_recv, y_send, y_recv, o_send, o_recv,
                x_send, x_recv, p_send, p_recv, b_send, b_recv, m_send, m_recv, c_send, c_recv, s_send, s_recv):
    columns, slots, capacity, block = shape
    half = block // 2
    part = half // PARTS
    wide = columns * block
    r = lax.axis_index("row")
    c = lax.axis_index("col")
    z = lax.div(r, 2)
    y = lax.rem(r, 2)
    x = lax.div(c, 2)
    t = lax.rem(c, 2)
    has_up = z < n_z - 1
    has_down = z > 0
    middle = has_up & has_down
    end = jnp.logical_not(middle)
    c_x = 2 * (1 - x) + t
    c_t = 2 * x + 1 - t
    to_up = {"row": r + 2, "col": c}
    to_down = {"row": r - 2, "col": c}
    to_y = {"row": 2 * z + 1 - y, "col": c}
    to_x = {"row": r, "col": c_x}
    to_core = {"row": r, "col": c_t}

    def remote(src, dst, send_sem, recv_sem, target):
        return pltpu.make_async_remote_copy(
            src_ref=src, dst_ref=dst, send_sem=send_sem, recv_sem=recv_sem,
            device_id=target, device_id_type=MESH)

    near = [(2 * z + (y if d < 4 else 1 - y), lax.rem(c + d, 4)) for d in range(1, 8)]

    barrier = pltpu.get_barrier_semaphore()
    for d in range(1, 2 * n_z):
        pl.semaphore_signal(
            barrier, inc=1, device_id={"row": lax.rem(r + d, 2 * n_z), "col": c}, device_id_type=MESH)
    for d, (row, col) in enumerate(near, 1):
        if d != 4:
            pl.semaphore_signal(barrier, inc=1, device_id={"row": row, "col": col}, device_id_type=MESH)
    pl.semaphore_wait(barrier, 2 * n_z - 1 + 6)

    def give_cand():
        return remote(a_ref.at[1 - t], cand.at[pl.ds(t * capacity, capacity)], near_send.at[0], near_recv.at[0], to_core)

    def take_cand():
        return remote(a_ref.at[1 - t], cand.at[pl.ds((1 - t) * capacity, capacity)], near_send.at[0], near_recv.at[0],
                      to_core)

    def give_near():
        return remote(counts_ref, counts_near, near_send.at[1], near_recv.at[1], to_core)

    def metas(d):
        target = {"row": lax.rem(r + d, 2 * n_z), "col": c}
        return [remote(rows_ref, rows_all.at[r], m_send.at[0, d], m_recv.at[0, d], target),
                remote(counts_ref, counts_all.at[r], m_send.at[1, d], m_recv.at[1, d], target)]

    def inner_to(d):
        side = 0 if d < 4 else 1
        row, col = near[d - 1]
        return remote(inner_ref, inner_all.at[side, c], m_send.at[2, d], m_recv.at[2, d], {"row": row, "col": col})

    def used_to():
        return remote(used_ref, used_all, m_send.at[3, 0], m_recv.at[3, 0], to_y)

    def par_counts():
        return remote(counts_all, counts_par, m_send.at[3, 1], m_recv.at[3, 1], to_core)

    def slab(side, col, j):
        return b_all.at[side, col, j]

    def slab_copy(way, src, side, col, j, target):
        return remote(src, slab(side, col, j), b_send.at[way, side, col, j], b_recv.at[side, col, j], target)

    def slab_own(way, j):
        side, target = {0: (0, to_core), 1: (0, to_x), 2: (1, to_y)}[way]
        return slab_copy(way, b_ref.at[j], side, c, j, target)

    def slab_core(side, col, j):
        return slab_copy(0, slab(side, col, j), side, col, j, to_core)

    def slab_diag(j):
        if j == 0:
            return slab_copy(3, slab(0, c_x, j), 1, c_x, j, to_y)
        return slab_copy(3, slab(1, c, j), 1, c, j, to_x)

    def slab_wait(side, col, j):
        slab_copy(0, slab(side, col, j), side, col, j, to_core).wait_recv()

    def y_copy(m, tail):
        at, size = ((0, FIRST), (FIRST, OVER))[tail]
        return remote(y_out.at[m, pl.ds(at, size)], a_all.at[z, m, y, pl.ds(at, size)],
                      y_send.at[m, tail], y_recv.at[m, tail], to_y)

    def y_wait(m, tail):
        at, size = ((0, FIRST), (FIRST, OVER))[tail]
        remote(y_out.at[m, pl.ds(at, size)], a_all.at[z, m, 1 - y, pl.ds(at, size)],
               y_send.at[m, tail], y_recv.at[m, tail], to_y).wait_recv()

    def over_copy():
        return remote(over, over_in, o_send, o_recv, to_x)

    def z_first(way, m, side, tail):
        at, size = ((0, FIRST), (FIRST, OVER))[tail]
        piece = a_all.at[z, m, side, pl.ds(at, size)]
        return remote(piece, piece, z_send.at[way, z, m, 2 * side + tail], z_recv.at[z, m], (to_up, to_down)[way])

    def z_next(way, rank, m):
        piece = a_all.at[rank, m, :, pl.ds(0, LIST)]
        return remote(piece, piece, z_send.at[way, rank, m, 0], z_recv.at[rank, m], (to_up, to_down)[way])

    def z_wait(rank, m):
        piece = a_all.at[rank, m, :, pl.ds(0, LIST)]
        remote(piece, piece, z_send.at[0, rank, m, 0], z_recv.at[rank, m], to_y).wait_recv()

    def x_copy(rank, m):
        return remote(a_all.at[rank, m, :, pl.ds(FIRST, OVER)], a_all.at[rank, m, :, pl.ds(LIST, OVER)],
                      x_send.at[rank, m], x_recv.at[rank, m], to_x)

    def p_copy(rank, m):
        return remote(a_all.at[rank, m], a_par.at[rank, m], p_send.at[rank, m], p_recv.at[rank, m], to_core)

    def c_copy(m):
        return remote(c_out.at[m], c_in.at[m], c_send.at[m, 0], c_recv.at[m, 0], to_y)

    def top_copy(m):
        return remote(top_out.at[m], top_in.at[m], c_send.at[m, 1], c_recv.at[m, 1], to_y)

    def sums_copy(d):
        row, col = near[d - 1]
        side = 0 if d < 4 else 1
        return remote(sums_acc.at[side], sums_all.at[side, c], s_send.at[d], s_recv.at[d], {"row": row, "col": col})

    def both(m, side, tail, act):
        @pl.when(has_up)
        def _():
            act(z_first(0, m, side, tail))

        @pl.when(has_down)
        def _():
            act(z_first(1, m, side, tail))

    def start(copy):
        copy.start()

    def wait_send(copy):
        copy.wait_send()

    def parts(work):
        def one(m, carry):
            work(m)
            return carry

        lax.fori_loop(0, PARTS, one, 0)

    def rank_of(n):
        low = z < n_z // 2
        at = jnp.where(low, z, n_z - 1 - z)
        rank = n - 1 + jnp.where(n - 1 >= at, 1, 0)
        rank = jnp.where(low, rank, n_z - 1 - rank)
        return jnp.where(n == 0, z, rank)

    mine = [pltpu.make_async_copy(a_ref.at[t], cand.at[pl.ds(t * capacity, capacity)], local.at[0])]
    give_cand().start()
    give_near().start()
    mine[0].start()
    for d in range(1, 2 * n_z):
        for copy in metas(d):
            copy.start()
    for d in range(1, 8):
        inner_to(d).start()
    used_to().start()
    mine += [
        pltpu.make_async_copy(rows_ref, rows_all.at[r], local.at[1]),
        pltpu.make_async_copy(counts_ref, counts_all.at[r], local.at[2]),
        pltpu.make_async_copy(inner_ref, inner_all.at[0, c], local.at[3]),
        pltpu.make_async_copy(b_ref, b_all.at[0, c], local.at[4]),
    ]
    for copy in mine[1:]:
        copy.start()
    acc[...] = jnp.zeros_like(acc)
    sums_acc[...] = jnp.zeros_like(sums_acc)

    give_near().wait_recv()
    fetch = pltpu.make_async_copy(counts_near, near_s, local.at[5])
    fetch.start()
    fetch.wait()
    mine[0].wait()
    take_cand().wait_recv()

    own_count = counts_in[0, t]
    near_count = near_s[0, t]
    first_count = jnp.where(t == 0, own_count, near_count)
    total_count = own_count + near_count

    def place(p):
        return jnp.where(p < first_count, p, capacity + jnp.minimum(jnp.maximum(p - first_count, 0), capacity - 1))

    for p in range(OVER):
        over[p] = cand[place(LIST + p)]
    over_copy().start()

    def rows_at(side, m):
        return pl.ds(pl.multiple_of(side * half + m * part, part), part)

    def pack(p, carry):
        at = place(p)
        for m in range(PARTS):
            a_all[z, m, y, p] = cand[at, rows_at(y, m), :]
            y_out[m, p] = cand[at, rows_at(1 - y, m), :]
        return carry

    def pack_tail(p, carry):
        at = place(FIRST + p)
        keep = total_count > FIRST
        for m in range(PARTS):
            for side, there in ((y, True), (1 - y, False)):
                value = jnp.where(keep, cand[at, rows_at(side, m), :], over_in[p, rows_at(side, m), :])
                if there:
                    a_all[z, m, y, FIRST + p] = value
                else:
                    y_out[m, FIRST + p] = value
        return carry

    lax.fori_loop(0, FIRST, pack, 0)
    for m in range(PARTS):
        y_copy(m, 0).start()
        both(m, y, 0, start)
    for j in range(columns):
        slab_own(1, j).start()
        slab_own(0, j).start()
    for m in range(PARTS):
        y_wait(m, 0)
        both(m, 1 - y, 0, start)
    over_copy().wait_recv()
    lax.fori_loop(0, OVER, pack_tail, 0)
    for m in range(PARTS):
        y_copy(m, 1).start()
        both(m, y, 1, start)
    for j in range(columns):
        slab_own(2, j).start()
    for m in range(PARTS):
        y_wait(m, 1)
        both(m, 1 - y, 1, start)

    def relay(n, m):
        rank = rank_of(n)
        z_wait(rank, m)

        @pl.when((rank < z) & has_up)
        def _():
            z_next(0, rank, m).start()

        @pl.when((rank > z) & has_down)
        def _():
            z_next(1, rank, m).start()

    def near_relay(m):
        relay(1, m)

        @pl.when(middle)
        def _():
            relay(2, m)

    def far_relay(m):
        n = jnp.where(middle, 3, 2)
        relay(n, m)
        x_copy(rank_of(n), m).start()

    def table(k, carry):
        rank = lax.div(k, 2)
        kk = lax.rem(k, 2)
        for side in range(2):
            for j in range(columns):
                limit = used_in[0, j] if side == 0 else used_s[0, j]
                q = jnp.int32(-1)
                for n in range(4 * slots):
                    found = (inner_s[side, n // slots, j, n % slots] == k) & (n < limit)
                    q = jnp.where(found, n, q)
                source_s[k, side * columns + j] = q
        base = jnp.where(t == 1, counts_par_s[rank, 0, kk], 0)
        live = counts_s[rank, 0, kk]
        for i in range(RB_DEV):
            p = jnp.int32(-1)
            for n in range(capacity):
                found = (rows_s[rank, kk, n] == i) & (n < live)
                p = jnp.where(found, n + base, p)
            slot_s[k, i] = p
        return carry

    def complete():
        for copy in mine[1:4]:
            copy.wait()
        for d in range(1, 2 * n_z):
            for copy in metas(d):
                copy.wait()
        par_counts().start()
        for d in range(1, 8):
            inner_to(d).wait()
        used_to().wait()
        par_counts().wait()
        for n, (src, dst) in enumerate((
                (rows_all, rows_s), (counts_all, counts_s), (counts_par, counts_par_s), (inner_all, inner_s),
                (used_all, used_s))):
            pltpu.make_async_copy(src, dst, ready.at[n]).start()
        for n, (src, dst) in enumerate((
                (rows_all, rows_s), (counts_all, counts_s), (counts_par, counts_par_s), (inner_all, inner_s),
                (used_all, used_s))):
            pltpu.make_async_copy(src, dst, ready.at[n]).wait()
        lax.fori_loop(0, 4 * n_z, table, 0)

    near_relay(0)
    near_relay(1)
    complete()
    slab_wait(0, c_x, 0)
    slab_diag(0).start()
    slab_core(0, c_x, 0).start()
    slab_wait(1, c, 0)
    slab_core(1, c, 0).start()
    for m in range(2, PARTS):
        near_relay(m)
    slab_wait(1, c, 1)
    slab_diag(1).start()
    slab_core(1, c, 1).start()
    slab_wait(0, c_x, 1)
    slab_core(0, c_x, 1).start()

    def near_side(m):
        x_copy(z, m).start()
        x_copy(rank_of(1), m).start()

        @pl.when(middle)
        def _():
            x_copy(rank_of(2), m).start()

    parts(near_side)

    def give_core(rank, m):
        x_copy(rank, m).wait_recv()
        p_copy(rank, m).start()

    def near_core(m):
        give_core(z, m)
        give_core(rank_of(1), m)

        @pl.when(middle)
        def _():
            give_core(rank_of(2), m)

    for m in range(PARTS // 2):
        far_relay(m)
    slab_wait(1, c_x, 0)
    slab_core(1, c_x, 0).start()
    slab_wait(1, c_x, 1)
    slab_core(1, c_x, 1).start()
    for m in range(PARTS // 2, PARTS):
        far_relay(m)
    parts(near_core)

    mine[4].wait()
    for j in range(columns):
        for side in range(2):
            for col in (c_t, 2 * (1 - x) + 1 - t):
                slab_wait(side, col, j)

    def gather_right(n, carry):
        rank = lax.div(n, 4)
        side = lax.rem(lax.div(n, 2), 2)
        u = lax.rem(n, 2)
        k = 2 * (2 * rank + side) + jnp.where(u == 0, t, 1 - t)
        rows = pl.ds(pl.multiple_of(lax.rem(n, 4) * block, block), block)
        for s in range(2):
            for j in range(columns):
                q = source_s[k, s * columns + j]
                at = jnp.maximum(q, 0)
                value = b_all[s, lax.div(at, slots), j, lax.rem(at, slots)]
                to = (s * columns + j) * block
                right[rank, rows, to:to + block] = jnp.where(q >= 0, value, jnp.zeros_like(value))
        return carry

    lax.fori_loop(0, 4 * n_z, gather_right, 0)

    def multiply(rank, m):
        p_copy(rank, m).wait_recv()
        for u, source in enumerate((a_all, a_par)):
            for side in range(2):
                stage[u, side] = source[rank, m, side]
        for side in range(2):
            for u in range(2):
                k = 2 * (2 * rank + side) + (t if u == 0 else 1 - t)
                at = (2 * side + u) * block
                for i in range(RB_DEV):
                    p = slot_s[k, i]
                    value = stage[u, side, jnp.maximum(p, 0)]
                    lhs[i * part:(i + 1) * part, at:at + block] = jnp.where(p >= 0, value, jnp.zeros_like(value))
        for n in range(2):
            cols = slice(n * wide, (n + 1) * wide)
            acc[m, :, cols] += jnp.dot(lhs[...], right[rank, :, cols], preferred_element_type=jnp.float32)

    def units(low, high):
        def one(n, carry):
            multiply(rank_of(lax.div(n, PARTS)), lax.rem(n, PARTS))
            return carry

        lax.fori_loop(low * PARTS, high * PARTS, one, 0)

    units(0, 2)

    def far_core(m):
        give_core(rank_of(jnp.where(middle, 3, 2)), m)

    parts(far_core)
    units(2, 3)

    def finish_part(m):
        for n in range(2):
            value = acc[m, :, n * wide:(n + 1) * wide]
            squared = value * value
            sums_acc[n] += jnp.sum(squared.reshape(-1, 8, wide), axis=0)
        value = acc[m, :, wide:]
        top = jnp.maximum(jnp.max(value, axis=0, keepdims=True), 1e-30)
        scaled = value * (LEVELS / top) + 0.5
        coded = jnp.minimum(scaled, LEVELS).astype(jnp.int32)
        word = lax.shift_left(coded[:, :block], jnp.int32(16)) | coded[:, block:]
        c_out[m] = word
        top_out[m] = jnp.broadcast_to(top, (8, wide))
        c_copy(m).start()
        top_copy(m).start()

    def last(m):
        @pl.when(end)
        def _():
            rank = rank_of(3)
            z_wait(rank, m)
            x_copy(rank, m).start()
            give_core(rank, m)

        multiply(rank_of(3), m)
        finish_part(m)

    parts(last)
    for d in range(1, 8):
        sums_copy(d).start()

    give_cand().wait_send()
    give_near().wait_send()
    over_copy().wait_send()
    for way in range(3):
        for j in range(columns):
            slab_own(way, j).wait_send()
    for j in range(columns):
        slab_diag(j).wait_send()
        for side, col in ((0, c_x), (1, c), (1, c_x)):
            slab_core(side, col, j).wait_send()

    def drain(m):
        for tail in range(2):
            y_copy(m, tail).wait_send()
            both(m, 0, tail, wait_send)
            both(m, 1, tail, wait_send)

        def one(rank, carry):
            x_copy(rank, m).wait_send()
            p_copy(rank, m).wait_send()

            @pl.when((rank < z) & has_up)
            def _():
                z_next(0, rank, m).wait_send()

            @pl.when((rank > z) & has_down)
            def _():
                z_next(1, rank, m).wait_send()
            return carry

        lax.fori_loop(0, n_z, one, 0)
        c_copy(m).wait_send()
        top_copy(m).wait_send()

    for d in range(1, 8):
        sums_copy(d).wait()
    sums = sums_acc[0]
    for d in range(1, 8):
        sums = sums + sums_all[0 if d < 4 else 1, near[d - 1][1]]
    factor = float(RB_DEV * 4 * block) / jnp.sum(sums, axis=0, keepdims=True)

    def store(value, m, side):
        value = value.astype(jnp.bfloat16)
        for i in range(RB_DEV):
            for j in range(columns):
                result[j, i, rows_at(side, m), :] = value[i * part:(i + 1) * part, j * block:(j + 1) * block]

    def scale_own(m):
        value = acc[m, :, :wide]
        store(value * value * factor, m, y)

    def scale_other(m):
        c_copy(m).wait_recv()
        top_copy(m).wait_recv()
        word = c_in[m]
        step = top_in[m][0:1, :] * (1.0 / LEVELS)
        upper = lax.shift_right_logical(word, jnp.int32(16)).astype(jnp.float32)
        lower = (word & jnp.int32(65535)).astype(jnp.float32)
        value = jnp.concatenate([upper, lower], axis=1) * step
        store(value * value * factor, m, 1 - y)

    parts(scale_own)
    parts(scale_other)
    flush = pltpu.make_async_copy(result, out_ref, local.at[6])
    flush.start()
    parts(drain)
    flush.wait()


def paired(n_z, matrix_blocks, matrix_rows, matrix_counts, slab_blocks, slab_inner, slab_counts):
    capacity, block = matrix_blocks.shape[1], matrix_blocks.shape[2]
    columns, slots = slab_blocks.shape[0], slab_blocks.shape[1]
    part = block // 2 // PARTS
    counts = matrix_counts.reshape(1, 2)
    used = slab_counts.reshape(1, columns)
    hbm = pl.BlockSpec(memory_space=pltpu.HBM)
    smem = pl.BlockSpec(memory_space=pltpu.SMEM)
    dma = pltpu.SemaphoreType.DMA
    half_word, full = jnp.bfloat16, jnp.float32
    rows_shape, counts_shape, inner_shape = (2 * n_z, 2, capacity), (2 * n_z, 1, 2), (2, 4) + slab_inner.shape
    lists = (n_z, PARTS, 2, SLOTS, part, block)
    vmem = [
        ((2 * capacity, block, block), half_word),
        ((OVER, block, block), half_word),
        ((OVER, block, block), half_word),
        ((PARTS, LIST, part, block), half_word),
        (lists, half_word),
        (lists, half_word),
        ((2, 4) + slab_blocks.shape, half_word),
        ((n_z, 4 * block, 2 * columns * block), half_word),
        ((2, 2, SLOTS, part, block), half_word),
        ((RB_DEV * part, 4 * block), half_word),
        ((PARTS, RB_DEV * part, 2 * columns * block), full),
        ((columns, RB_DEV, block, block), half_word),
        ((2, 8, columns * block), full),
        ((2, 4, 8, columns * block), full),
        ((PARTS, RB_DEV * part, block), jnp.int32),
        ((PARTS, RB_DEV * part, block), jnp.int32),
        ((PARTS, 8, columns * block), full),
        ((PARTS, 8, columns * block), full),
        (rows_shape, jnp.int32), (counts_shape, jnp.int32), (counts_shape, jnp.int32), ((1, 2), jnp.int32),
        (inner_shape, jnp.int32), ((1, columns), jnp.int32),
    ]
    words = [rows_shape, counts_shape, counts_shape, (1, 2), inner_shape, (1, columns),
             (4 * n_z, RB_DEV), (4 * n_z, 2 * columns)]
    sems = [(7,), (5,), (2,), (2,), (2, n_z, PARTS, 4), (n_z, PARTS), (PARTS, 2), (PARTS, 2), None, None,
            (n_z, PARTS), (n_z, PARTS), (n_z, PARTS), (n_z, PARTS), (4, 2, 4, columns), (2, 4, columns),
            (4, 2 * n_z), (4, 2 * n_z), (PARTS, 2), (PARTS, 2), (8,), (8,)]
    return pl.pallas_call(
        functools.partial(pair_kernel, n_z, (columns, slots, capacity, block)),
        out_shape=jax.ShapeDtypeStruct((columns, RB_DEV, block, block), jnp.bfloat16),
        in_specs=[hbm] * 6 + [smem] * 2,
        out_specs=hbm,
        scratch_shapes=[pltpu.VMEM(s, d) for s, d in vmem] + [pltpu.SMEM(s, jnp.int32) for s in words]
        + [dma if s is None else dma(s) for s in sems],
        compiler_params=pltpu.CompilerParams(
            collective_id=1, has_side_effects=True, vmem_limit_bytes=62 << 20),
        name="packed_pair_multiply",
    )(matrix_blocks, slab_blocks, matrix_rows, counts, slab_inner, used, counts, used)


def choose(n_row, n_col, *args):
    if n_row == 8 and n_col == 4 and args[0].shape[0] == 2 and args[0].shape[1] == SLOTS // 2:
        return paired(n_row // 2, *args)
    return on_device(n_row, n_col, *args)


def solution(mesh):
    return jax.shard_map(
        functools.partial(choose, mesh.shape["row"], mesh.shape["col"]),
        mesh=mesh,
        in_specs=(
            P("row", "col", None, None),
            P("row", "col"),
            P("row", "col"),
            P("row", "col", None, None),
            P("row", "col"),
            P("row"),
        ),
        out_specs=P("row", "col", None, None),
        check_vma=False,
    )
```

```python
import functools

import jax
import jax.numpy as jnp
from jax import lax
from jax.experimental import pallas as pl
from jax.experimental.pallas import tpu as pltpu
from jax.sharding import PartitionSpec as P

RB_DEV = 8
MESH = pl.DeviceIdType.MESH
CHUNKS = 6
PLAIN = CHUNKS - 1
UP, DOWN, SIDE = 0, 1, 2


def step_kernel(n_row, n_col, shape, a_ref, b_ref, rows_ref, counts_ref, inner_ref, slab_counts, out_ref,
                a_all, b_all, rows_all, counts_all, inner_all, rows_s, counts_s, inner_s,
                slot_s, source_s, stage, right, acc, sums_all, result,
                send, recv, b_send, b_recv, m_send, m_recv, s_send, s_recv, local, done):
    columns, slots, per_rank, capacity, block = shape
    each = CHUNKS // per_rank
    size = capacity // each
    n_z = n_row // 2
    r = lax.axis_index("row")
    c = lax.axis_index("col")
    z = lax.div(r, 2)
    y = lax.rem(r, 2)
    other = 1 - y
    beside = 2 * z + other
    has_up = z < n_z - 1
    has_down = z > 0

    barrier = pltpu.get_barrier_semaphore()
    for d in range(1, n_row):
        pl.semaphore_signal(barrier, inc=1, device_id={"row": lax.rem(r + d, n_row)}, device_id_type=MESH)
    for d in range(1, n_col):
        pl.semaphore_signal(barrier, inc=1, device_id={"col": lax.rem(c + d, n_col)}, device_id_type=MESH)
    pl.semaphore_wait(barrier, n_row + n_col - 2)

    def chunk(way, rank, ch, own=False):
        target = {UP: r + 2, DOWN: r - 2, SIDE: beside}[way]
        src = a_ref.at[ch] if own else a_all.at[rank, ch]
        return pltpu.make_async_remote_copy(
            src_ref=src, dst_ref=a_all.at[rank, ch], send_sem=send.at[way, rank, ch],
            recv_sem=recv.at[rank, ch], device_id={"row": target}, device_id_type=MESH)

    def arrived(rank, ch):
        pltpu.make_async_remote_copy(
            src_ref=a_all.at[rank, ch], dst_ref=a_all.at[rank, ch], send_sem=send.at[SIDE, rank, ch],
            recv_sem=recv.at[rank, ch], device_id={"row": beside}, device_id_type=MESH).wait_recv()

    def small(d):
        target = {"row": lax.rem(r + d, n_row)}
        return [
            pltpu.make_async_remote_copy(
                src_ref=src, dst_ref=dst.at[r], send_sem=m_send.at[n, d], recv_sem=m_recv.at[n, d],
                device_id=target, device_id_type=MESH)
            for n, (src, dst) in enumerate(((rows_ref, rows_all), (counts_ref, counts_all)))
        ]

    def slab(d):
        target = {"col": lax.rem(c + d, n_col)}
        return [
            pltpu.make_async_remote_copy(
                src_ref=inner_ref, dst_ref=inner_all.at[c], send_sem=b_send.at[1, d], recv_sem=b_recv.at[1, d],
                device_id=target, device_id_type=MESH),
            pltpu.make_async_remote_copy(
                src_ref=b_ref, dst_ref=b_all.at[c], send_sem=b_send.at[0, d], recv_sem=b_recv.at[0, d],
                device_id=target, device_id_type=MESH),
        ]

    def share(d):
        return pltpu.make_async_remote_copy(
            src_ref=sums_all.at[c], dst_ref=sums_all.at[c], send_sem=s_send.at[d], recv_sem=s_recv.at[d],
            device_id={"col": lax.rem(c + d, n_col)}, device_id_type=MESH)

    for ch in [PLAIN] + list(range(PLAIN)):
        chunk(SIDE, r, ch, True).start()
    for ch in range(CHUNKS):
        @pl.when(has_up)
        def _():
            chunk(UP, r, ch, True).start()

        @pl.when(has_down)
        def _():
            chunk(DOWN, r, ch, True).start()

    for d in range(1, n_row):
        for copy in small(d):
            copy.start()
    for d in range(1, n_col):
        for copy in slab(d):
            copy.start()
    mine = (
        pltpu.make_async_copy(a_ref, a_all.at[r], local.at[0]),
        pltpu.make_async_copy(b_ref, b_all.at[c], local.at[1]),
        pltpu.make_async_copy(rows_ref, rows_all.at[r], local.at[2]),
        pltpu.make_async_copy(counts_ref, counts_all.at[r], local.at[3]),
        pltpu.make_async_copy(inner_ref, inner_all.at[c], local.at[4]),
    )
    for copy in mine:
        copy.start()
    acc[...] = jnp.zeros_like(acc)

    arrived(beside, PLAIN)

    @pl.when(has_up)
    def _():
        chunk(UP, beside, PLAIN).start()

    @pl.when(has_down)
    def _():
        chunk(DOWN, beside, PLAIN).start()

    steps = [(0, ch, True) for ch in range(PLAIN)] + [(0, PLAIN, False), (1, PLAIN, False)]

    def sides(d, work):
        def one(side, carry):
            at = z + d * (2 * side - 1)

            @pl.when((at >= 0) & (at < n_z))
            def _():
                work(at)
            return carry

        lax.fori_loop(0, 2, one, 0)

    def relay(d, extra):
        for n, (flip, ch, cross) in enumerate(steps):
            column = other if flip else y

            @pl.when(z >= d)
            def _():
                rank = 2 * (z - d) + column
                arrived(rank, ch)

                @pl.when(has_up)
                def _():
                    chunk(UP, rank, ch).start()

                if cross:
                    chunk(SIDE, rank, ch).start()

            @pl.when(z + d < n_z)
            def _():
                rank = 2 * (z + d) + column
                arrived(rank, ch)

                @pl.when(has_down)
                def _():
                    chunk(DOWN, rank, ch).start()

                if cross:
                    chunk(SIDE, rank, ch).start()

            for work in extra.get(n, ()):
                work()

    def half(rank, kk):
        k = rank * per_rank + kk
        copy = pltpu.make_async_copy(a_all.at[rank, pl.ds(kk * each, each)], stage, local.at[0])
        copy.start()
        for j in range(columns):
            q = source_s[k, j]
            at = jnp.maximum(q, 0)
            value = b_all[lax.div(at, slots), j * slots + lax.rem(at, slots)]
            right[:, j * block:(j + 1) * block] = jnp.where(q >= 0, value, jnp.zeros_like(value))
        copy.wait()

        def block_row(i, carry):
            t = slot_s[k, i]
            at = jnp.maximum(t, 0)
            value = stage[lax.div(at, size), lax.rem(at, size)]
            left = jnp.where(t >= 0, value, jnp.zeros_like(value))
            rows = pl.ds(pl.multiple_of(i * block, block), block)
            acc[rows, :] += jnp.dot(left, right[...], preferred_element_type=jnp.float32)
            return carry

        lax.fori_loop(0, RB_DEV, block_row, 0, unroll=2)

    def whole(rank):
        def one(kk, carry):
            half(rank, kk)
            return carry

        lax.fori_loop(0, per_rank, one, 0)

    def await_side(rank, first, end):
        for ch in range(first, end):
            arrived(rank, ch)

    def own_whole(at):
        whole(2 * at + y)

    def side_whole(at):
        await_side(2 * at + other, 0, PLAIN)
        whole(2 * at + other)

    def own_half(kk):
        def work(at):
            half(2 * at + y, kk)
        return work

    def side_half(kk):
        def work(at):
            await_side(2 * at + other, kk * each, min(kk * each + each, PLAIN))
            half(2 * at + other, kk)
        return work

    relay(1, {})

    def complete():
        for copy in mine:
            copy.wait()
        for d in range(1, n_row):
            for copy in small(d):
                copy.wait()
        for d in range(1, n_col):
            for copy in slab(d):
                copy.wait()
        for n, (src, dst) in enumerate(((rows_all, rows_s), (counts_all, counts_s), (inner_all, inner_s))):
            copy = pltpu.make_async_copy(src, dst, local.at[5 + n])
            copy.start()
            copy.wait()
        lax.fori_loop(0, n_row, table, 0)

    def table(rank, carry):
        for kk in range(per_rank):
            k = rank * per_rank + kk
            for j in range(columns):
                q = jnp.int32(-1)
                for n in range(n_col * slots):
                    found = (inner_s[n // slots, j, n % slots] == k) & (n < slab_counts[j])
                    q = jnp.where(found, n, q)
                source_s[k, j] = q
            for i in range(RB_DEV):
                t = jnp.int32(-1)
                for n in range(capacity):
                    found = (rows_s[rank, kk, n] == i) & (n < counts_s[rank, 0, kk])
                    t = jnp.where(found, n, t)
                slot_s[k, i] = t
        return carry

    def side_here():
        await_side(beside, 0, PLAIN)
        whole(beside)

    relay(2, {
        0: (complete,),
        1: (lambda: whole(r),),
        2: (side_here,),
        3: (lambda: sides(1, own_whole),),
    })
    sides(1, side_whole)
    sides(2, own_whole)

    def later(d, carry):
        relay(d, {})
        sides(d - 1, side_whole)
        sides(d, own_whole)
        return carry

    lax.fori_loop(3, n_z - 1, later, 0)
    far = n_z - 1

    def side_halves(at):
        side_half(0)(at)
        side_half(1)(at)

    relay(far, {
        each - 1: (lambda: sides(far, own_half(0)), lambda: sides(far - 1, side_halves)),
        CHUNKS - 1: (lambda: sides(far, own_half(1)), lambda: sides(far, side_half(0))),
        CHUNKS: (lambda: sides(far, side_half(1)),),
    })

    def square(i, total):
        rows = pl.ds(pl.multiple_of(i * block, block), block)
        value = acc[rows, :]
        value = value * value
        return total + jnp.sum(value.reshape(block // 8, 8, columns * block), axis=0)

    total = lax.fori_loop(0, RB_DEV, square, jnp.zeros((8, columns * block), jnp.float32))
    sums_all[c] = total
    for d in range(1, n_col):
        share(d).start()

    for ch in range(CHUNKS):
        chunk(SIDE, r, ch, True).wait_send()

        @pl.when(has_up)
        def _():
            chunk(UP, r, ch, True).wait_send()

        @pl.when(has_down)
        def _():
            chunk(DOWN, r, ch, True).wait_send()

    @pl.when(has_up)
    def _():
        chunk(UP, beside, PLAIN).wait_send()

    @pl.when(has_down)
    def _():
        chunk(DOWN, beside, PLAIN).wait_send()

    def drain(d, carry):
        for flip, ch, cross in steps:
            column = other if flip else y

            @pl.when(z >= d)
            def _():
                rank = 2 * (z - d) + column

                @pl.when(has_up)
                def _():
                    chunk(UP, rank, ch).wait_send()

                if cross:
                    chunk(SIDE, rank, ch).wait_send()

            @pl.when(z + d < n_z)
            def _():
                rank = 2 * (z + d) + column

                @pl.when(has_down)
                def _():
                    chunk(DOWN, rank, ch).wait_send()

                if cross:
                    chunk(SIDE, rank, ch).wait_send()
        return carry

    lax.fori_loop(1, n_z, drain, 0)

    for d in range(1, n_col):
        share(d).wait()
    sums = jnp.sum(jnp.sum(sums_all[...], axis=0), axis=0, keepdims=True)
    factor = float(RB_DEV * n_col * block) / sums

    def scale(i, carry):
        rows = pl.ds(pl.multiple_of(i * block, block), block)
        value = acc[rows, :]
        value = (value * value * factor).astype(jnp.bfloat16)
        for j in range(columns):
            result[j, i] = value[:, j * block:(j + 1) * block]
            pltpu.make_async_copy(result.at[j, i], out_ref.at[j, i], done.at[j, i]).start()
        return carry

    lax.fori_loop(0, RB_DEV, scale, 0)

    def finish(i, carry):
        for j in range(columns):
            pltpu.make_async_copy(result.at[j, i], out_ref.at[j, i], done.at[j, i]).wait()
        return carry

    lax.fori_loop(0, RB_DEV, finish, 0)


def on_device(n_row, n_col, matrix_blocks, matrix_rows, matrix_counts, slab_blocks, slab_inner, slab_counts):
    per_rank, capacity, block = matrix_blocks.shape[0], matrix_blocks.shape[1], matrix_blocks.shape[2]
    columns, slots = slab_blocks.shape[0], slab_blocks.shape[1]
    held = per_rank * capacity
    size = held // CHUNKS
    a = matrix_blocks.reshape(CHUNKS, size, block, block)
    b = slab_blocks.reshape(columns * slots, block, block)
    matrix_counts = matrix_counts.reshape(1, per_rank)
    hbm = pl.BlockSpec(memory_space=pltpu.HBM)
    dma = pltpu.SemaphoreType.DMA
    rows_shape, counts_shape, inner_shape = (
        (n_row,) + matrix_rows.shape, (n_row,) + matrix_counts.shape, (n_col,) + slab_inner.shape)
    return pl.pallas_call(
        functools.partial(step_kernel, n_row, n_col, (columns, slots, per_rank, capacity, block)),
        out_shape=jax.ShapeDtypeStruct((columns, RB_DEV, block, block), jnp.bfloat16),
        in_specs=[hbm, hbm, hbm, hbm, hbm, pl.BlockSpec(memory_space=pltpu.SMEM)],
        out_specs=hbm,
        scratch_shapes=[
            pltpu.VMEM((n_row,) + a.shape, a.dtype),
            pltpu.VMEM((n_col,) + b.shape, b.dtype),
            pltpu.VMEM(rows_shape, jnp.int32),
            pltpu.VMEM(counts_shape, jnp.int32),
            pltpu.VMEM(inner_shape, jnp.int32),
            pltpu.SMEM(rows_shape, jnp.int32),
            pltpu.SMEM(counts_shape, jnp.int32),
            pltpu.SMEM(inner_shape, jnp.int32),
            pltpu.SMEM((n_row * per_rank, RB_DEV), jnp.int32),
            pltpu.SMEM((n_row * per_rank, columns), jnp.int32),
            pltpu.VMEM((CHUNKS // per_rank, size, block, block), a.dtype),
            pltpu.VMEM((block, columns * block), b.dtype),
            pltpu.VMEM((RB_DEV * block, columns * block), jnp.float32),
            pltpu.VMEM((n_col, 8, columns * block), jnp.float32),
            pltpu.VMEM((columns, RB_DEV, block, block), jnp.bfloat16),
            dma((3, n_row, CHUNKS)), dma((n_row, CHUNKS)),
            dma((2, n_col)), dma((2, n_col)), dma((2, n_row)), dma((2, n_row)), dma((n_col,)), dma((n_col,)),
            dma((8,)), dma((columns, RB_DEV)),
        ],
        compiler_params=pltpu.CompilerParams(
            collective_id=0, has_side_effects=True, vmem_limit_bytes=63 << 20),
        name="gather_multiply_normalize",
    )(a, b, matrix_rows, matrix_counts, slab_inner, slab_counts)


LIST = 9
OVER = 3
FIRST = LIST - OVER
SLOTS = LIST + OVER
GRAIN = 16
PARTS = (2, 2, 2, 1, 1)
LEVELS = 65535.0


def pair_kernel(n_z, shape, a_ref, b_ref, rows_ref, counts_ref, inner_ref, used_ref, counts_in, used_in, out_ref,
                cand, over, over_in, y_out, a_all, a_par, b_all, right, stage, lhs, acc, result,
                sums_acc, sums_all, c_out, c_in, top_out, top_in,
                rows_all, counts_all, counts_par, counts_near, inner_all, used_all,
                rows_s, counts_s, counts_par_s, near_s, inner_s, used_s, slot_s, source_s,
                local, ready, near_send, near_recv, z_send, z_recv, y_send, y_recv, o_send, o_recv,
                over_y, x_send, x_recv, p_send, p_recv, b_send, b_recv, m_send, m_recv, c_send, c_recv, s_send, s_recv):
    columns, slots, capacity, block = shape
    half = block // 2
    starts = [sum(PARTS[:m]) for m in range(len(PARTS))]
    span = [pl.ds(first, size) for first, size in zip(starts, PARTS)]
    every = range(len(PARTS))
    wide = columns * block
    r = lax.axis_index("row")
    c = lax.axis_index("col")
    z = lax.div(r, 2)
    y = lax.rem(r, 2)
    x = lax.div(c, 2)
    t = lax.rem(c, 2)
    has_up = z < n_z - 1
    has_down = z > 0
    middle = has_up & has_down
    end = jnp.logical_not(middle)
    c_x = 2 * (1 - x) + t
    c_t = 2 * x + 1 - t
    to_up = {"row": r + 2, "col": c}
    to_down = {"row": r - 2, "col": c}
    to_y = {"row": 2 * z + 1 - y, "col": c}
    to_x = {"row": r, "col": c_x}
    to_core = {"row": r, "col": c_t}

    def remote(src, dst, send_sem, recv_sem, target):
        return pltpu.make_async_remote_copy(
            src_ref=src, dst_ref=dst, send_sem=send_sem, recv_sem=recv_sem,
            device_id=target, device_id_type=MESH)

    near = [(2 * z + (y if d < 4 else 1 - y), lax.rem(c + d, 4)) for d in range(1, 8)]

    barrier = pltpu.get_barrier_semaphore()
    for d in range(1, 2 * n_z):
        pl.semaphore_signal(
            barrier, inc=1, device_id={"row": lax.rem(r + d, 2 * n_z), "col": c}, device_id_type=MESH)
    for d, (row, col) in enumerate(near, 1):
        if d != 4:
            pl.semaphore_signal(barrier, inc=1, device_id={"row": row, "col": col}, device_id_type=MESH)
    pl.semaphore_wait(barrier, 2 * n_z - 1 + 6)

    def give_cand():
        return remote(a_ref.at[1 - t], cand.at[pl.ds(t * capacity, capacity)], near_send.at[0], near_recv.at[0], to_core)

    def take_cand():
        return remote(a_ref.at[1 - t], cand.at[pl.ds((1 - t) * capacity, capacity)], near_send.at[0], near_recv.at[0],
                      to_core)

    def give_near():
        return remote(counts_ref, counts_near, near_send.at[1], near_recv.at[1], to_core)

    def metas(d):
        target = {"row": lax.rem(r + d, 2 * n_z), "col": c}
        return [remote(rows_ref, rows_all.at[r], m_send.at[0, d], m_recv.at[0, d], target),
                remote(counts_ref, counts_all.at[r], m_send.at[1, d], m_recv.at[1, d], target)]

    def inner_to(d):
        side = 0 if d < 4 else 1
        row, col = near[d - 1]
        return remote(inner_ref, inner_all.at[side, c], m_send.at[2, d], m_recv.at[2, d], {"row": row, "col": col})

    def used_to():
        return remote(used_ref, used_all, m_send.at[3, 0], m_recv.at[3, 0], to_y)

    def par_counts():
        return remote(counts_all, counts_par, m_send.at[3, 1], m_recv.at[3, 1], to_core)

    def slab(side, col, j):
        return b_all.at[side, col, j]

    def slab_copy(way, src, side, col, j, target):
        return remote(src, slab(side, col, j), b_send.at[way, side, col, j], b_recv.at[side, col, j], target)

    def slab_own(way, j):
        side, target = {0: (0, to_core), 1: (0, to_x), 2: (1, to_y)}[way]
        return slab_copy(way, b_ref.at[j], side, c, j, target)

    def slab_core(side, col, j):
        return slab_copy(0, slab(side, col, j), side, col, j, to_core)

    def slab_diag(j):
        if j == 0:
            return slab_copy(3, slab(0, c_x, j), 1, c_x, j, to_y)
        return slab_copy(3, slab(1, c, j), 1, c, j, to_x)

    def slab_wait(side, col, j):
        slab_copy(0, slab(side, col, j), side, col, j, to_core).wait_recv()

    def y_copy(m, tail):
        at, size = ((0, FIRST), (FIRST, OVER))[tail]
        return remote(y_out.at[span[m], pl.ds(at, size)], a_all.at[z, span[m], y, pl.ds(at, size)],
                      y_send.at[m, tail], y_recv.at[m, tail], to_y)

    def y_wait(m, tail):
        at, size = ((0, FIRST), (FIRST, OVER))[tail]
        remote(y_out.at[span[m], pl.ds(at, size)], a_all.at[z, span[m], 1 - y, pl.ds(at, size)],
               y_send.at[m, tail], y_recv.at[m, tail], to_y).wait_recv()

    def y_over(to):
        return remote(y_out.at[:, pl.ds(LIST, OVER)], a_all.at[z, :, to, pl.ds(LIST, OVER)],
                      over_y.at[0], over_y.at[1], to_y)

    def over_copy():
        return remote(over, over_in, o_send, o_recv, to_x)

    def z_first(way, m, side, tail):
        at, size = ((0, FIRST), (FIRST, OVER))[tail]
        piece = a_all.at[z, span[m], side, pl.ds(at, size)]
        return remote(piece, piece, z_send.at[way, z, m, 2 * side + tail], z_recv.at[z, m], (to_up, to_down)[way])

    def z_next(way, rank, m):
        piece = a_all.at[rank, span[m], :, pl.ds(0, LIST)]
        return remote(piece, piece, z_send.at[way, rank, m, 0], z_recv.at[rank, m], (to_up, to_down)[way])

    def z_wait(rank, m):
        piece = a_all.at[rank, span[m], :, pl.ds(0, LIST)]
        remote(piece, piece, z_send.at[0, rank, m, 0], z_recv.at[rank, m], to_y).wait_recv()

    def x_copy(rank, m):
        return remote(a_all.at[rank, span[m], :, pl.ds(FIRST, OVER)], a_all.at[rank, span[m], :, pl.ds(LIST, OVER)],
                      x_send.at[rank, m], x_recv.at[rank, m], to_x)

    def p_copy(rank, m, over_part):
        piece = (rank, span[m], slice(None), (pl.ds(0, LIST), pl.ds(LIST, OVER))[over_part])
        return remote(a_all.at[piece], a_par.at[piece], p_send.at[rank, m, over_part], p_recv.at[rank, m, over_part],
                      to_core)

    def c_copy(m):
        return remote(c_out.at[span[m]], c_in.at[span[m]], c_send.at[m, 0], c_recv.at[m, 0], to_y)

    def top_copy(m):
        return remote(top_out.at[m], top_in.at[m], c_send.at[m, 1], c_recv.at[m, 1], to_y)

    def sums_copy(d):
        row, col = near[d - 1]
        side = 0 if d < 4 else 1
        return remote(sums_acc.at[side], sums_all.at[side, c], s_send.at[d], s_recv.at[d], {"row": row, "col": col})

    def both(m, side, tail, act):
        @pl.when(has_up)
        def _():
            act(z_first(0, m, side, tail))

        @pl.when(has_down)
        def _():
            act(z_first(1, m, side, tail))

    def start(copy):
        copy.start()

    def wait_send(copy):
        copy.wait_send()

    def rank_of(n):
        low = z < n_z // 2
        at = jnp.where(low, z, n_z - 1 - z)
        rank = n - 1 + jnp.where(n - 1 >= at, 1, 0)
        rank = jnp.where(low, rank, n_z - 1 - rank)
        return jnp.where(n == 0, z, rank)

    mine = [pltpu.make_async_copy(a_ref.at[t], cand.at[pl.ds(t * capacity, capacity)], local.at[0])]
    give_cand().start()
    give_near().start()
    mine[0].start()
    mine += [
        pltpu.make_async_copy(rows_ref, rows_all.at[r], local.at[1]),
        pltpu.make_async_copy(counts_ref, counts_all.at[r], local.at[2]),
        pltpu.make_async_copy(inner_ref, inner_all.at[0, c], local.at[3]),
        pltpu.make_async_copy(b_ref, b_all.at[0, c], local.at[4]),
    ]
    acc[...] = jnp.zeros_like(acc)
    sums_acc[...] = jnp.zeros_like(sums_acc)

    give_near().wait_recv()
    fetch = pltpu.make_async_copy(counts_near, near_s, local.at[5])
    fetch.start()
    fetch.wait()
    mine[0].wait()
    take_cand().wait_recv()

    own_count = counts_in[0, t]
    near_count = near_s[0, t]
    first_count = jnp.where(t == 0, own_count, near_count)
    total_count = own_count + near_count

    def place(p):
        return jnp.where(p < first_count, p, capacity + jnp.minimum(jnp.maximum(p - first_count, 0), capacity - 1))

    for p in range(OVER):
        over[p] = cand[place(LIST + p)]
    over_copy().start()

    def rows_at(side, m):
        return pl.ds(pl.multiple_of(side * half + m * GRAIN, GRAIN), GRAIN)

    grains = half // GRAIN

    def pack(p, carry):
        at = place(p)
        for g in range(grains):
            a_all[z, g, y, p] = cand[at, rows_at(y, g), :]
            y_out[g, p] = cand[at, rows_at(1 - y, g), :]
        return carry

    def pack_tail(p, carry):
        at = place(FIRST + p)
        keep = total_count > FIRST
        for g in range(grains):
            for side, there in ((y, True), (1 - y, False)):
                value = jnp.where(keep, cand[at, rows_at(side, g), :], over_in[p, rows_at(side, g), :])
                if there:
                    a_all[z, g, y, FIRST + p] = value
                else:
                    y_out[g, FIRST + p] = value
        return carry

    def pack_over(p, carry):
        for g in range(grains):
            a_all[z, g, y, LIST + p] = over[p, rows_at(y, g), :]
            y_out[g, LIST + p] = over[p, rows_at(1 - y, g), :]
        return carry

    lax.fori_loop(0, FIRST, pack, 0)
    for m in every:
        y_copy(m, 0).start()
        both(m, y, 0, start)
    slab_own(1, 0).start()
    for j in range(columns):
        slab_own(0, j).start()
    for d in range(1, 2 * n_z):
        for copy in metas(d):
            copy.start()
    for d in range(1, 8):
        inner_to(d).start()
    used_to().start()
    for copy in mine[1:]:
        copy.start()
    lax.fori_loop(0, OVER, pack_over, 0)
    for m in every:
        y_wait(m, 0)
        both(m, 1 - y, 0, start)
    over_copy().wait_recv()
    lax.fori_loop(0, OVER, pack_tail, 0)
    for m in every:
        y_copy(m, 1).start()
        both(m, y, 1, start)
    slab_own(1, 1).start()
    slab_own(2, 1).start()
    for m in every:
        y_wait(m, 1)
        both(m, 1 - y, 1, start)
        p_copy(z, m, 0).start()
    slab_own(2, 0).start()

    def relay(n, m):
        rank = rank_of(n)
        z_wait(rank, m)

        @pl.when((rank < z) & has_up)
        def _():
            z_next(0, rank, m).start()

        @pl.when((rank > z) & has_down)
        def _():
            z_next(1, rank, m).start()

        p_copy(rank, m, 0).start()

    def near_x(m):
        x_copy(rank_of(1), m).start()

        @pl.when(middle)
        def _():
            x_copy(rank_of(2), m).start()

    def near_relay(m):
        relay(1, m)

        @pl.when(middle)
        def _():
            relay(2, m)

    def far_relay(m):
        relay(jnp.where(middle, 3, 2), m)

    def far_x(m):
        x_copy(rank_of(jnp.where(middle, 3, 2)), m).start()

    def table(k, carry):
        rank = lax.div(k, 2)
        kk = lax.rem(k, 2)
        for side in range(2):
            for j in range(columns):
                limit = used_in[0, j] if side == 0 else used_s[0, j]
                q = jnp.int32(-1)
                for n in range(4 * slots):
                    found = (inner_s[side, n // slots, j, n % slots] == k) & (n < limit)
                    q = jnp.where(found, n, q)
                source_s[k, side * columns + j] = q
        base = jnp.where(t == 1, counts_par_s[rank, 0, kk], 0)
        live = counts_s[rank, 0, kk]
        for i in range(RB_DEV):
            p = jnp.int32(-1)
            for n in range(capacity):
                found = (rows_s[rank, kk, n] == i) & (n < live)
                p = jnp.where(found, n + base, p)
            slot_s[k, i] = p
        return carry

    def complete():
        for copy in mine[1:4]:
            copy.wait()
        for d in range(1, 2 * n_z):
            for copy in metas(d):
                copy.wait()
        par_counts().start()
        for d in range(1, 8):
            inner_to(d).wait()
        used_to().wait()
        par_counts().wait()
        for n, (src, dst) in enumerate((
                (rows_all, rows_s), (counts_all, counts_s), (counts_par, counts_par_s), (inner_all, inner_s),
                (used_all, used_s))):
            pltpu.make_async_copy(src, dst, ready.at[n]).start()
        for n, (src, dst) in enumerate((
                (rows_all, rows_s), (counts_all, counts_s), (counts_par, counts_par_s), (inner_all, inner_s),
                (used_all, used_s))):
            pltpu.make_async_copy(src, dst, ready.at[n]).wait()
        lax.fori_loop(0, 4 * n_z, table, 0)

    def give_core(rank, m):
        x_copy(rank, m).wait_recv()
        p_copy(rank, m, 1).start()

    def near_core(m):
        give_core(rank_of(1), m)

        @pl.when(middle)
        def _():
            give_core(rank_of(2), m)

    def slab_next(side, col, j):
        slab_wait(side, col, j)
        slab_core(side, col, j).start()

    for m in every:
        near_relay(m)
    slab_next(0, c_x, 0)
    slab_diag(0).start()
    y_over(y).start()
    complete()
    slab_next(1, c, 1)
    slab_diag(1).start()
    far_relay(0)
    slab_next(0, c_x, 1)
    near_x(0)
    far_relay(1)
    far_x(0)
    slab_next(1, c, 0)
    far_relay(2)
    near_x(1)
    far_x(1)
    far_relay(3)
    slab_next(1, c_x, 1)
    near_x(2)
    far_relay(4)
    slab_next(1, c_x, 0)
    y_over(1 - y).wait_recv()
    for m in every:
        p_copy(z, m, 1).start()
    far_x(2)
    for m in every[3:]:
        near_x(m)
        far_x(m)

    mine[4].wait()
    for j in range(columns):
        for side in range(2):
            for col in (c_t, 2 * (1 - x) + 1 - t):
                slab_wait(side, col, j)

    def gather_right(n, carry):
        rank = lax.div(n, 4)
        side = lax.rem(lax.div(n, 2), 2)
        u = lax.rem(n, 2)
        k = 2 * (2 * rank + side) + jnp.where(u == 0, t, 1 - t)
        rows = pl.ds(pl.multiple_of(lax.rem(n, 4) * block, block), block)
        for s in range(2):
            for j in range(columns):
                q = source_s[k, s * columns + j]
                at = jnp.maximum(q, 0)
                value = b_all[s, lax.div(at, slots), j, lax.rem(at, slots)]
                to = (s * columns + j) * block
                right[rank, rows, to:to + block] = jnp.where(q >= 0, value, jnp.zeros_like(value))
        return carry

    lax.fori_loop(0, 4 * n_z, gather_right, 0)

    tall = RB_DEV * GRAIN

    def multiply(rank, m):
        size = PARTS[m]
        p_copy(rank, m, 0).wait_recv()
        p_copy(rank, m, 1).wait_recv()
        for g in range(size):
            for u, source in enumerate((a_all, a_par)):
                for side in range(2):
                    stage[u, side, g] = source[rank, starts[m] + g, side]
        for side in range(2):
            for u in range(2):
                k = 2 * (2 * rank + side) + (t if u == 0 else 1 - t)
                at = (2 * side + u) * block
                for i in range(RB_DEV):
                    p = slot_s[k, i]
                    for g in range(size):
                        value = stage[u, side, g, jnp.maximum(p, 0)]
                        to = g * tall + i * GRAIN
                        lhs[to:to + GRAIN, at:at + block] = jnp.where(p >= 0, value, jnp.zeros_like(value))
        for n in range(2):
            cols = slice(n * wide, (n + 1) * wide)
            product = jnp.dot(lhs[:size * tall], right[rank, :, cols], preferred_element_type=jnp.float32)
            acc[starts[m]:starts[m] + size, :, cols] += product.reshape(size, tall, wide)

    def first_ranks(m):
        near_core(m)
        give_core(rank_of(jnp.where(middle, 3, 2)), m)

        def one(n, carry):
            multiply(rank_of(n), m)
            return carry

        lax.fori_loop(0, 3, one, 0)

    def last_relay(m):
        @pl.when(end)
        def _():
            rank = rank_of(3)
            z_wait(rank, m)
            x_copy(rank, m).start()
            p_copy(rank, m, 0).start()

    def finish_part(m):
        rows = slice(starts[m], starts[m] + PARTS[m])
        for n in range(2):
            value = acc[rows, :, n * wide:(n + 1) * wide]
            squared = value * value
            sums_acc[n] += jnp.sum(squared.reshape(-1, 8, wide), axis=0)
        value = acc[rows, :, wide:].reshape(-1, wide)
        top = jnp.maximum(jnp.max(value, axis=0, keepdims=True), 1e-30)
        scaled = value * (LEVELS / top) + 0.5
        coded = jnp.minimum(scaled, LEVELS).astype(jnp.int32)
        word = lax.shift_left(coded[:, :block], jnp.int32(16)) | coded[:, block:]
        c_out[rows] = word.reshape(-1, tall, block)
        top_out[m] = jnp.broadcast_to(top, (8, wide))
        c_copy(m).start()
        top_copy(m).start()

    first_ranks(0)
    for m in every:
        last_relay(m)
        if m + 1 < len(PARTS):
            first_ranks(m + 1)

        @pl.when(end)
        def _():
            give_core(rank_of(3), m)

        multiply(rank_of(3), m)
        finish_part(m)

    for d in range(1, 8):
        sums_copy(d).start()

    give_cand().wait_send()
    give_near().wait_send()
    over_copy().wait_send()
    y_over(y).wait_send()
    for way in range(3):
        for j in range(columns):
            slab_own(way, j).wait_send()
    for j in range(columns):
        slab_diag(j).wait_send()
        for side, col in ((0, c_x), (1, c), (1, c_x)):
            slab_core(side, col, j).wait_send()

    def drain(m):
        for tail in range(2):
            y_copy(m, tail).wait_send()
            both(m, 0, tail, wait_send)
            both(m, 1, tail, wait_send)

        def one(rank, carry):
            @pl.when(rank != z)
            def _():
                x_copy(rank, m).wait_send()

            p_copy(rank, m, 0).wait_send()
            p_copy(rank, m, 1).wait_send()

            @pl.when((rank < z) & has_up)
            def _():
                z_next(0, rank, m).wait_send()

            @pl.when((rank > z) & has_down)
            def _():
                z_next(1, rank, m).wait_send()
            return carry

        lax.fori_loop(0, n_z, one, 0)
        c_copy(m).wait_send()
        top_copy(m).wait_send()

    for d in range(1, 8):
        sums_copy(d).wait()
    sums = sums_acc[0]
    for d in range(1, 8):
        sums = sums + sums_all[0 if d < 4 else 1, near[d - 1][1]]
    factor = float(RB_DEV * 4 * block) / jnp.sum(sums, axis=0, keepdims=True)

    def store(value, g, side):
        value = value.astype(jnp.bfloat16)
        for i in range(RB_DEV):
            for j in range(columns):
                result[j, i, rows_at(side, g), :] = value[i * GRAIN:(i + 1) * GRAIN, j * block:(j + 1) * block]

    def scale_own(g, carry):
        value = acc[g, :, :wide]
        store(value * value * factor, g, y)
        return carry

    def out_half(side):
        rows = pl.ds(pl.multiple_of(side * half, half), half)
        return pltpu.make_async_copy(
            result.at[:, :, rows], out_ref.at[:, :, rows], local.at[6 + side])

    lax.fori_loop(0, grains, scale_own, 0)
    out_half(y).start()
    for m in every:
        c_copy(m).wait_recv()
        top_copy(m).wait_recv()
        step = top_in[m][0:1, :] * (1.0 / LEVELS)
        for g in range(starts[m], starts[m] + PARTS[m]):
            word = c_in[g]
            upper = lax.shift_right_logical(word, jnp.int32(16)).astype(jnp.float32)
            lower = (word & jnp.int32(65535)).astype(jnp.float32)
            value = jnp.concatenate([upper, lower], axis=1) * step
            store(value * value * factor, g, 1 - y)
    out_half(1 - y).start()
    for m in every:
        drain(m)
    out_half(0).wait()
    out_half(1).wait()


def paired(n_z, matrix_blocks, matrix_rows, matrix_counts, slab_blocks, slab_inner, slab_counts):
    capacity, block = matrix_blocks.shape[1], matrix_blocks.shape[2]
    columns, slots = slab_blocks.shape[0], slab_blocks.shape[1]
    grains = block // 2 // GRAIN
    counts = matrix_counts.reshape(1, 2)
    used = slab_counts.reshape(1, columns)
    hbm = pl.BlockSpec(memory_space=pltpu.HBM)
    smem = pl.BlockSpec(memory_space=pltpu.SMEM)
    dma = pltpu.SemaphoreType.DMA
    half_word, full = jnp.bfloat16, jnp.float32
    rows_shape, counts_shape, inner_shape = (2 * n_z, 2, capacity), (2 * n_z, 1, 2), (2, 4) + slab_inner.shape
    lists = (n_z, grains, 2, SLOTS, GRAIN, block)
    parts, most = len(PARTS), max(PARTS)
    vmem = [
        ((2 * capacity, block, block), half_word),
        ((OVER, block, block), half_word),
        ((OVER, block, block), half_word),
        ((grains, SLOTS, GRAIN, block), half_word),
        (lists, half_word),
        (lists, half_word),
        ((2, 4) + slab_blocks.shape, half_word),
        ((n_z, 4 * block, 2 * columns * block), half_word),
        ((2, 2, most, SLOTS, GRAIN, block), half_word),
        ((most * RB_DEV * GRAIN, 4 * block), half_word),
        ((grains, RB_DEV * GRAIN, 2 * columns * block), full),
        ((columns, RB_DEV, block, block), half_word),
        ((2, 8, columns * block), full),
        ((2, 4, 8, columns * block), full),
        ((grains, RB_DEV * GRAIN, block), jnp.int32),
        ((grains, RB_DEV * GRAIN, block), jnp.int32),
        ((parts, 8, columns * block), full),
        ((parts, 8, columns * block), full),
        (rows_shape, jnp.int32), (counts_shape, jnp.int32), (counts_shape, jnp.int32), ((1, 2), jnp.int32),
        (inner_shape, jnp.int32), ((1, columns), jnp.int32),
    ]
    words = [rows_shape, counts_shape, counts_shape, (1, 2), inner_shape, (1, columns),
             (4 * n_z, RB_DEV), (4 * n_z, 2 * columns)]
    sems = [(8,), (5,), (2,), (2,), (2, n_z, parts, 4), (n_z, parts), (parts, 2), (parts, 2), None, None, (2,),
            (n_z, parts), (n_z, parts), (n_z, parts, 2), (n_z, parts, 2), (4, 2, 4, columns), (2, 4, columns),
            (4, 2 * n_z), (4, 2 * n_z), (parts, 2), (parts, 2), (8,), (8,)]
    return pl.pallas_call(
        functools.partial(pair_kernel, n_z, (columns, slots, capacity, block)),
        out_shape=jax.ShapeDtypeStruct((columns, RB_DEV, block, block), jnp.bfloat16),
        in_specs=[hbm] * 6 + [smem] * 2,
        out_specs=hbm,
        scratch_shapes=[pltpu.VMEM(s, d) for s, d in vmem] + [pltpu.SMEM(s, jnp.int32) for s in words]
        + [dma if s is None else dma(s) for s in sems],
        compiler_params=pltpu.CompilerParams(
            collective_id=1, has_side_effects=True, vmem_limit_bytes=62 << 20),
        name="packed_pair_multiply",
    )(matrix_blocks, slab_blocks, matrix_rows, counts, slab_inner, used, counts, used)


def choose(n_row, n_col, *args):
    if n_row == 8 and n_col == 4 and args[0].shape[0] == 2 and args[0].shape[1] == SLOTS // 2:
        return paired(n_row // 2, *args)
    return on_device(n_row, n_col, *args)


def solution(mesh):
    return jax.shard_map(
        functools.partial(choose, mesh.shape["row"], mesh.shape["col"]),
        mesh=mesh,
        in_specs=(
            P("row", "col", None, None),
            P("row", "col"),
            P("row", "col"),
            P("row", "col", None, None),
            P("row", "col"),
            P("row"),
        ),
        out_specs=P("row", "col", None, None),
        check_vma=False,
    )
```

```python
import functools

import jax
import jax.numpy as jnp
from jax import lax
from jax.experimental import pallas as pl
from jax.experimental.pallas import tpu as pltpu
from jax.sharding import PartitionSpec as P

RB_DEV = 8
MESH = pl.DeviceIdType.MESH
CHUNKS = 6
PLAIN = CHUNKS - 1
UP, DOWN, SIDE = 0, 1, 2


def step_kernel(n_row, n_col, shape, a_ref, b_ref, rows_ref, counts_ref, inner_ref, slab_counts, out_ref,
                a_all, b_all, rows_all, counts_all, inner_all, rows_s, counts_s, inner_s,
                slot_s, source_s, stage, right, acc, sums_all, result,
                send, recv, b_send, b_recv, m_send, m_recv, s_send, s_recv, local, done):
    columns, slots, per_rank, capacity, block = shape
    each = CHUNKS // per_rank
    size = capacity // each
    n_z = n_row // 2
    r = lax.axis_index("row")
    c = lax.axis_index("col")
    z = lax.div(r, 2)
    y = lax.rem(r, 2)
    other = 1 - y
    beside = 2 * z + other
    has_up = z < n_z - 1
    has_down = z > 0

    barrier = pltpu.get_barrier_semaphore()
    for d in range(1, n_row):
        pl.semaphore_signal(barrier, inc=1, device_id={"row": lax.rem(r + d, n_row)}, device_id_type=MESH)
    for d in range(1, n_col):
        pl.semaphore_signal(barrier, inc=1, device_id={"col": lax.rem(c + d, n_col)}, device_id_type=MESH)
    pl.semaphore_wait(barrier, n_row + n_col - 2)

    def chunk(way, rank, ch, own=False):
        target = {UP: r + 2, DOWN: r - 2, SIDE: beside}[way]
        src = a_ref.at[ch] if own else a_all.at[rank, ch]
        return pltpu.make_async_remote_copy(
            src_ref=src, dst_ref=a_all.at[rank, ch], send_sem=send.at[way, rank, ch],
            recv_sem=recv.at[rank, ch], device_id={"row": target}, device_id_type=MESH)

    def arrived(rank, ch):
        pltpu.make_async_remote_copy(
            src_ref=a_all.at[rank, ch], dst_ref=a_all.at[rank, ch], send_sem=send.at[SIDE, rank, ch],
            recv_sem=recv.at[rank, ch], device_id={"row": beside}, device_id_type=MESH).wait_recv()

    def small(d):
        target = {"row": lax.rem(r + d, n_row)}
        return [
            pltpu.make_async_remote_copy(
                src_ref=src, dst_ref=dst.at[r], send_sem=m_send.at[n, d], recv_sem=m_recv.at[n, d],
                device_id=target, device_id_type=MESH)
            for n, (src, dst) in enumerate(((rows_ref, rows_all), (counts_ref, counts_all)))
        ]

    def slab(d):
        target = {"col": lax.rem(c + d, n_col)}
        return [
            pltpu.make_async_remote_copy(
                src_ref=inner_ref, dst_ref=inner_all.at[c], send_sem=b_send.at[1, d], recv_sem=b_recv.at[1, d],
                device_id=target, device_id_type=MESH),
            pltpu.make_async_remote_copy(
                src_ref=b_ref, dst_ref=b_all.at[c], send_sem=b_send.at[0, d], recv_sem=b_recv.at[0, d],
                device_id=target, device_id_type=MESH),
        ]

    def share(d):
        return pltpu.make_async_remote_copy(
            src_ref=sums_all.at[c], dst_ref=sums_all.at[c], send_sem=s_send.at[d], recv_sem=s_recv.at[d],
            device_id={"col": lax.rem(c + d, n_col)}, device_id_type=MESH)

    for ch in [PLAIN] + list(range(PLAIN)):
        chunk(SIDE, r, ch, True).start()
    for ch in range(CHUNKS):
        @pl.when(has_up)
        def _():
            chunk(UP, r, ch, True).start()

        @pl.when(has_down)
        def _():
            chunk(DOWN, r, ch, True).start()

    for d in range(1, n_row):
        for copy in small(d):
            copy.start()
    for d in range(1, n_col):
        for copy in slab(d):
            copy.start()
    mine = (
        pltpu.make_async_copy(a_ref, a_all.at[r], local.at[0]),
        pltpu.make_async_copy(b_ref, b_all.at[c], local.at[1]),
        pltpu.make_async_copy(rows_ref, rows_all.at[r], local.at[2]),
        pltpu.make_async_copy(counts_ref, counts_all.at[r], local.at[3]),
        pltpu.make_async_copy(inner_ref, inner_all.at[c], local.at[4]),
    )
    for copy in mine:
        copy.start()
    acc[...] = jnp.zeros_like(acc)

    arrived(beside, PLAIN)

    @pl.when(has_up)
    def _():
        chunk(UP, beside, PLAIN).start()

    @pl.when(has_down)
    def _():
        chunk(DOWN, beside, PLAIN).start()

    steps = [(0, ch, True) for ch in range(PLAIN)] + [(0, PLAIN, False), (1, PLAIN, False)]

    def sides(d, work):
        def one(side, carry):
            at = z + d * (2 * side - 1)

            @pl.when((at >= 0) & (at < n_z))
            def _():
                work(at)
            return carry

        lax.fori_loop(0, 2, one, 0)

    def relay(d, extra):
        for n, (flip, ch, cross) in enumerate(steps):
            column = other if flip else y

            @pl.when(z >= d)
            def _():
                rank = 2 * (z - d) + column
                arrived(rank, ch)

                @pl.when(has_up)
                def _():
                    chunk(UP, rank, ch).start()

                if cross:
                    chunk(SIDE, rank, ch).start()

            @pl.when(z + d < n_z)
            def _():
                rank = 2 * (z + d) + column
                arrived(rank, ch)

                @pl.when(has_down)
                def _():
                    chunk(DOWN, rank, ch).start()

                if cross:
                    chunk(SIDE, rank, ch).start()

            for work in extra.get(n, ()):
                work()

    def half(rank, kk):
        k = rank * per_rank + kk
        copy = pltpu.make_async_copy(a_all.at[rank, pl.ds(kk * each, each)], stage, local.at[0])
        copy.start()
        for j in range(columns):
            q = source_s[k, j]
            at = jnp.maximum(q, 0)
            value = b_all[lax.div(at, slots), j * slots + lax.rem(at, slots)]
            right[:, j * block:(j + 1) * block] = jnp.where(q >= 0, value, jnp.zeros_like(value))
        copy.wait()

        def block_row(i, carry):
            t = slot_s[k, i]
            at = jnp.maximum(t, 0)
            value = stage[lax.div(at, size), lax.rem(at, size)]
            left = jnp.where(t >= 0, value, jnp.zeros_like(value))
            rows = pl.ds(pl.multiple_of(i * block, block), block)
            acc[rows, :] += jnp.dot(left, right[...], preferred_element_type=jnp.float32)
            return carry

        lax.fori_loop(0, RB_DEV, block_row, 0, unroll=2)

    def whole(rank):
        def one(kk, carry):
            half(rank, kk)
            return carry

        lax.fori_loop(0, per_rank, one, 0)

    def await_side(rank, first, end):
        for ch in range(first, end):
            arrived(rank, ch)

    def own_whole(at):
        whole(2 * at + y)

    def side_whole(at):
        await_side(2 * at + other, 0, PLAIN)
        whole(2 * at + other)

    def own_half(kk):
        def work(at):
            half(2 * at + y, kk)
        return work

    def side_half(kk):
        def work(at):
            await_side(2 * at + other, kk * each, min(kk * each + each, PLAIN))
            half(2 * at + other, kk)
        return work

    relay(1, {})

    def complete():
        for copy in mine:
            copy.wait()
        for d in range(1, n_row):
            for copy in small(d):
                copy.wait()
        for d in range(1, n_col):
            for copy in slab(d):
                copy.wait()
        for n, (src, dst) in enumerate(((rows_all, rows_s), (counts_all, counts_s), (inner_all, inner_s))):
            copy = pltpu.make_async_copy(src, dst, local.at[5 + n])
            copy.start()
            copy.wait()
        lax.fori_loop(0, n_row, table, 0)

    def table(rank, carry):
        for kk in range(per_rank):
            k = rank * per_rank + kk
            for j in range(columns):
                q = jnp.int32(-1)
                for n in range(n_col * slots):
                    found = (inner_s[n // slots, j, n % slots] == k) & (n < slab_counts[j])
                    q = jnp.where(found, n, q)
                source_s[k, j] = q
            for i in range(RB_DEV):
                t = jnp.int32(-1)
                for n in range(capacity):
                    found = (rows_s[rank, kk, n] == i) & (n < counts_s[rank, 0, kk])
                    t = jnp.where(found, n, t)
                slot_s[k, i] = t
        return carry

    def side_here():
        await_side(beside, 0, PLAIN)
        whole(beside)

    relay(2, {
        0: (complete,),
        1: (lambda: whole(r),),
        2: (side_here,),
        3: (lambda: sides(1, own_whole),),
    })
    sides(1, side_whole)
    sides(2, own_whole)

    def later(d, carry):
        relay(d, {})
        sides(d - 1, side_whole)
        sides(d, own_whole)
        return carry

    lax.fori_loop(3, n_z - 1, later, 0)
    far = n_z - 1

    def side_halves(at):
        side_half(0)(at)
        side_half(1)(at)

    relay(far, {
        each - 1: (lambda: sides(far, own_half(0)), lambda: sides(far - 1, side_halves)),
        CHUNKS - 1: (lambda: sides(far, own_half(1)), lambda: sides(far, side_half(0))),
        CHUNKS: (lambda: sides(far, side_half(1)),),
    })

    def square(i, total):
        rows = pl.ds(pl.multiple_of(i * block, block), block)
        value = acc[rows, :]
        value = value * value
        return total + jnp.sum(value.reshape(block // 8, 8, columns * block), axis=0)

    total = lax.fori_loop(0, RB_DEV, square, jnp.zeros((8, columns * block), jnp.float32))
    sums_all[c] = total
    for d in range(1, n_col):
        share(d).start()

    for ch in range(CHUNKS):
        chunk(SIDE, r, ch, True).wait_send()

        @pl.when(has_up)
        def _():
            chunk(UP, r, ch, True).wait_send()

        @pl.when(has_down)
        def _():
            chunk(DOWN, r, ch, True).wait_send()

    @pl.when(has_up)
    def _():
        chunk(UP, beside, PLAIN).wait_send()

    @pl.when(has_down)
    def _():
        chunk(DOWN, beside, PLAIN).wait_send()

    def drain(d, carry):
        for flip, ch, cross in steps:
            column = other if flip else y

            @pl.when(z >= d)
            def _():
                rank = 2 * (z - d) + column

                @pl.when(has_up)
                def _():
                    chunk(UP, rank, ch).wait_send()

                if cross:
                    chunk(SIDE, rank, ch).wait_send()

            @pl.when(z + d < n_z)
            def _():
                rank = 2 * (z + d) + column

                @pl.when(has_down)
                def _():
                    chunk(DOWN, rank, ch).wait_send()

                if cross:
                    chunk(SIDE, rank, ch).wait_send()
        return carry

    lax.fori_loop(1, n_z, drain, 0)

    for d in range(1, n_col):
        share(d).wait()
    sums = jnp.sum(jnp.sum(sums_all[...], axis=0), axis=0, keepdims=True)
    factor = float(RB_DEV * n_col * block) / sums

    def scale(i, carry):
        rows = pl.ds(pl.multiple_of(i * block, block), block)
        value = acc[rows, :]
        value = (value * value * factor).astype(jnp.bfloat16)
        for j in range(columns):
            result[j, i] = value[:, j * block:(j + 1) * block]
            pltpu.make_async_copy(result.at[j, i], out_ref.at[j, i], done.at[j, i]).start()
        return carry

    lax.fori_loop(0, RB_DEV, scale, 0)

    def finish(i, carry):
        for j in range(columns):
            pltpu.make_async_copy(result.at[j, i], out_ref.at[j, i], done.at[j, i]).wait()
        return carry

    lax.fori_loop(0, RB_DEV, finish, 0)


def on_device(n_row, n_col, matrix_blocks, matrix_rows, matrix_counts, slab_blocks, slab_inner, slab_counts):
    per_rank, capacity, block = matrix_blocks.shape[0], matrix_blocks.shape[1], matrix_blocks.shape[2]
    columns, slots = slab_blocks.shape[0], slab_blocks.shape[1]
    held = per_rank * capacity
    size = held // CHUNKS
    a = matrix_blocks.reshape(CHUNKS, size, block, block)
    b = slab_blocks.reshape(columns * slots, block, block)
    matrix_counts = matrix_counts.reshape(1, per_rank)
    hbm = pl.BlockSpec(memory_space=pltpu.HBM)
    dma = pltpu.SemaphoreType.DMA
    rows_shape, counts_shape, inner_shape = (
        (n_row,) + matrix_rows.shape, (n_row,) + matrix_counts.shape, (n_col,) + slab_inner.shape)
    return pl.pallas_call(
        functools.partial(step_kernel, n_row, n_col, (columns, slots, per_rank, capacity, block)),
        out_shape=jax.ShapeDtypeStruct((columns, RB_DEV, block, block), jnp.bfloat16),
        in_specs=[hbm, hbm, hbm, hbm, hbm, pl.BlockSpec(memory_space=pltpu.SMEM)],
        out_specs=hbm,
        scratch_shapes=[
            pltpu.VMEM((n_row,) + a.shape, a.dtype),
            pltpu.VMEM((n_col,) + b.shape, b.dtype),
            pltpu.VMEM(rows_shape, jnp.int32),
            pltpu.VMEM(counts_shape, jnp.int32),
            pltpu.VMEM(inner_shape, jnp.int32),
            pltpu.SMEM(rows_shape, jnp.int32),
            pltpu.SMEM(counts_shape, jnp.int32),
            pltpu.SMEM(inner_shape, jnp.int32),
            pltpu.SMEM((n_row * per_rank, RB_DEV), jnp.int32),
            pltpu.SMEM((n_row * per_rank, columns), jnp.int32),
            pltpu.VMEM((CHUNKS // per_rank, size, block, block), a.dtype),
            pltpu.VMEM((block, columns * block), b.dtype),
            pltpu.VMEM((RB_DEV * block, columns * block), jnp.float32),
            pltpu.VMEM((n_col, 8, columns * block), jnp.float32),
            pltpu.VMEM((columns, RB_DEV, block, block), jnp.bfloat16),
            dma((3, n_row, CHUNKS)), dma((n_row, CHUNKS)),
            dma((2, n_col)), dma((2, n_col)), dma((2, n_row)), dma((2, n_row)), dma((n_col,)), dma((n_col,)),
            dma((8,)), dma((columns, RB_DEV)),
        ],
        compiler_params=pltpu.CompilerParams(
            collective_id=0, has_side_effects=True, vmem_limit_bytes=63 << 20),
        name="gather_multiply_normalize",
    )(a, b, matrix_rows, matrix_counts, slab_inner, slab_counts)


LIST = 9
OVER = 3
FIRST = LIST - OVER
SLOTS = LIST + OVER
GRAIN = 16
PARTS = 4
BY_Y = 3
LEVELS = 65535.0


def pair_kernel(n_z, shape, a_ref, b_ref, rows_ref, counts_ref, inner_ref, used_ref, counts_in, used_in, out_ref,
                cand, over, over_in, y_out, a_all, a_par, b_all, right, stage, lhs, acc, result,
                sums_acc, sums_all, c_out, c_in, top_out, top_in,
                rows_all, counts_all, counts_par, counts_near, inner_all, used_all,
                rows_s, counts_s, counts_par_s, inner_s, used_s, slot_s, source_s,
                local, ready, near_send, near_recv, z_send, z_recv, y_send, y_recv, o_send, o_recv,
                over_y, x_send, x_recv, p_send, p_recv, b_send, b_recv, m_send, m_recv, c_send, c_recv, s_send, s_recv):
    columns, slots, capacity, block = shape
    half = block // 2
    size = half // GRAIN // PARTS
    grains = half // GRAIN
    wide = columns * block
    r = lax.axis_index("row")
    c = lax.axis_index("col")
    z = lax.div(r, 2)
    y = lax.rem(r, 2)
    x = lax.div(c, 2)
    t = lax.rem(c, 2)
    has_up = z < n_z - 1
    has_down = z > 0
    middle = has_up & has_down
    end = jnp.logical_not(middle)
    c_x = 2 * (1 - x) + t
    c_t = 2 * x + 1 - t
    to_up = {"row": r + 2, "col": c}
    to_down = {"row": r - 2, "col": c}
    to_y = {"row": 2 * z + 1 - y, "col": c}
    to_x = {"row": r, "col": c_x}
    to_core = {"row": r, "col": c_t}

    def span(m):
        return pl.ds(m * size, size)

    def parts(work, first=0, end_at=PARTS):
        def one(m, carry):
            work(m)
            return carry

        lax.fori_loop(first, end_at, one, 0)

    def quarter(work, n):
        parts(work, n * PARTS // 4, (n + 1) * PARTS // 4)

    def remote(src, dst, send_sem, recv_sem, target):
        return pltpu.make_async_remote_copy(
            src_ref=src, dst_ref=dst, send_sem=send_sem, recv_sem=recv_sem,
            device_id=target, device_id_type=MESH)

    near = [(2 * z + (y if d < 4 else 1 - y), lax.rem(c + d, 4)) for d in range(1, 8)]

    barrier = pltpu.get_barrier_semaphore()
    for d in range(1, 2 * n_z):
        pl.semaphore_signal(
            barrier, inc=1, device_id={"row": lax.rem(r + d, 2 * n_z), "col": c}, device_id_type=MESH)
    for d, (row, col) in enumerate(near, 1):
        if d != 4:
            pl.semaphore_signal(barrier, inc=1, device_id={"row": row, "col": col}, device_id_type=MESH)
    pl.semaphore_wait(barrier, 2 * n_z - 1 + 6)

    def give_cand(n):
        return remote(a_ref.at[1 - t, pl.ds(2 * n, 2)], cand.at[pl.ds(t * capacity + 2 * n, 2)],
                      near_send.at[0, n], near_recv.at[0, n], to_core)

    def take_cand(n):
        return remote(a_ref.at[1 - t, pl.ds(2 * n, 2)], cand.at[pl.ds((1 - t) * capacity + 2 * n, 2)],
                      near_send.at[0, n], near_recv.at[0, n], to_core)

    def give_near():
        return remote(counts_ref, counts_near, near_send.at[1, 0], near_recv.at[1, 0], to_core)

    def metas(d):
        target = {"row": lax.rem(r + d, 2 * n_z), "col": c}
        return [remote(rows_ref, rows_all.at[r], m_send.at[0, d], m_recv.at[0, d], target),
                remote(counts_ref, counts_all.at[r], m_send.at[1, d], m_recv.at[1, d], target)]

    def inner_to(d):
        side = 0 if d < 4 else 1
        row, col = near[d - 1]
        return remote(inner_ref, inner_all.at[side, c], m_send.at[2, d], m_recv.at[2, d], {"row": row, "col": col})

    def used_to():
        return remote(used_ref, used_all, m_send.at[3, 0], m_recv.at[3, 0], to_y)

    def par_counts():
        return remote(counts_all, counts_par, m_send.at[3, 1], m_recv.at[3, 1], to_core)

    def slab(side, col, j):
        return b_all.at[side, col, j]

    def slab_copy(way, src, side, col, j, target, first=0, size=slots):
        piece = pl.ds(first, size)
        return remote(src.at[piece], b_all.at[side, col, j, piece], b_send.at[way, side, col, j],
                      b_recv.at[side, col, j], target)

    def slab_own(way, j, first=0, size=slots):
        side, target = {0: (0, to_core), 1: (0, to_x), 2: (1, to_y)}[way]
        return slab_copy(way, b_ref.at[j], side, c, j, target, first, size)

    def slab_core(side, col, j):
        return slab_copy(0, slab(side, col, j), side, col, j, to_core)

    def slab_diag(j, over_x):
        first, size = 0, slots
        if j == 0:
            first, size = (BY_Y, slots - BY_Y) if over_x else (0, BY_Y)
        if over_x:
            return slab_copy(3, slab(1, c, j), 1, c, j, to_x, first, size)
        return slab_copy(3, slab(0, c_x, j), 1, c_x, j, to_y, first, size)

    def slab_wait(side, col, j):
        slab_copy(0, slab(side, col, j), side, col, j, to_core).wait_recv()

    def y_copy(m, tail):
        at, many = ((0, FIRST), (FIRST, OVER))[tail]
        return remote(y_out.at[span(m), pl.ds(at, many)], a_all.at[z, span(m), y, pl.ds(at, many)],
                      y_send.at[m, tail], y_recv.at[m, tail], to_y)

    def y_wait(m, tail):
        at, many = ((0, FIRST), (FIRST, OVER))[tail]
        remote(y_out.at[span(m), pl.ds(at, many)], a_all.at[z, span(m), 1 - y, pl.ds(at, many)],
               y_send.at[m, tail], y_recv.at[m, tail], to_y).wait_recv()

    def y_over(to):
        return remote(y_out.at[:, pl.ds(LIST, OVER)], a_all.at[z, :, to, pl.ds(LIST, OVER)],
                      over_y.at[0], over_y.at[1], to_y)

    def over_copy():
        return remote(over, over_in, o_send, o_recv, to_x)

    def z_first(way, m, side, tail):
        at, many = ((0, FIRST), (FIRST, OVER))[tail]
        piece = a_all.at[z, span(m), side, pl.ds(at, many)]
        return remote(piece, piece, z_send.at[way, z, m, 2 * side + tail], z_recv.at[z, m, tail],
                      (to_up, to_down)[way])

    def z_piece(rank, m, tail):
        return a_all.at[rank, span(m), :, (pl.ds(0, FIRST), pl.ds(FIRST, OVER))[tail]]

    def z_next(way, rank, m, tail):
        piece = z_piece(rank, m, tail)
        return remote(piece, piece, z_send.at[way, rank, m, tail], z_recv.at[rank, m, tail], (to_up, to_down)[way])

    def z_wait(rank, m, tail):
        piece = z_piece(rank, m, tail)
        remote(piece, piece, z_send.at[0, rank, m, tail], z_recv.at[rank, m, tail], to_y).wait_recv()

    def moved(step, act):
        @pl.when(step == 0)
        def _():
            act(0, 1)

        @pl.when(step + 1 < PARTS)
        def _():
            act(step + 1, 1)

        act(step, 0)

    def x_copy(rank, m):
        return remote(a_all.at[rank, span(m), :, pl.ds(FIRST, OVER)], a_all.at[rank, span(m), :, pl.ds(LIST, OVER)],
                      x_send.at[rank, m], x_recv.at[rank, m], to_x)

    def p_copy(rank, m, over_part):
        piece = (rank, span(m), slice(None), (pl.ds(0, FIRST), pl.ds(FIRST, 2 * OVER))[over_part])
        return remote(a_all.at[piece], a_par.at[piece], p_send.at[rank, m, over_part], p_recv.at[rank, m, over_part],
                      to_core)

    def c_copy(m):
        return remote(c_out.at[span(m)], c_in.at[span(m)], c_send.at[m, 0], c_recv.at[m, 0], to_y)

    def top_copy(m):
        return remote(top_out.at[m], top_in.at[m], c_send.at[m, 1], c_recv.at[m, 1], to_y)

    def sums_copy(d):
        row, col = near[d - 1]
        side = 0 if d < 4 else 1
        return remote(sums_acc.at[side], sums_all.at[side, c], s_send.at[d], s_recv.at[d], {"row": row, "col": col})

    def both(m, side, tail, act):
        @pl.when(has_up)
        def _():
            act(z_first(0, m, side, tail))

        @pl.when(has_down)
        def _():
            act(z_first(1, m, side, tail))

    def start(copy):
        copy.start()

    def wait_send(copy):
        copy.wait_send()

    def rank_of(n):
        low = z < n_z // 2
        at = jnp.where(low, z, n_z - 1 - z)
        rank = n - 1 + jnp.where(n - 1 >= at, 1, 0)
        rank = jnp.where(low, rank, n_z - 1 - rank)
        return jnp.where(n == 0, z, rank)

    mine = [pltpu.make_async_copy(a_ref.at[t], cand.at[pl.ds(t * capacity, capacity)], local.at[0])]
    give_near().start()
    for n in range(capacity // 2):
        give_cand(n).start()
    mine[0].start()
    slab_own(2, 1, 0, 2).start()
    slab_own(1, 0, 0, 1).start()
    mine += [
        pltpu.make_async_copy(rows_ref, rows_all.at[r], local.at[1]),
        pltpu.make_async_copy(counts_ref, counts_all.at[r], local.at[2]),
        pltpu.make_async_copy(inner_ref, inner_all.at[0, c], local.at[3]),
        pltpu.make_async_copy(b_ref, b_all.at[0, c], local.at[4]),
    ]
    acc[...] = jnp.zeros_like(acc)
    sums_acc[...] = jnp.zeros_like(sums_acc)

    give_near().wait_recv()
    at_rank = lax.broadcasted_iota(jnp.int32, (1, 2), 1)
    near_count = jnp.max(jnp.where(at_rank == t, counts_near[...], 0))
    mine[0].wait()
    for n in range(capacity // 2):
        take_cand(n).wait_recv()

    own_count = counts_in[0, t]
    first_count = jnp.where(t == 0, own_count, near_count)
    total_count = own_count + near_count

    def place(p):
        return jnp.where(p < first_count, p, capacity + jnp.minimum(jnp.maximum(p - first_count, 0), capacity - 1))

    for p in range(OVER):
        over[p] = cand[place(LIST + p)]
    over_copy().start()

    def rows_at(side, m):
        return pl.ds(pl.multiple_of(side * half + m * GRAIN, GRAIN), GRAIN)

    def pack(p, carry):
        at = place(p)
        for g in range(grains):
            a_all[z, g, y, p] = cand[at, rows_at(y, g), :]
            y_out[g, p] = cand[at, rows_at(1 - y, g), :]
        return carry

    def pack_tail(p, carry):
        at = place(FIRST + p)
        keep = total_count > FIRST
        for g in range(grains):
            for side, there in ((y, True), (1 - y, False)):
                value = jnp.where(keep, cand[at, rows_at(side, g), :], over_in[p, rows_at(side, g), :])
                if there:
                    a_all[z, g, y, FIRST + p] = value
                else:
                    y_out[g, FIRST + p] = value
        return carry

    def pack_over(p, carry):
        for g in range(grains):
            a_all[z, g, y, LIST + p] = over[p, rows_at(y, g), :]
            y_out[g, LIST + p] = over[p, rows_at(1 - y, g), :]
        return carry

    lax.fori_loop(0, FIRST, pack, 0)
    def own_main(m):
        y_copy(m, 0).start()
        both(m, y, 0, start)

    def beside_main(m):
        y_wait(m, 0)
        both(m, 1 - y, 0, start)
        p_copy(z, m, 0).start()

    def own_tail(m):
        y_copy(m, 1).start()
        both(m, y, 1, start)

    def beside_tail(m):
        y_wait(m, 1)
        both(m, 1 - y, 1, start)

    parts(own_main)
    slab_own(1, 0, 1, slots - 1).start()
    for j in range(columns):
        slab_own(0, j).start()
    for d in range(1, 2 * n_z):
        for copy in metas(d):
            copy.start()
    for d in range(1, 8):
        inner_to(d).start()
    used_to().start()
    for copy in mine[1:]:
        copy.start()
    lax.fori_loop(0, OVER, pack_over, 0)
    parts(beside_main)
    over_copy().wait_recv()
    lax.fori_loop(0, OVER, pack_tail, 0)
    parts(own_tail)
    slab_own(1, 1).start()
    slab_own(2, 1, 2, slots - 2).start()
    parts(beside_tail)
    slab_own(2, 0).start()

    def relay(n, step):
        rank = rank_of(n)

        def act(m, tail):
            z_wait(rank, m, tail)

            @pl.when((rank < z) & has_up)
            def _():
                z_next(0, rank, m, tail).start()

            @pl.when((rank > z) & has_down)
            def _():
                z_next(1, rank, m, tail).start()

        moved(step, act)
        p_copy(rank, step, 0).start()

    def near_x(m):
        x_copy(rank_of(1), m).start()

        @pl.when(middle)
        def _():
            x_copy(rank_of(2), m).start()

    def near_relay(m):
        relay(1, m)

        @pl.when(middle)
        def _():
            relay(2, m)

    def far_relay(m):
        relay(jnp.where(middle, 3, 2), m)

    def far_x(m):
        x_copy(rank_of(jnp.where(middle, 3, 2)), m).start()

    def table(k, carry):
        rank = lax.div(k, 2)
        kk = lax.rem(k, 2)
        for side in range(2):
            for j in range(columns):
                limit = used_in[0, j] if side == 0 else used_s[0, j]
                q = jnp.int32(-1)
                for n in range(4 * slots):
                    found = (inner_s[side, n // slots, j, n % slots] == k) & (n < limit)
                    q = jnp.where(found, n, q)
                source_s[k, side * columns + j] = q
        base = jnp.where(t == 1, counts_par_s[rank, 0, kk], 0)
        live = counts_s[rank, 0, kk]
        for i in range(RB_DEV):
            p = jnp.int32(-1)
            for n in range(capacity):
                found = (rows_s[rank, kk, n] == i) & (n < live)
                p = jnp.where(found, n + base, p)
            slot_s[k, i] = p
        return carry

    def complete():
        for copy in mine[1:4]:
            copy.wait()
        for d in range(1, 2 * n_z):
            for copy in metas(d):
                copy.wait()
        par_counts().start()
        for d in range(1, 8):
            inner_to(d).wait()
        used_to().wait()
        par_counts().wait()
        for n, (src, dst) in enumerate((
                (rows_all, rows_s), (counts_all, counts_s), (counts_par, counts_par_s), (inner_all, inner_s),
                (used_all, used_s))):
            pltpu.make_async_copy(src, dst, ready.at[n]).start()
        for n, (src, dst) in enumerate((
                (rows_all, rows_s), (counts_all, counts_s), (counts_par, counts_par_s), (inner_all, inner_s),
                (used_all, used_s))):
            pltpu.make_async_copy(src, dst, ready.at[n]).wait()
        lax.fori_loop(0, 4 * n_z, table, 0)

    def give_core(rank, m):
        x_copy(rank, m).wait_recv()
        p_copy(rank, m, 1).start()

    def near_core(m):
        give_core(rank_of(1), m)

        @pl.when(middle)
        def _():
            give_core(rank_of(2), m)

    def slab_next(side, col, j):
        slab_wait(side, col, j)
        slab_core(side, col, j).start()

    def forward(m):
        near_x(m)
        far_x(m)

    slab_next(0, c_x, 0)
    slab_diag(0, False).start()
    parts(near_relay)
    slab_next(1, c, 1)
    slab_diag(1, True).start()
    slab_next(0, c_x, 1)
    complete()
    quarter(far_relay, 0)
    slab_next(1, c, 0)
    slab_diag(0, True).start()
    y_over(y).start()
    quarter(far_relay, 1)
    slab_next(1, c_x, 1)
    quarter(forward, 0)
    slab_next(1, c_x, 0)
    quarter(forward, 1)
    quarter(far_relay, 2)

    mine[4].wait()
    for j in range(columns):
        for side in range(2):
            for col in (c_t, 2 * (1 - x) + 1 - t):
                slab_wait(side, col, j)

    def gather_right(n, carry):
        rank = lax.div(n, 4)
        side = lax.rem(lax.div(n, 2), 2)
        u = lax.rem(n, 2)
        k = 2 * (2 * rank + side) + jnp.where(u == 0, t, 1 - t)
        rows = pl.ds(pl.multiple_of(lax.rem(n, 4) * block, block), block)
        for s in range(2):
            for j in range(columns):
                q = source_s[k, s * columns + j]
                at = jnp.maximum(q, 0)
                value = b_all[s, lax.div(at, slots), j, lax.rem(at, slots)]
                to = (s * columns + j) * block
                right[rank, rows, to:to + block] = jnp.where(q >= 0, value, jnp.zeros_like(value))
        return carry

    lax.fori_loop(0, 4 * n_z, gather_right, 0)

    tall = RB_DEV * GRAIN

    def multiply(rank, m):
        p_copy(rank, m, 0).wait_recv()
        p_copy(rank, m, 1).wait_recv()
        for g in range(size):
            for u, source in enumerate((a_all, a_par)):
                for side in range(2):
                    stage[u, side, g] = source[rank, m * size + g, side]
        for side in range(2):
            for u in range(2):
                k = 2 * (2 * rank + side) + (t if u == 0 else 1 - t)
                at = (2 * side + u) * block
                for i in range(RB_DEV):
                    p = slot_s[k, i]
                    for g in range(size):
                        value = stage[u, side, g, jnp.maximum(p, 0)]
                        to = g * tall + i * GRAIN
                        lhs[to:to + GRAIN, at:at + block] = jnp.where(p >= 0, value, jnp.zeros_like(value))
        for n in range(2):
            cols = slice(n * wide, (n + 1) * wide)
            product = jnp.dot(lhs[...], right[rank, :, cols], preferred_element_type=jnp.float32)
            acc[span(m), :, cols] += product.reshape(size, tall, wide)

    def cores(m):
        near_core(m)
        give_core(rank_of(jnp.where(middle, 3, 2)), m)

    def last_relay(m):
        rank = rank_of(3)

        def act(n, tail):
            z_wait(rank, n, tail)
            if tail:
                x_copy(rank, n).start()

        moved(m, act)
        p_copy(rank, m, 0).start()
        give_core(rank, m)

    def finish_part(m):
        for n in range(2):
            value = acc[span(m), :, n * wide:(n + 1) * wide]
            squared = value * value
            sums_acc[n] += jnp.sum(squared.reshape(-1, 8, wide), axis=0)
        value = acc[span(m), :, wide:].reshape(-1, wide)
        top = jnp.maximum(jnp.max(value, axis=0, keepdims=True), 1e-30)
        scaled = value * (LEVELS / top) + 0.5
        coded = jnp.minimum(scaled, LEVELS).astype(jnp.int32)
        word = lax.shift_left(coded[:, :block], jnp.int32(16)) | coded[:, block:]
        c_out[span(m)] = word.reshape(size, tall, block)
        top_out[m] = jnp.broadcast_to(top, (8, wide))
        c_copy(m).start()
        top_copy(m).start()

    quarter(forward, 2)
    quarter(far_relay, 3)
    quarter(forward, 3)
    y_over(1 - y).wait_recv()
    parts(lambda m: p_copy(z, m, 1).start())
    cores(0)

    def drain_start():
        give_near().wait_send()
        for n in range(capacity // 2):
            give_cand(n).wait_send()
        over_copy().wait_send()
        y_over(y).wait_send()
        for way in range(3):
            for j in range(columns):
                slab_own(way, j).wait_send()
        for j in range(columns):
            slab_diag(j, True).wait_send()
            if j == 0:
                slab_diag(j, False).wait_send()
            for side, col in ((0, c_x), (1, c), (1, c_x)):
                slab_core(side, col, j).wait_send()

    def drain_rank(rank, m):
        p_copy(rank, m, 0).wait_send()
        p_copy(rank, m, 1).wait_send()

        @pl.when(rank != z)
        def _():
            x_copy(rank, m).wait_send()

    def drain_part(m):
        for tail in range(2):
            y_copy(m, tail).wait_send()
            both(m, 0, tail, wait_send)
            both(m, 1, tail, wait_send)

        def one(n, carry):
            drain_rank(rank_of(n), m)
            return carry

        lax.fori_loop(0, 3, one, 0)

    def drain_last(m):
        drain_rank(rank_of(3), m)
        c_copy(m).wait_send()
        top_copy(m).wait_send()

        @pl.when(middle)
        def _():
            def one(rank, carry):
                for tail in range(2):
                    @pl.when((rank < z) & has_up)
                    def _():
                        z_next(0, rank, m, tail).wait_send()

                    @pl.when((rank > z) & has_down)
                    def _():
                        z_next(1, rank, m, tail).wait_send()
                return carry

            lax.fori_loop(0, n_z, one, 0)

    def one_part(m):
        @pl.when(m + 1 < PARTS)
        def _():
            cores(m + 1)

        def one_rank(n, carry):
            @pl.when((n == 3) & end)
            def _():
                last_relay(m)

            multiply(rank_of(jnp.where(n == 3, 3, lax.rem(n + 1, 3))), m)
            return carry

        lax.fori_loop(0, 4, one_rank, 0)
        finish_part(m)

        @pl.when(m + 1 < PARTS)
        def _():
            @pl.when(m == 0)
            def _():
                drain_start()

            drain_part(m)

    parts(one_part)
    for d in range(1, 8):
        sums_copy(d).start()
    drain_part(PARTS - 1)

    for d in range(1, 8):
        sums_copy(d).wait()
    sums = sums_acc[0]
    for d in range(1, 8):
        sums = sums + sums_all[0 if d < 4 else 1, near[d - 1][1]]
    factor = float(RB_DEV * 4 * block) / jnp.sum(sums, axis=0, keepdims=True)

    def store(value, g, side):
        value = value.astype(jnp.bfloat16)
        for i in range(RB_DEV):
            for j in range(columns):
                result[j, i, rows_at(side, g), :] = value[i * GRAIN:(i + 1) * GRAIN, j * block:(j + 1) * block]

    def scale_own(g, carry):
        value = acc[g, :, :wide]
        store(value * value * factor, g, y)
        return carry

    def out_half(side):
        rows = pl.ds(pl.multiple_of(side * half, half), half)
        return pltpu.make_async_copy(
            result.at[:, :, rows], out_ref.at[:, :, rows], local.at[6 + side])

    lax.fori_loop(0, grains, scale_own, 0)
    out_half(y).start()
    def scale_other(m):
        c_copy(m).wait_recv()
        top_copy(m).wait_recv()
        step = top_in[m][0:1, :] * (1.0 / LEVELS)

        def one(g, carry):
            word = c_in[g]
            upper = lax.shift_right_logical(word, jnp.int32(16)).astype(jnp.float32)
            lower = (word & jnp.int32(65535)).astype(jnp.float32)
            value = jnp.concatenate([upper, lower], axis=1) * step
            store(value * value * factor, g, 1 - y)
            return carry

        lax.fori_loop(m * size, (m + 1) * size, one, 0)

    parts(scale_other)
    out_half(1 - y).start()
    parts(drain_last)
    out_half(0).wait()
    out_half(1).wait()


def paired(n_z, matrix_blocks, matrix_rows, matrix_counts, slab_blocks, slab_inner, slab_counts):
    capacity, block = matrix_blocks.shape[1], matrix_blocks.shape[2]
    columns, slots = slab_blocks.shape[0], slab_blocks.shape[1]
    grains = block // 2 // GRAIN
    counts = matrix_counts.reshape(1, 2)
    used = slab_counts.reshape(1, columns)
    hbm = pl.BlockSpec(memory_space=pltpu.HBM)
    smem = pl.BlockSpec(memory_space=pltpu.SMEM)
    dma = pltpu.SemaphoreType.DMA
    half_word, full = jnp.bfloat16, jnp.float32
    rows_shape, counts_shape, inner_shape = (2 * n_z, 2, capacity), (2 * n_z, 1, 2), (2, 4) + slab_inner.shape
    lists = (n_z, grains, 2, SLOTS, GRAIN, block)
    parts, most = PARTS, grains // PARTS
    vmem = [
        ((2 * capacity, block, block), half_word),
        ((OVER, block, block), half_word),
        ((OVER, block, block), half_word),
        ((grains, SLOTS, GRAIN, block), half_word),
        (lists, half_word),
        (lists, half_word),
        ((2, 4) + slab_blocks.shape, half_word),
        ((n_z, 4 * block, 2 * columns * block), half_word),
        ((2, 2, most, SLOTS, GRAIN, block), half_word),
        ((most * RB_DEV * GRAIN, 4 * block), half_word),
        ((grains, RB_DEV * GRAIN, 2 * columns * block), full),
        ((columns, RB_DEV, block, block), half_word),
        ((2, 8, columns * block), full),
        ((2, 4, 8, columns * block), full),
        ((grains, RB_DEV * GRAIN, block), jnp.int32),
        ((grains, RB_DEV * GRAIN, block), jnp.int32),
        ((parts, 8, columns * block), full),
        ((parts, 8, columns * block), full),
        (rows_shape, jnp.int32), (counts_shape, jnp.int32), (counts_shape, jnp.int32), ((1, 2), jnp.int32),
        (inner_shape, jnp.int32), ((1, columns), jnp.int32),
    ]
    words = [rows_shape, counts_shape, counts_shape, inner_shape, (1, columns),
             (4 * n_z, RB_DEV), (4 * n_z, 2 * columns)]
    sems = [(8,), (5,), (2, capacity // 2), (2, capacity // 2), (2, n_z, parts, 4), (n_z, parts, 2), (parts, 2), (parts, 2), None, None, (2,),
            (n_z, parts), (n_z, parts), (n_z, parts, 2), (n_z, parts, 2), (4, 2, 4, columns), (2, 4, columns),
            (4, 2 * n_z), (4, 2 * n_z), (parts, 2), (parts, 2), (8,), (8,)]
    return pl.pallas_call(
        functools.partial(pair_kernel, n_z, (columns, slots, capacity, block)),
        out_shape=jax.ShapeDtypeStruct((columns, RB_DEV, block, block), jnp.bfloat16),
        in_specs=[hbm] * 6 + [smem] * 2,
        out_specs=hbm,
        scratch_shapes=[pltpu.VMEM(s, d) for s, d in vmem] + [pltpu.SMEM(s, jnp.int32) for s in words]
        + [dma if s is None else dma(s) for s in sems],
        compiler_params=pltpu.CompilerParams(
            collective_id=1, has_side_effects=True, vmem_limit_bytes=62 << 20),
        name="packed_pair_multiply",
    )(matrix_blocks, slab_blocks, matrix_rows, counts, slab_inner, used, counts, used)


def choose(n_row, n_col, *args):
    if n_row == 8 and n_col == 4 and args[0].shape[0] == 2 and args[0].shape[1] == SLOTS // 2:
        return paired(n_row // 2, *args)
    return on_device(n_row, n_col, *args)


def solution(mesh):
    return jax.shard_map(
        functools.partial(choose, mesh.shape["row"], mesh.shape["col"]),
        mesh=mesh,
        in_specs=(
            P("row", "col", None, None),
            P("row", "col"),
            P("row", "col"),
            P("row", "col", None, None),
            P("row", "col"),
            P("row"),
        ),
        out_specs=P("row", "col", None, None),
        check_vma=False,
    )
```

```python
import functools

import jax
import jax.numpy as jnp
from jax import lax
from jax.experimental import pallas as pl
from jax.experimental.pallas import tpu as pltpu
from jax.sharding import PartitionSpec as P

RB_DEV = 8
MESH = pl.DeviceIdType.MESH
CHUNKS = 6
PLAIN = CHUNKS - 1
UP, DOWN, SIDE = 0, 1, 2


def step_kernel(n_row, n_col, shape, a_ref, b_ref, rows_ref, counts_ref, inner_ref, slab_counts, out_ref,
                a_all, b_all, rows_all, counts_all, inner_all, rows_s, counts_s, inner_s,
                slot_s, source_s, stage, right, acc, sums_all, result,
                send, recv, b_send, b_recv, m_send, m_recv, s_send, s_recv, local, done):
    columns, slots, per_rank, capacity, block = shape
    each = CHUNKS // per_rank
    size = capacity // each
    n_z = n_row // 2
    r = lax.axis_index("row")
    c = lax.axis_index("col")
    z = lax.div(r, 2)
    y = lax.rem(r, 2)
    other = 1 - y
    beside = 2 * z + other
    has_up = z < n_z - 1
    has_down = z > 0

    barrier = pltpu.get_barrier_semaphore()
    for d in range(1, n_row):
        pl.semaphore_signal(barrier, inc=1, device_id={"row": lax.rem(r + d, n_row)}, device_id_type=MESH)
    for d in range(1, n_col):
        pl.semaphore_signal(barrier, inc=1, device_id={"col": lax.rem(c + d, n_col)}, device_id_type=MESH)
    pl.semaphore_wait(barrier, n_row + n_col - 2)

    def chunk(way, rank, ch, own=False):
        target = {UP: r + 2, DOWN: r - 2, SIDE: beside}[way]
        src = a_ref.at[ch] if own else a_all.at[rank, ch]
        return pltpu.make_async_remote_copy(
            src_ref=src, dst_ref=a_all.at[rank, ch], send_sem=send.at[way, rank, ch],
            recv_sem=recv.at[rank, ch], device_id={"row": target}, device_id_type=MESH)

    def arrived(rank, ch):
        pltpu.make_async_remote_copy(
            src_ref=a_all.at[rank, ch], dst_ref=a_all.at[rank, ch], send_sem=send.at[SIDE, rank, ch],
            recv_sem=recv.at[rank, ch], device_id={"row": beside}, device_id_type=MESH).wait_recv()

    def small(d):
        target = {"row": lax.rem(r + d, n_row)}
        return [
            pltpu.make_async_remote_copy(
                src_ref=src, dst_ref=dst.at[r], send_sem=m_send.at[n, d], recv_sem=m_recv.at[n, d],
                device_id=target, device_id_type=MESH)
            for n, (src, dst) in enumerate(((rows_ref, rows_all), (counts_ref, counts_all)))
        ]

    def slab(d):
        target = {"col": lax.rem(c + d, n_col)}
        return [
            pltpu.make_async_remote_copy(
                src_ref=inner_ref, dst_ref=inner_all.at[c], send_sem=b_send.at[1, d], recv_sem=b_recv.at[1, d],
                device_id=target, device_id_type=MESH),
            pltpu.make_async_remote_copy(
                src_ref=b_ref, dst_ref=b_all.at[c], send_sem=b_send.at[0, d], recv_sem=b_recv.at[0, d],
                device_id=target, device_id_type=MESH),
        ]

    def share(d):
        return pltpu.make_async_remote_copy(
            src_ref=sums_all.at[c], dst_ref=sums_all.at[c], send_sem=s_send.at[d], recv_sem=s_recv.at[d],
            device_id={"col": lax.rem(c + d, n_col)}, device_id_type=MESH)

    for ch in [PLAIN] + list(range(PLAIN)):
        chunk(SIDE, r, ch, True).start()
    for ch in range(CHUNKS):
        @pl.when(has_up)
        def _():
            chunk(UP, r, ch, True).start()

        @pl.when(has_down)
        def _():
            chunk(DOWN, r, ch, True).start()

    for d in range(1, n_row):
        for copy in small(d):
            copy.start()
    for d in range(1, n_col):
        for copy in slab(d):
            copy.start()
    mine = (
        pltpu.make_async_copy(a_ref, a_all.at[r], local.at[0]),
        pltpu.make_async_copy(b_ref, b_all.at[c], local.at[1]),
        pltpu.make_async_copy(rows_ref, rows_all.at[r], local.at[2]),
        pltpu.make_async_copy(counts_ref, counts_all.at[r], local.at[3]),
        pltpu.make_async_copy(inner_ref, inner_all.at[c], local.at[4]),
    )
    for copy in mine:
        copy.start()
    acc[...] = jnp.zeros_like(acc)

    arrived(beside, PLAIN)

    @pl.when(has_up)
    def _():
        chunk(UP, beside, PLAIN).start()

    @pl.when(has_down)
    def _():
        chunk(DOWN, beside, PLAIN).start()

    steps = [(0, ch, True) for ch in range(PLAIN)] + [(0, PLAIN, False), (1, PLAIN, False)]

    def sides(d, work):
        def one(side, carry):
            at = z + d * (2 * side - 1)

            @pl.when((at >= 0) & (at < n_z))
            def _():
                work(at)
            return carry

        lax.fori_loop(0, 2, one, 0)

    def relay(d, extra):
        for n, (flip, ch, cross) in enumerate(steps):
            column = other if flip else y

            @pl.when(z >= d)
            def _():
                rank = 2 * (z - d) + column
                arrived(rank, ch)

                @pl.when(has_up)
                def _():
                    chunk(UP, rank, ch).start()

                if cross:
                    chunk(SIDE, rank, ch).start()

            @pl.when(z + d < n_z)
            def _():
                rank = 2 * (z + d) + column
                arrived(rank, ch)

                @pl.when(has_down)
                def _():
                    chunk(DOWN, rank, ch).start()

                if cross:
                    chunk(SIDE, rank, ch).start()

            for work in extra.get(n, ()):
                work()

    def half(rank, kk):
        k = rank * per_rank + kk
        copy = pltpu.make_async_copy(a_all.at[rank, pl.ds(kk * each, each)], stage, local.at[0])
        copy.start()
        for j in range(columns):
            q = source_s[k, j]
            at = jnp.maximum(q, 0)
            value = b_all[lax.div(at, slots), j * slots + lax.rem(at, slots)]
            right[:, j * block:(j + 1) * block] = jnp.where(q >= 0, value, jnp.zeros_like(value))
        copy.wait()

        def block_row(i, carry):
            t = slot_s[k, i]
            at = jnp.maximum(t, 0)
            value = stage[lax.div(at, size), lax.rem(at, size)]
            left = jnp.where(t >= 0, value, jnp.zeros_like(value))
            rows = pl.ds(pl.multiple_of(i * block, block), block)
            acc[rows, :] += jnp.dot(left, right[...], preferred_element_type=jnp.float32)
            return carry

        lax.fori_loop(0, RB_DEV, block_row, 0, unroll=2)

    def whole(rank):
        def one(kk, carry):
            half(rank, kk)
            return carry

        lax.fori_loop(0, per_rank, one, 0)

    def await_side(rank, first, end):
        for ch in range(first, end):
            arrived(rank, ch)

    def own_whole(at):
        whole(2 * at + y)

    def side_whole(at):
        await_side(2 * at + other, 0, PLAIN)
        whole(2 * at + other)

    def own_half(kk):
        def work(at):
            half(2 * at + y, kk)
        return work

    def side_half(kk):
        def work(at):
            await_side(2 * at + other, kk * each, min(kk * each + each, PLAIN))
            half(2 * at + other, kk)
        return work

    relay(1, {})

    def complete():
        for copy in mine:
            copy.wait()
        for d in range(1, n_row):
            for copy in small(d):
                copy.wait()
        for d in range(1, n_col):
            for copy in slab(d):
                copy.wait()
        for n, (src, dst) in enumerate(((rows_all, rows_s), (counts_all, counts_s), (inner_all, inner_s))):
            copy = pltpu.make_async_copy(src, dst, local.at[5 + n])
            copy.start()
            copy.wait()
        lax.fori_loop(0, n_row, table, 0)

    def table(rank, carry):
        for kk in range(per_rank):
            k = rank * per_rank + kk
            for j in range(columns):
                q = jnp.int32(-1)
                for n in range(n_col * slots):
                    found = (inner_s[n // slots, j, n % slots] == k) & (n < slab_counts[j])
                    q = jnp.where(found, n, q)
                source_s[k, j] = q
            for i in range(RB_DEV):
                t = jnp.int32(-1)
                for n in range(capacity):
                    found = (rows_s[rank, kk, n] == i) & (n < counts_s[rank, 0, kk])
                    t = jnp.where(found, n, t)
                slot_s[k, i] = t
        return carry

    def side_here():
        await_side(beside, 0, PLAIN)
        whole(beside)

    relay(2, {
        0: (complete,),
        1: (lambda: whole(r),),
        2: (side_here,),
        3: (lambda: sides(1, own_whole),),
    })
    sides(1, side_whole)
    sides(2, own_whole)

    def later(d, carry):
        relay(d, {})
        sides(d - 1, side_whole)
        sides(d, own_whole)
        return carry

    lax.fori_loop(3, n_z - 1, later, 0)
    far = n_z - 1

    def side_halves(at):
        side_half(0)(at)
        side_half(1)(at)

    relay(far, {
        each - 1: (lambda: sides(far, own_half(0)), lambda: sides(far - 1, side_halves)),
        CHUNKS - 1: (lambda: sides(far, own_half(1)), lambda: sides(far, side_half(0))),
        CHUNKS: (lambda: sides(far, side_half(1)),),
    })

    def square(i, total):
        rows = pl.ds(pl.multiple_of(i * block, block), block)
        value = acc[rows, :]
        value = value * value
        return total + jnp.sum(value.reshape(block // 8, 8, columns * block), axis=0)

    total = lax.fori_loop(0, RB_DEV, square, jnp.zeros((8, columns * block), jnp.float32))
    sums_all[c] = total
    for d in range(1, n_col):
        share(d).start()

    for ch in range(CHUNKS):
        chunk(SIDE, r, ch, True).wait_send()

        @pl.when(has_up)
        def _():
            chunk(UP, r, ch, True).wait_send()

        @pl.when(has_down)
        def _():
            chunk(DOWN, r, ch, True).wait_send()

    @pl.when(has_up)
    def _():
        chunk(UP, beside, PLAIN).wait_send()

    @pl.when(has_down)
    def _():
        chunk(DOWN, beside, PLAIN).wait_send()

    def drain(d, carry):
        for flip, ch, cross in steps:
            column = other if flip else y

            @pl.when(z >= d)
            def _():
                rank = 2 * (z - d) + column

                @pl.when(has_up)
                def _():
                    chunk(UP, rank, ch).wait_send()

                if cross:
                    chunk(SIDE, rank, ch).wait_send()

            @pl.when(z + d < n_z)
            def _():
                rank = 2 * (z + d) + column

                @pl.when(has_down)
                def _():
                    chunk(DOWN, rank, ch).wait_send()

                if cross:
                    chunk(SIDE, rank, ch).wait_send()
        return carry

    lax.fori_loop(1, n_z, drain, 0)

    for d in range(1, n_col):
        share(d).wait()
    sums = jnp.sum(jnp.sum(sums_all[...], axis=0), axis=0, keepdims=True)
    factor = float(RB_DEV * n_col * block) / sums

    def scale(i, carry):
        rows = pl.ds(pl.multiple_of(i * block, block), block)
        value = acc[rows, :]
        value = (value * value * factor).astype(jnp.bfloat16)
        for j in range(columns):
            result[j, i] = value[:, j * block:(j + 1) * block]
            pltpu.make_async_copy(result.at[j, i], out_ref.at[j, i], done.at[j, i]).start()
        return carry

    lax.fori_loop(0, RB_DEV, scale, 0)

    def finish(i, carry):
        for j in range(columns):
            pltpu.make_async_copy(result.at[j, i], out_ref.at[j, i], done.at[j, i]).wait()
        return carry

    lax.fori_loop(0, RB_DEV, finish, 0)


def on_device(n_row, n_col, matrix_blocks, matrix_rows, matrix_counts, slab_blocks, slab_inner, slab_counts):
    per_rank, capacity, block = matrix_blocks.shape[0], matrix_blocks.shape[1], matrix_blocks.shape[2]
    columns, slots = slab_blocks.shape[0], slab_blocks.shape[1]
    held = per_rank * capacity
    size = held // CHUNKS
    a = matrix_blocks.reshape(CHUNKS, size, block, block)
    b = slab_blocks.reshape(columns * slots, block, block)
    matrix_counts = matrix_counts.reshape(1, per_rank)
    hbm = pl.BlockSpec(memory_space=pltpu.HBM)
    dma = pltpu.SemaphoreType.DMA
    rows_shape, counts_shape, inner_shape = (
        (n_row,) + matrix_rows.shape, (n_row,) + matrix_counts.shape, (n_col,) + slab_inner.shape)
    return pl.pallas_call(
        functools.partial(step_kernel, n_row, n_col, (columns, slots, per_rank, capacity, block)),
        out_shape=jax.ShapeDtypeStruct((columns, RB_DEV, block, block), jnp.bfloat16),
        in_specs=[hbm, hbm, hbm, hbm, hbm, pl.BlockSpec(memory_space=pltpu.SMEM)],
        out_specs=hbm,
        scratch_shapes=[
            pltpu.VMEM((n_row,) + a.shape, a.dtype),
            pltpu.VMEM((n_col,) + b.shape, b.dtype),
            pltpu.VMEM(rows_shape, jnp.int32),
            pltpu.VMEM(counts_shape, jnp.int32),
            pltpu.VMEM(inner_shape, jnp.int32),
            pltpu.SMEM(rows_shape, jnp.int32),
            pltpu.SMEM(counts_shape, jnp.int32),
            pltpu.SMEM(inner_shape, jnp.int32),
            pltpu.SMEM((n_row * per_rank, RB_DEV), jnp.int32),
            pltpu.SMEM((n_row * per_rank, columns), jnp.int32),
            pltpu.VMEM((CHUNKS // per_rank, size, block, block), a.dtype),
            pltpu.VMEM((block, columns * block), b.dtype),
            pltpu.VMEM((RB_DEV * block, columns * block), jnp.float32),
            pltpu.VMEM((n_col, 8, columns * block), jnp.float32),
            pltpu.VMEM((columns, RB_DEV, block, block), jnp.bfloat16),
            dma((3, n_row, CHUNKS)), dma((n_row, CHUNKS)),
            dma((2, n_col)), dma((2, n_col)), dma((2, n_row)), dma((2, n_row)), dma((n_col,)), dma((n_col,)),
            dma((8,)), dma((columns, RB_DEV)),
        ],
        compiler_params=pltpu.CompilerParams(
            collective_id=0, has_side_effects=True, vmem_limit_bytes=63 << 20),
        name="gather_multiply_normalize",
    )(a, b, matrix_rows, matrix_counts, slab_inner, slab_counts)


LIST = 9
OVER = 3
FIRST = LIST - OVER
SLOTS = LIST + OVER
GRAIN = 16
PARTS = 4
BY_Y = 3
LEVELS = 65535.0


def pair_kernel(n_z, shape, a_ref, b_ref, rows_ref, counts_ref, inner_ref, used_ref, counts_in, used_in, out_ref,
                cand, over, over_in, y_out, a_all, a_par, b_all, right, stage, lhs, acc, result,
                sums_acc, sums_all, c_out, c_in, top_out, top_in,
                rows_all, counts_all, counts_par, counts_near, inner_all, used_all,
                rows_s, counts_s, counts_par_s, inner_s, used_s, slot_s, source_s,
                local, ready, near_send, near_recv, z_send, z_recv, y_send, y_recv, o_send, o_recv,
                over_y, x_send, x_recv, p_send, p_recv, b_send, b_recv, m_send, m_recv, c_send, c_recv, s_send, s_recv):
    columns, slots, capacity, block = shape
    half = block // 2
    size = half // GRAIN // PARTS
    grains = half // GRAIN
    wide = columns * block
    r = lax.axis_index("row")
    c = lax.axis_index("col")
    z = lax.div(r, 2)
    y = lax.rem(r, 2)
    x = lax.div(c, 2)
    t = lax.rem(c, 2)
    has_up = z < n_z - 1
    has_down = z > 0
    middle = has_up & has_down
    end = jnp.logical_not(middle)
    c_x = 2 * (1 - x) + t
    c_t = 2 * x + 1 - t
    to_up = {"row": r + 2, "col": c}
    to_down = {"row": r - 2, "col": c}
    to_y = {"row": 2 * z + 1 - y, "col": c}
    to_x = {"row": r, "col": c_x}
    to_core = {"row": r, "col": c_t}

    def span(m):
        return pl.ds(m * size, size)

    def parts(work, first=0, end_at=PARTS):
        def one(m, carry):
            work(m)
            return carry

        lax.fori_loop(first, end_at, one, 0)

    def quarter(work, n):
        parts(work, n * PARTS // 4, (n + 1) * PARTS // 4)

    def remote(src, dst, send_sem, recv_sem, target):
        return pltpu.make_async_remote_copy(
            src_ref=src, dst_ref=dst, send_sem=send_sem, recv_sem=recv_sem,
            device_id=target, device_id_type=MESH)

    near = [(2 * z + (y if d < 4 else 1 - y), lax.rem(c + d, 4)) for d in range(1, 8)]

    barrier = pltpu.get_barrier_semaphore()
    for d in range(1, 2 * n_z):
        pl.semaphore_signal(
            barrier, inc=1, device_id={"row": lax.rem(r + d, 2 * n_z), "col": c}, device_id_type=MESH)
    for d, (row, col) in enumerate(near, 1):
        if d != 4:
            pl.semaphore_signal(barrier, inc=1, device_id={"row": row, "col": col}, device_id_type=MESH)
    pl.semaphore_wait(barrier, 2 * n_z - 1 + 6)

    def give_cand(n):
        return remote(a_ref.at[1 - t, pl.ds(2 * n, 2)], cand.at[pl.ds(t * capacity + 2 * n, 2)],
                      near_send.at[0, n], near_recv.at[0, n], to_core)

    def take_cand(n):
        return remote(a_ref.at[1 - t, pl.ds(2 * n, 2)], cand.at[pl.ds((1 - t) * capacity + 2 * n, 2)],
                      near_send.at[0, n], near_recv.at[0, n], to_core)

    def give_near():
        return remote(counts_ref, counts_near, near_send.at[1, 0], near_recv.at[1, 0], to_core)

    def metas(d):
        target = {"row": lax.rem(r + d, 2 * n_z), "col": c}
        return [remote(rows_ref, rows_all.at[r], m_send.at[0, d], m_recv.at[0, d], target),
                remote(counts_ref, counts_all.at[r], m_send.at[1, d], m_recv.at[1, d], target)]

    def inner_to(d):
        side = 0 if d < 4 else 1
        row, col = near[d - 1]
        return remote(inner_ref, inner_all.at[side, c], m_send.at[2, d], m_recv.at[2, d], {"row": row, "col": col})

    def used_to():
        return remote(used_ref, used_all, m_send.at[3, 0], m_recv.at[3, 0], to_y)

    def par_counts():
        return remote(counts_all, counts_par, m_send.at[3, 1], m_recv.at[3, 1], to_core)

    def slab(side, col, j):
        return b_all.at[side, col, j]

    def slab_copy(way, src, side, col, j, target, first=0, size=slots):
        piece = pl.ds(first, size)
        return remote(src.at[piece], b_all.at[side, col, j, piece], b_send.at[way, side, col, j],
                      b_recv.at[side, col, j], target)

    def slab_own(way, j, first=0, size=slots):
        side, target = {0: (0, to_core), 1: (0, to_x), 2: (1, to_y)}[way]
        return slab_copy(way, b_ref.at[j], side, c, j, target, first, size)

    def slab_core(side, col, j):
        return slab_copy(0, slab(side, col, j), side, col, j, to_core)

    def slab_diag(j, over_x):
        first, size = 0, slots
        if j == 0:
            first, size = (BY_Y, slots - BY_Y) if over_x else (0, BY_Y)
        if over_x:
            return slab_copy(3, slab(1, c, j), 1, c, j, to_x, first, size)
        return slab_copy(3, slab(0, c_x, j), 1, c_x, j, to_y, first, size)

    def slab_wait(side, col, j):
        slab_copy(0, slab(side, col, j), side, col, j, to_core).wait_recv()

    def y_copy(m, tail):
        at, many = ((0, FIRST), (FIRST, OVER))[tail]
        return remote(y_out.at[span(m), pl.ds(at, many)], a_all.at[z, span(m), y, pl.ds(at, many)],
                      y_send.at[m, tail], y_recv.at[m, tail], to_y)

    def y_wait(m, tail):
        at, many = ((0, FIRST), (FIRST, OVER))[tail]
        remote(y_out.at[span(m), pl.ds(at, many)], a_all.at[z, span(m), 1 - y, pl.ds(at, many)],
               y_send.at[m, tail], y_recv.at[m, tail], to_y).wait_recv()

    def y_over(to):
        return remote(y_out.at[:, pl.ds(LIST, OVER)], a_all.at[z, :, to, pl.ds(LIST, OVER)],
                      over_y.at[0], over_y.at[1], to_y)

    def over_copy():
        return remote(over, over_in, o_send, o_recv, to_x)

    def z_first(way, m, side, tail):
        at, many = ((0, FIRST), (FIRST, OVER))[tail]
        piece = a_all.at[z, span(m), side, pl.ds(at, many)]
        return remote(piece, piece, z_send.at[way, z, m, 2 * side + tail], z_recv.at[z, m, tail],
                      (to_up, to_down)[way])

    def z_piece(rank, m, tail):
        return a_all.at[rank, span(m), :, (pl.ds(0, FIRST), pl.ds(FIRST, OVER))[tail]]

    def z_next(way, rank, m, tail):
        piece = z_piece(rank, m, tail)
        return remote(piece, piece, z_send.at[way, rank, m, tail], z_recv.at[rank, m, tail], (to_up, to_down)[way])

    def z_wait(rank, m, tail):
        piece = z_piece(rank, m, tail)
        remote(piece, piece, z_send.at[0, rank, m, tail], z_recv.at[rank, m, tail], to_y).wait_recv()

    def moved(step, act):
        @pl.when(step == 0)
        def _():
            act(0, 1)

        @pl.when(step + 1 < PARTS)
        def _():
            act(step + 1, 1)

        act(step, 0)

    def x_copy(rank, m):
        return remote(a_all.at[rank, span(m), :, pl.ds(FIRST, OVER)], a_all.at[rank, span(m), :, pl.ds(LIST, OVER)],
                      x_send.at[rank, m], x_recv.at[rank, m], to_x)

    def p_copy(rank, m, over_part):
        piece = (rank, span(m), slice(None), (pl.ds(0, FIRST), pl.ds(FIRST, 2 * OVER))[over_part])
        return remote(a_all.at[piece], a_par.at[piece], p_send.at[rank, m, over_part], p_recv.at[rank, m, over_part],
                      to_core)

    def c_copy(m):
        return remote(c_out.at[span(m)], c_in.at[span(m)], c_send.at[m, 0], c_recv.at[m, 0], to_y)

    def top_copy(m):
        return remote(top_out.at[m], top_in.at[m], c_send.at[m, 1], c_recv.at[m, 1], to_y)

    def sums_copy(d):
        row, col = near[d - 1]
        side = 0 if d < 4 else 1
        return remote(sums_acc.at[side], sums_all.at[side, c], s_send.at[d], s_recv.at[d], {"row": row, "col": col})

    def both(m, side, tail, act):
        @pl.when(has_up)
        def _():
            act(z_first(0, m, side, tail))

        @pl.when(has_down)
        def _():
            act(z_first(1, m, side, tail))

    def start(copy):
        copy.start()

    def wait_send(copy):
        copy.wait_send()

    def rank_of(n):
        low = z < n_z // 2
        at = jnp.where(low, z, n_z - 1 - z)
        rank = n - 1 + jnp.where(n - 1 >= at, 1, 0)
        rank = jnp.where(low, rank, n_z - 1 - rank)
        return jnp.where(n == 0, z, rank)

    mine = [pltpu.make_async_copy(a_ref.at[t], cand.at[pl.ds(t * capacity, capacity)], local.at[0])]
    give_near().start()
    for n in range(capacity // 2):
        give_cand(n).start()
    mine[0].start()
    slab_own(2, 1, 0, 2).start()
    slab_own(1, 0, 0, 1).start()
    mine += [
        pltpu.make_async_copy(rows_ref, rows_all.at[r], local.at[1]),
        pltpu.make_async_copy(counts_ref, counts_all.at[r], local.at[2]),
        pltpu.make_async_copy(inner_ref, inner_all.at[0, c], local.at[3]),
        pltpu.make_async_copy(b_ref, b_all.at[0, c], local.at[4]),
    ]
    acc[...] = jnp.zeros_like(acc)
    sums_acc[...] = jnp.zeros_like(sums_acc)

    give_near().wait_recv()
    at_rank = lax.broadcasted_iota(jnp.int32, (1, 2), 1)
    near_count = jnp.max(jnp.where(at_rank == t, counts_near[...], 0))
    mine[0].wait()
    for n in range(capacity // 2):
        take_cand(n).wait_recv()

    own_count = counts_in[0, t]
    first_count = jnp.where(t == 0, own_count, near_count)
    total_count = own_count + near_count

    def place(p):
        return jnp.where(p < first_count, p, capacity + jnp.minimum(jnp.maximum(p - first_count, 0), capacity - 1))

    for p in range(OVER):
        over[p] = cand[place(LIST + p)]
    over_copy().start()

    def rows_at(side, m):
        return pl.ds(pl.multiple_of(side * half + m * GRAIN, GRAIN), GRAIN)

    def pack(p, carry):
        at = place(p)
        for g in range(grains):
            a_all[z, g, y, p] = cand[at, rows_at(y, g), :]
            y_out[g, p] = cand[at, rows_at(1 - y, g), :]
        return carry

    def pack_tail(p, carry):
        at = place(FIRST + p)
        keep = total_count > FIRST
        for g in range(grains):
            for side, there in ((y, True), (1 - y, False)):
                value = jnp.where(keep, cand[at, rows_at(side, g), :], over_in[p, rows_at(side, g), :])
                if there:
                    a_all[z, g, y, FIRST + p] = value
                else:
                    y_out[g, FIRST + p] = value
        return carry

    def pack_over(p, carry):
        for g in range(grains):
            a_all[z, g, y, LIST + p] = over[p, rows_at(y, g), :]
            y_out[g, LIST + p] = over[p, rows_at(1 - y, g), :]
        return carry

    lax.fori_loop(0, FIRST, pack, 0)
    def own_main(m):
        y_copy(m, 0).start()
        both(m, y, 0, start)

    def beside_main(m):
        y_wait(m, 0)
        both(m, 1 - y, 0, start)
        p_copy(z, m, 0).start()

    def own_tail(m):
        y_copy(m, 1).start()
        both(m, y, 1, start)

    def beside_tail(m):
        y_wait(m, 1)
        both(m, 1 - y, 1, start)

    parts(own_main)
    slab_own(1, 0, 1, slots - 1).start()
    for j in range(columns):
        slab_own(0, j).start()
    for d in range(1, 2 * n_z):
        for copy in metas(d):
            copy.start()
    for d in range(1, 8):
        inner_to(d).start()
    used_to().start()
    for copy in mine[1:]:
        copy.start()
    lax.fori_loop(0, OVER, pack_over, 0)
    parts(beside_main)
    over_copy().wait_recv()
    lax.fori_loop(0, OVER, pack_tail, 0)
    parts(own_tail)
    slab_own(1, 1).start()
    slab_own(2, 1, 2, slots - 2).start()
    parts(beside_tail)
    slab_own(2, 0).start()

    def relay(n, step):
        rank = rank_of(n)

        def act(m, tail):
            z_wait(rank, m, tail)

            @pl.when((rank < z) & has_up)
            def _():
                z_next(0, rank, m, tail).start()

            @pl.when((rank > z) & has_down)
            def _():
                z_next(1, rank, m, tail).start()

        moved(step, act)
        p_copy(rank, step, 0).start()

    def near_x(m):
        x_copy(rank_of(1), m).start()

        @pl.when(middle)
        def _():
            x_copy(rank_of(2), m).start()

    def near_relay(m):
        relay(1, m)

        @pl.when(middle)
        def _():
            relay(2, m)

    def far_relay(m):
        relay(jnp.where(middle, 3, 2), m)

    def far_x(m):
        x_copy(rank_of(jnp.where(middle, 3, 2)), m).start()

    def table(k, carry):
        rank = lax.div(k, 2)
        kk = lax.rem(k, 2)
        for side in range(2):
            for j in range(columns):
                limit = used_in[0, j] if side == 0 else used_s[0, j]
                q = jnp.int32(-1)
                for n in range(4 * slots):
                    found = (inner_s[side, n // slots, j, n % slots] == k) & (n < limit)
                    q = jnp.where(found, n, q)
                source_s[k, side * columns + j] = q
        base = jnp.where(t == 1, counts_par_s[rank, 0, kk], 0)
        live = counts_s[rank, 0, kk]
        for i in range(RB_DEV):
            p = jnp.int32(-1)
            for n in range(capacity):
                found = (rows_s[rank, kk, n] == i) & (n < live)
                p = jnp.where(found, n + base, p)
            slot_s[k, i] = p
        return carry

    def complete():
        for copy in mine[1:4]:
            copy.wait()
        for d in range(1, 2 * n_z):
            for copy in metas(d):
                copy.wait()
        par_counts().start()
        for d in range(1, 8):
            inner_to(d).wait()
        used_to().wait()
        par_counts().wait()
        for n, (src, dst) in enumerate((
                (rows_all, rows_s), (counts_all, counts_s), (counts_par, counts_par_s), (inner_all, inner_s),
                (used_all, used_s))):
            pltpu.make_async_copy(src, dst, ready.at[n]).start()
        for n, (src, dst) in enumerate((
                (rows_all, rows_s), (counts_all, counts_s), (counts_par, counts_par_s), (inner_all, inner_s),
                (used_all, used_s))):
            pltpu.make_async_copy(src, dst, ready.at[n]).wait()
        lax.fori_loop(0, 4 * n_z, table, 0)

    def give_core(rank, m):
        x_copy(rank, m).wait_recv()
        p_copy(rank, m, 1).start()

    def near_core(m):
        give_core(rank_of(1), m)

        @pl.when(middle)
        def _():
            give_core(rank_of(2), m)

    def slab_next(side, col, j):
        slab_wait(side, col, j)
        slab_core(side, col, j).start()

    def forward(m):
        near_x(m)
        far_x(m)

    slab_next(0, c_x, 0)
    slab_diag(0, False).start()
    parts(near_relay)
    slab_next(1, c, 1)
    slab_diag(1, True).start()
    slab_next(0, c_x, 1)
    complete()
    quarter(far_relay, 0)
    slab_next(1, c, 0)
    slab_diag(0, True).start()
    y_over(y).start()
    quarter(far_relay, 1)
    slab_next(1, c_x, 1)
    quarter(forward, 0)
    slab_next(1, c_x, 0)
    quarter(forward, 1)
    quarter(far_relay, 2)

    mine[4].wait()
    for j in range(columns):
        for side in range(2):
            for col in (c_t, 2 * (1 - x) + 1 - t):
                slab_wait(side, col, j)

    def gather_right(n, carry):
        rank = lax.div(n, 4)
        side = lax.rem(lax.div(n, 2), 2)
        u = lax.rem(n, 2)
        k = 2 * (2 * rank + side) + jnp.where(u == 0, t, 1 - t)
        rows = pl.ds(pl.multiple_of(lax.rem(n, 4) * block, block), block)
        for s in range(2):
            for j in range(columns):
                q = source_s[k, s * columns + j]
                at = jnp.maximum(q, 0)
                value = b_all[s, lax.div(at, slots), j, lax.rem(at, slots)]
                to = (s * columns + j) * block
                right[rank, rows, to:to + block] = jnp.where(q >= 0, value, jnp.zeros_like(value))
        return carry

    lax.fori_loop(0, 4 * n_z, gather_right, 0)

    tall = RB_DEV * GRAIN

    def multiply(rank, m):
        p_copy(rank, m, 0).wait_recv()
        p_copy(rank, m, 1).wait_recv()
        for g in range(size):
            for u, source in enumerate((a_all, a_par)):
                for side in range(2):
                    stage[u, side, g] = source[rank, m * size + g, side]
        for side in range(2):
            for u in range(2):
                k = 2 * (2 * rank + side) + (t if u == 0 else 1 - t)
                at = (2 * side + u) * block
                for i in range(RB_DEV):
                    p = slot_s[k, i]
                    for g in range(size):
                        value = stage[u, side, g, jnp.maximum(p, 0)]
                        to = g * tall + i * GRAIN
                        lhs[to:to + GRAIN, at:at + block] = jnp.where(p >= 0, value, jnp.zeros_like(value))
        for n in range(2):
            cols = slice(n * wide, (n + 1) * wide)
            product = jnp.dot(lhs[...], right[rank, :, cols], preferred_element_type=jnp.float32)
            acc[span(m), :, cols] += product.reshape(size, tall, wide)

    def cores(m):
        near_core(m)
        give_core(rank_of(jnp.where(middle, 3, 2)), m)

    def last_relay(m):
        rank = rank_of(3)

        def act(n, tail):
            z_wait(rank, n, tail)
            if tail:
                x_copy(rank, n).start()

        moved(m, act)
        p_copy(rank, m, 0).start()
        give_core(rank, m)

    def finish_part(m):
        for n in range(2):
            value = acc[span(m), :, n * wide:(n + 1) * wide]
            squared = value * value
            sums_acc[n] += jnp.sum(squared.reshape(-1, 8, wide), axis=0)
        value = acc[span(m), :, wide:].reshape(-1, wide)
        top = jnp.maximum(jnp.max(value, axis=0, keepdims=True), 1e-30)
        scaled = value * (LEVELS / top) + 0.5
        coded = jnp.minimum(scaled, LEVELS).astype(jnp.int32)
        word = lax.shift_left(coded[:, :block], jnp.int32(16)) | coded[:, block:]
        c_out[span(m)] = word.reshape(size, tall, block)
        top_out[m] = jnp.broadcast_to(top, (8, wide))
        c_copy(m).start()
        top_copy(m).start()

    quarter(forward, 2)
    quarter(far_relay, 3)
    quarter(forward, 3)
    y_over(1 - y).wait_recv()
    parts(lambda m: p_copy(z, m, 1).start())
    cores(0)

    def drain_start():
        give_near().wait_send()
        for n in range(capacity // 2):
            give_cand(n).wait_send()
        over_copy().wait_send()
        y_over(y).wait_send()
        for way in range(3):
            for j in range(columns):
                slab_own(way, j).wait_send()
        for j in range(columns):
            slab_diag(j, True).wait_send()
            if j == 0:
                slab_diag(j, False).wait_send()
            for side, col in ((0, c_x), (1, c), (1, c_x)):
                slab_core(side, col, j).wait_send()

    def drain_rank(rank, m):
        p_copy(rank, m, 0).wait_send()
        p_copy(rank, m, 1).wait_send()

        @pl.when(rank != z)
        def _():
            x_copy(rank, m).wait_send()

    def drain_part(m):
        for tail in range(2):
            y_copy(m, tail).wait_send()
            both(m, 0, tail, wait_send)
            both(m, 1, tail, wait_send)

        def one(n, carry):
            drain_rank(rank_of(n), m)
            return carry

        lax.fori_loop(0, 3, one, 0)

    def drain_last(m):
        drain_rank(rank_of(3), m)
        c_copy(m).wait_send()
        top_copy(m).wait_send()

        @pl.when(middle)
        def _():
            def one(rank, carry):
                for tail in range(2):
                    @pl.when((rank < z) & has_up)
                    def _():
                        z_next(0, rank, m, tail).wait_send()

                    @pl.when((rank > z) & has_down)
                    def _():
                        z_next(1, rank, m, tail).wait_send()
                return carry

            lax.fori_loop(0, n_z, one, 0)

    def one_part(m):
        @pl.when(m + 1 < PARTS)
        def _():
            cores(m + 1)

        def one_rank(n, carry):
            @pl.when((n == 3) & end)
            def _():
                last_relay(m)

            multiply(rank_of(jnp.where(n == 3, 3, lax.rem(n + 1, 3))), m)
            return carry

        lax.fori_loop(0, 4, one_rank, 0)
        finish_part(m)

        @pl.when(m + 1 < PARTS)
        def _():
            @pl.when(m == 0)
            def _():
                drain_start()

            drain_part(m)

    parts(one_part)
    for d in range(1, 8):
        sums_copy(d).start()
    drain_part(PARTS - 1)

    for d in range(1, 8):
        sums_copy(d).wait()
    sums = sums_acc[0]
    for d in range(1, 8):
        sums = sums + sums_all[0 if d < 4 else 1, near[d - 1][1]]
    factor = float(RB_DEV * 4 * block) / jnp.sum(sums, axis=0, keepdims=True)

    def store(value, g, side):
        value = value.astype(jnp.bfloat16)
        for i in range(RB_DEV):
            for j in range(columns):
                result[j, i, rows_at(side, g), :] = value[i * GRAIN:(i + 1) * GRAIN, j * block:(j + 1) * block]

    def scale_own(g, carry):
        value = acc[g, :, :wide]
        store(value * value * factor, g, y)
        return carry

    def out_half(side):
        rows = pl.ds(pl.multiple_of(side * half, half), half)
        return pltpu.make_async_copy(
            result.at[:, :, rows], out_ref.at[:, :, rows], local.at[6 + side])

    lax.fori_loop(0, grains, scale_own, 0)
    out_half(y).start()
    def scale_other(m):
        c_copy(m).wait_recv()
        top_copy(m).wait_recv()
        step = top_in[m][0:1, :] * (1.0 / LEVELS)

        def one(g, carry):
            word = c_in[g]
            upper = lax.shift_right_logical(word, jnp.int32(16)).astype(jnp.float32)
            lower = (word & jnp.int32(65535)).astype(jnp.float32)
            value = jnp.concatenate([upper, lower], axis=1) * step
            store(value * value * factor, g, 1 - y)
            return carry

        lax.fori_loop(m * size, (m + 1) * size, one, 0)

    parts(scale_other)
    out_half(1 - y).start()
    parts(drain_last)
    out_half(0).wait()
    out_half(1).wait()


def paired(n_z, matrix_blocks, matrix_rows, matrix_counts, slab_blocks, slab_inner, slab_counts):
    capacity, block = matrix_blocks.shape[1], matrix_blocks.shape[2]
    columns, slots = slab_blocks.shape[0], slab_blocks.shape[1]
    grains = block // 2 // GRAIN
    counts = matrix_counts.reshape(1, 2)
    used = slab_counts.reshape(1, columns)
    hbm = pl.BlockSpec(memory_space=pltpu.HBM)
    smem = pl.BlockSpec(memory_space=pltpu.SMEM)
    dma = pltpu.SemaphoreType.DMA
    half_word, full = jnp.bfloat16, jnp.float32
    rows_shape, counts_shape, inner_shape = (2 * n_z, 2, capacity), (2 * n_z, 1, 2), (2, 4) + slab_inner.shape
    lists = (n_z, grains, 2, SLOTS, GRAIN, block)
    parts, most = PARTS, grains // PARTS
    vmem = [
        ((2 * capacity, block, block), half_word),
        ((OVER, block, block), half_word),
        ((OVER, block, block), half_word),
        ((grains, SLOTS, GRAIN, block), half_word),
        (lists, half_word),
        (lists, half_word),
        ((2, 4) + slab_blocks.shape, half_word),
        ((n_z, 4 * block, 2 * columns * block), half_word),
        ((2, 2, most, SLOTS, GRAIN, block), half_word),
        ((most * RB_DEV * GRAIN, 4 * block), half_word),
        ((grains, RB_DEV * GRAIN, 2 * columns * block), full),
        ((columns, RB_DEV, block, block), half_word),
        ((2, 8, columns * block), full),
        ((2, 4, 8, columns * block), full),
        ((grains, RB_DEV * GRAIN, block), jnp.int32),
        ((grains, RB_DEV * GRAIN, block), jnp.int32),
        ((parts, 8, columns * block), full),
        ((parts, 8, columns * block), full),
        (rows_shape, jnp.int32), (counts_shape, jnp.int32), (counts_shape, jnp.int32), ((1, 2), jnp.int32),
        (inner_shape, jnp.int32), ((1, columns), jnp.int32),
    ]
    words = [rows_shape, counts_shape, counts_shape, inner_shape, (1, columns),
             (4 * n_z, RB_DEV), (4 * n_z, 2 * columns)]
    sems = [(8,), (5,), (2, capacity // 2), (2, capacity // 2), (2, n_z, parts, 4), (n_z, parts, 2), (parts, 2), (parts, 2), None, None, (2,),
            (n_z, parts), (n_z, parts), (n_z, parts, 2), (n_z, parts, 2), (4, 2, 4, columns), (2, 4, columns),
            (4, 2 * n_z), (4, 2 * n_z), (parts, 2), (parts, 2), (8,), (8,)]
    return pl.pallas_call(
        functools.partial(pair_kernel, n_z, (columns, slots, capacity, block)),
        out_shape=jax.ShapeDtypeStruct((columns, RB_DEV, block, block), jnp.bfloat16),
        in_specs=[hbm] * 6 + [smem] * 2,
        out_specs=pl.BlockSpec(memory_space=pl.ANY),
        scratch_shapes=[pltpu.VMEM(s, d) for s, d in vmem] + [pltpu.SMEM(s, jnp.int32) for s in words]
        + [dma if s is None else dma(s) for s in sems],
        compiler_params=pltpu.CompilerParams(
            collective_id=1, has_side_effects=True, vmem_limit_bytes=44 << 20),
        name="packed_pair_multiply",
    )(*[pltpu.with_memory_space_constraint(v, pltpu.HBM) for v in (
        matrix_blocks, slab_blocks, matrix_rows, counts, slab_inner, used)], counts, used)


def choose(n_row, n_col, *args):
    if n_row == 8 and n_col == 4 and args[0].shape[0] == 2 and args[0].shape[1] == SLOTS // 2:
        return paired(n_row // 2, *args)
    return on_device(n_row, n_col, *args)


def solution(mesh):
    return jax.shard_map(
        functools.partial(choose, mesh.shape["row"], mesh.shape["col"]),
        mesh=mesh,
        in_specs=(
            P("row", "col", None, None),
            P("row", "col"),
            P("row", "col"),
            P("row", "col", None, None),
            P("row", "col"),
            P("row"),
        ),
        out_specs=P("row", "col", None, None),
        check_vma=False,
    )
```

```python
import functools

import jax
import jax.numpy as jnp
from jax import lax
from jax.experimental import pallas as pl
from jax.experimental.pallas import tpu as pltpu
from jax.sharding import PartitionSpec as P

RB_DEV = 8
MESH = pl.DeviceIdType.MESH
CHUNKS = 6
PLAIN = CHUNKS - 1
UP, DOWN, SIDE = 0, 1, 2


def step_kernel(n_row, n_col, shape, a_ref, b_ref, rows_ref, counts_ref, inner_ref, slab_counts, out_ref,
                a_all, b_all, rows_all, counts_all, inner_all, rows_s, counts_s, inner_s,
                slot_s, source_s, stage, right, acc, sums_all, result,
                send, recv, b_send, b_recv, m_send, m_recv, s_send, s_recv, local, done):
    columns, slots, per_rank, capacity, block = shape
    each = CHUNKS // per_rank
    size = capacity // each
    n_z = n_row // 2
    r = lax.axis_index("row")
    c = lax.axis_index("col")
    z = lax.div(r, 2)
    y = lax.rem(r, 2)
    other = 1 - y
    beside = 2 * z + other
    has_up = z < n_z - 1
    has_down = z > 0

    barrier = pltpu.get_barrier_semaphore()
    for d in range(1, n_row):
        pl.semaphore_signal(barrier, inc=1, device_id={"row": lax.rem(r + d, n_row)}, device_id_type=MESH)
    for d in range(1, n_col):
        pl.semaphore_signal(barrier, inc=1, device_id={"col": lax.rem(c + d, n_col)}, device_id_type=MESH)
    pl.semaphore_wait(barrier, n_row + n_col - 2)

    def chunk(way, rank, ch, own=False):
        target = {UP: r + 2, DOWN: r - 2, SIDE: beside}[way]
        src = a_ref.at[ch] if own else a_all.at[rank, ch]
        return pltpu.make_async_remote_copy(
            src_ref=src, dst_ref=a_all.at[rank, ch], send_sem=send.at[way, rank, ch],
            recv_sem=recv.at[rank, ch], device_id={"row": target}, device_id_type=MESH)

    def arrived(rank, ch):
        pltpu.make_async_remote_copy(
            src_ref=a_all.at[rank, ch], dst_ref=a_all.at[rank, ch], send_sem=send.at[SIDE, rank, ch],
            recv_sem=recv.at[rank, ch], device_id={"row": beside}, device_id_type=MESH).wait_recv()

    def small(d):
        target = {"row": lax.rem(r + d, n_row)}
        return [
            pltpu.make_async_remote_copy(
                src_ref=src, dst_ref=dst.at[r], send_sem=m_send.at[n, d], recv_sem=m_recv.at[n, d],
                device_id=target, device_id_type=MESH)
            for n, (src, dst) in enumerate(((rows_ref, rows_all), (counts_ref, counts_all)))
        ]

    def slab(d):
        target = {"col": lax.rem(c + d, n_col)}
        return [
            pltpu.make_async_remote_copy(
                src_ref=inner_ref, dst_ref=inner_all.at[c], send_sem=b_send.at[1, d], recv_sem=b_recv.at[1, d],
                device_id=target, device_id_type=MESH),
            pltpu.make_async_remote_copy(
                src_ref=b_ref, dst_ref=b_all.at[c], send_sem=b_send.at[0, d], recv_sem=b_recv.at[0, d],
                device_id=target, device_id_type=MESH),
        ]

    def share(d):
        return pltpu.make_async_remote_copy(
            src_ref=sums_all.at[c], dst_ref=sums_all.at[c], send_sem=s_send.at[d], recv_sem=s_recv.at[d],
            device_id={"col": lax.rem(c + d, n_col)}, device_id_type=MESH)

    for ch in [PLAIN] + list(range(PLAIN)):
        chunk(SIDE, r, ch, True).start()
    for ch in range(CHUNKS):
        @pl.when(has_up)
        def _():
            chunk(UP, r, ch, True).start()

        @pl.when(has_down)
        def _():
            chunk(DOWN, r, ch, True).start()

    for d in range(1, n_row):
        for copy in small(d):
            copy.start()
    for d in range(1, n_col):
        for copy in slab(d):
            copy.start()
    mine = (
        pltpu.make_async_copy(a_ref, a_all.at[r], local.at[0]),
        pltpu.make_async_copy(b_ref, b_all.at[c], local.at[1]),
        pltpu.make_async_copy(rows_ref, rows_all.at[r], local.at[2]),
        pltpu.make_async_copy(counts_ref, counts_all.at[r], local.at[3]),
        pltpu.make_async_copy(inner_ref, inner_all.at[c], local.at[4]),
    )
    for copy in mine:
        copy.start()
    acc[...] = jnp.zeros_like(acc)

    arrived(beside, PLAIN)

    @pl.when(has_up)
    def _():
        chunk(UP, beside, PLAIN).start()

    @pl.when(has_down)
    def _():
        chunk(DOWN, beside, PLAIN).start()

    steps = [(0, ch, True) for ch in range(PLAIN)] + [(0, PLAIN, False), (1, PLAIN, False)]

    def sides(d, work):
        def one(side, carry):
            at = z + d * (2 * side - 1)

            @pl.when((at >= 0) & (at < n_z))
            def _():
                work(at)
            return carry

        lax.fori_loop(0, 2, one, 0)

    def relay(d, extra):
        for n, (flip, ch, cross) in enumerate(steps):
            column = other if flip else y

            @pl.when(z >= d)
            def _():
                rank = 2 * (z - d) + column
                arrived(rank, ch)

                @pl.when(has_up)
                def _():
                    chunk(UP, rank, ch).start()

                if cross:
                    chunk(SIDE, rank, ch).start()

            @pl.when(z + d < n_z)
            def _():
                rank = 2 * (z + d) + column
                arrived(rank, ch)

                @pl.when(has_down)
                def _():
                    chunk(DOWN, rank, ch).start()

                if cross:
                    chunk(SIDE, rank, ch).start()

            for work in extra.get(n, ()):
                work()

    def half(rank, kk):
        k = rank * per_rank + kk
        copy = pltpu.make_async_copy(a_all.at[rank, pl.ds(kk * each, each)], stage, local.at[0])
        copy.start()
        for j in range(columns):
            q = source_s[k, j]
            at = jnp.maximum(q, 0)
            value = b_all[lax.div(at, slots), j * slots + lax.rem(at, slots)]
            right[:, j * block:(j + 1) * block] = jnp.where(q >= 0, value, jnp.zeros_like(value))
        copy.wait()

        def block_row(i, carry):
            t = slot_s[k, i]
            at = jnp.maximum(t, 0)
            value = stage[lax.div(at, size), lax.rem(at, size)]
            left = jnp.where(t >= 0, value, jnp.zeros_like(value))
            rows = pl.ds(pl.multiple_of(i * block, block), block)
            acc[rows, :] += jnp.dot(left, right[...], preferred_element_type=jnp.float32)
            return carry

        lax.fori_loop(0, RB_DEV, block_row, 0, unroll=2)

    def whole(rank):
        def one(kk, carry):
            half(rank, kk)
            return carry

        lax.fori_loop(0, per_rank, one, 0)

    def await_side(rank, first, end):
        for ch in range(first, end):
            arrived(rank, ch)

    def own_whole(at):
        whole(2 * at + y)

    def side_whole(at):
        await_side(2 * at + other, 0, PLAIN)
        whole(2 * at + other)

    def own_half(kk):
        def work(at):
            half(2 * at + y, kk)
        return work

    def side_half(kk):
        def work(at):
            await_side(2 * at + other, kk * each, min(kk * each + each, PLAIN))
            half(2 * at + other, kk)
        return work

    relay(1, {})

    def complete():
        for copy in mine:
            copy.wait()
        for d in range(1, n_row):
            for copy in small(d):
                copy.wait()
        for d in range(1, n_col):
            for copy in slab(d):
                copy.wait()
        for n, (src, dst) in enumerate(((rows_all, rows_s), (counts_all, counts_s), (inner_all, inner_s))):
            copy = pltpu.make_async_copy(src, dst, local.at[5 + n])
            copy.start()
            copy.wait()
        lax.fori_loop(0, n_row, table, 0)

    def table(rank, carry):
        for kk in range(per_rank):
            k = rank * per_rank + kk
            for j in range(columns):
                q = jnp.int32(-1)
                for n in range(n_col * slots):
                    found = (inner_s[n // slots, j, n % slots] == k) & (n < slab_counts[j])
                    q = jnp.where(found, n, q)
                source_s[k, j] = q
            for i in range(RB_DEV):
                t = jnp.int32(-1)
                for n in range(capacity):
                    found = (rows_s[rank, kk, n] == i) & (n < counts_s[rank, 0, kk])
                    t = jnp.where(found, n, t)
                slot_s[k, i] = t
        return carry

    def side_here():
        await_side(beside, 0, PLAIN)
        whole(beside)

    relay(2, {
        0: (complete,),
        1: (lambda: whole(r),),
        2: (side_here,),
        3: (lambda: sides(1, own_whole),),
    })
    sides(1, side_whole)
    sides(2, own_whole)

    def later(d, carry):
        relay(d, {})
        sides(d - 1, side_whole)
        sides(d, own_whole)
        return carry

    lax.fori_loop(3, n_z - 1, later, 0)
    far = n_z - 1

    def side_halves(at):
        side_half(0)(at)
        side_half(1)(at)

    relay(far, {
        each - 1: (lambda: sides(far, own_half(0)), lambda: sides(far - 1, side_halves)),
        CHUNKS - 1: (lambda: sides(far, own_half(1)), lambda: sides(far, side_half(0))),
        CHUNKS: (lambda: sides(far, side_half(1)),),
    })

    def square(i, total):
        rows = pl.ds(pl.multiple_of(i * block, block), block)
        value = acc[rows, :]
        value = value * value
        return total + jnp.sum(value.reshape(block // 8, 8, columns * block), axis=0)

    total = lax.fori_loop(0, RB_DEV, square, jnp.zeros((8, columns * block), jnp.float32))
    sums_all[c] = total
    for d in range(1, n_col):
        share(d).start()

    for ch in range(CHUNKS):
        chunk(SIDE, r, ch, True).wait_send()

        @pl.when(has_up)
        def _():
            chunk(UP, r, ch, True).wait_send()

        @pl.when(has_down)
        def _():
            chunk(DOWN, r, ch, True).wait_send()

    @pl.when(has_up)
    def _():
        chunk(UP, beside, PLAIN).wait_send()

    @pl.when(has_down)
    def _():
        chunk(DOWN, beside, PLAIN).wait_send()

    def drain(d, carry):
        for flip, ch, cross in steps:
            column = other if flip else y

            @pl.when(z >= d)
            def _():
                rank = 2 * (z - d) + column

                @pl.when(has_up)
                def _():
                    chunk(UP, rank, ch).wait_send()

                if cross:
                    chunk(SIDE, rank, ch).wait_send()

            @pl.when(z + d < n_z)
            def _():
                rank = 2 * (z + d) + column

                @pl.when(has_down)
                def _():
                    chunk(DOWN, rank, ch).wait_send()

                if cross:
                    chunk(SIDE, rank, ch).wait_send()
        return carry

    lax.fori_loop(1, n_z, drain, 0)

    for d in range(1, n_col):
        share(d).wait()
    sums = jnp.sum(jnp.sum(sums_all[...], axis=0), axis=0, keepdims=True)
    factor = float(RB_DEV * n_col * block) / sums

    def scale(i, carry):
        rows = pl.ds(pl.multiple_of(i * block, block), block)
        value = acc[rows, :]
        value = (value * value * factor).astype(jnp.bfloat16)
        for j in range(columns):
            result[j, i] = value[:, j * block:(j + 1) * block]
            pltpu.make_async_copy(result.at[j, i], out_ref.at[j, i], done.at[j, i]).start()
        return carry

    lax.fori_loop(0, RB_DEV, scale, 0)

    def finish(i, carry):
        for j in range(columns):
            pltpu.make_async_copy(result.at[j, i], out_ref.at[j, i], done.at[j, i]).wait()
        return carry

    lax.fori_loop(0, RB_DEV, finish, 0)


def on_device(n_row, n_col, matrix_blocks, matrix_rows, matrix_counts, slab_blocks, slab_inner, slab_counts):
    per_rank, capacity, block = matrix_blocks.shape[0], matrix_blocks.shape[1], matrix_blocks.shape[2]
    columns, slots = slab_blocks.shape[0], slab_blocks.shape[1]
    held = per_rank * capacity
    size = held // CHUNKS
    a = matrix_blocks.reshape(CHUNKS, size, block, block)
    b = slab_blocks.reshape(columns * slots, block, block)
    matrix_counts = matrix_counts.reshape(1, per_rank)
    hbm = pl.BlockSpec(memory_space=pltpu.HBM)
    dma = pltpu.SemaphoreType.DMA
    rows_shape, counts_shape, inner_shape = (
        (n_row,) + matrix_rows.shape, (n_row,) + matrix_counts.shape, (n_col,) + slab_inner.shape)
    return pl.pallas_call(
        functools.partial(step_kernel, n_row, n_col, (columns, slots, per_rank, capacity, block)),
        out_shape=jax.ShapeDtypeStruct((columns, RB_DEV, block, block), jnp.bfloat16),
        in_specs=[hbm, hbm, hbm, hbm, hbm, pl.BlockSpec(memory_space=pltpu.SMEM)],
        out_specs=hbm,
        scratch_shapes=[
            pltpu.VMEM((n_row,) + a.shape, a.dtype),
            pltpu.VMEM((n_col,) + b.shape, b.dtype),
            pltpu.VMEM(rows_shape, jnp.int32),
            pltpu.VMEM(counts_shape, jnp.int32),
            pltpu.VMEM(inner_shape, jnp.int32),
            pltpu.SMEM(rows_shape, jnp.int32),
            pltpu.SMEM(counts_shape, jnp.int32),
            pltpu.SMEM(inner_shape, jnp.int32),
            pltpu.SMEM((n_row * per_rank, RB_DEV), jnp.int32),
            pltpu.SMEM((n_row * per_rank, columns), jnp.int32),
            pltpu.VMEM((CHUNKS // per_rank, size, block, block), a.dtype),
            pltpu.VMEM((block, columns * block), b.dtype),
            pltpu.VMEM((RB_DEV * block, columns * block), jnp.float32),
            pltpu.VMEM((n_col, 8, columns * block), jnp.float32),
            pltpu.VMEM((columns, RB_DEV, block, block), jnp.bfloat16),
            dma((3, n_row, CHUNKS)), dma((n_row, CHUNKS)),
            dma((2, n_col)), dma((2, n_col)), dma((2, n_row)), dma((2, n_row)), dma((n_col,)), dma((n_col,)),
            dma((8,)), dma((columns, RB_DEV)),
        ],
        compiler_params=pltpu.CompilerParams(
            collective_id=0, has_side_effects=True, vmem_limit_bytes=63 << 20),
        name="gather_multiply_normalize",
    )(a, b, matrix_rows, matrix_counts, slab_inner, slab_counts)


LIST = 9
OVER = 3
FIRST = LIST - OVER
SLOTS = LIST + OVER
GRAIN = 16
PARTS = 4
BY_Y = 3
LEVELS = 65535.0


def pair_kernel(n_z, shape, a_ref, b_ref, rows_ref, counts_ref, inner_ref, used_ref, counts_in, used_in, out_ref,
                cand, over, over_in, y_out, a_all, a_par, b_all, right, stage, lhs, acc, result,
                sums_acc, sums_out, sums_all, c_out, c_in, top_out, top_in,
                rows_all, counts_all, counts_par, counts_near, inner_all, used_all,
                rows_s, counts_s, counts_par_s, inner_s, used_s, slot_s, source_s,
                local, ready, near_send, near_recv, z_send, z_recv, y_send, y_recv, o_send, o_recv,
                over_y, x_send, x_recv, p_send, p_recv, b_send, b_recv, m_send, m_recv, c_send, c_recv, s_send, s_recv):
    columns, slots, capacity, block = shape
    half = block // 2
    size = half // GRAIN // PARTS
    grains = half // GRAIN
    wide = columns * block
    r = lax.axis_index("row")
    c = lax.axis_index("col")
    z = lax.div(r, 2)
    y = lax.rem(r, 2)
    x = lax.div(c, 2)
    t = lax.rem(c, 2)
    has_up = z < n_z - 1
    has_down = z > 0
    middle = has_up & has_down
    end = jnp.logical_not(middle)
    c_x = 2 * (1 - x) + t
    c_t = 2 * x + 1 - t
    to_up = {"row": r + 2, "col": c}
    to_down = {"row": r - 2, "col": c}
    to_y = {"row": 2 * z + 1 - y, "col": c}
    to_x = {"row": r, "col": c_x}
    to_core = {"row": r, "col": c_t}

    def span(m):
        return pl.ds(m * size, size)

    def parts(work, first=0, end_at=PARTS):
        def one(m, carry):
            work(m)
            return carry

        lax.fori_loop(first, end_at, one, 0)

    def quarter(work, n):
        parts(work, n * PARTS // 4, (n + 1) * PARTS // 4)

    def remote(src, dst, send_sem, recv_sem, target):
        return pltpu.make_async_remote_copy(
            src_ref=src, dst_ref=dst, send_sem=send_sem, recv_sem=recv_sem,
            device_id=target, device_id_type=MESH)

    near = [(2 * z + (y if d < 4 else 1 - y), lax.rem(c + d, 4)) for d in range(1, 8)]

    barrier = pltpu.get_barrier_semaphore()
    for d in range(1, 2 * n_z):
        pl.semaphore_signal(
            barrier, inc=1, device_id={"row": lax.rem(r + d, 2 * n_z), "col": c}, device_id_type=MESH)
    for d, (row, col) in enumerate(near, 1):
        if d != 4:
            pl.semaphore_signal(barrier, inc=1, device_id={"row": row, "col": col}, device_id_type=MESH)
    pl.semaphore_wait(barrier, 2 * n_z - 1 + 6)

    def give_cand(n):
        return remote(a_ref.at[1 - t, pl.ds(2 * n, 2)], cand.at[pl.ds(t * capacity + 2 * n, 2)],
                      near_send.at[0, n], near_recv.at[0, n], to_core)

    def take_cand(n):
        return remote(a_ref.at[1 - t, pl.ds(2 * n, 2)], cand.at[pl.ds((1 - t) * capacity + 2 * n, 2)],
                      near_send.at[0, n], near_recv.at[0, n], to_core)

    def give_near():
        return remote(counts_ref, counts_near, near_send.at[1, 0], near_recv.at[1, 0], to_core)

    def metas(d):
        target = {"row": lax.rem(r + d, 2 * n_z), "col": c}
        return [remote(rows_ref, rows_all.at[r], m_send.at[0, d], m_recv.at[0, d], target),
                remote(counts_ref, counts_all.at[r], m_send.at[1, d], m_recv.at[1, d], target)]

    def inner_to(d):
        side = 0 if d < 4 else 1
        row, col = near[d - 1]
        return remote(inner_ref, inner_all.at[side, c], m_send.at[2, d], m_recv.at[2, d], {"row": row, "col": col})

    def used_to():
        return remote(used_ref, used_all, m_send.at[3, 0], m_recv.at[3, 0], to_y)

    def par_counts():
        return remote(counts_all, counts_par, m_send.at[3, 1], m_recv.at[3, 1], to_core)

    def slab(side, col, j):
        return b_all.at[side, col, j]

    def slab_copy(way, src, side, col, j, target, first=0, size=slots):
        piece = pl.ds(first, size)
        return remote(src.at[piece], b_all.at[side, col, j, piece], b_send.at[way, side, col, j],
                      b_recv.at[side, col, j], target)

    def slab_own(way, j, first=0, size=slots):
        side, target = {0: (0, to_core), 1: (0, to_x), 2: (1, to_y)}[way]
        return slab_copy(way, b_ref.at[j], side, c, j, target, first, size)

    def slab_core(side, col, j):
        return slab_copy(0, slab(side, col, j), side, col, j, to_core)

    def slab_diag(j, over_x):
        first, size = 0, slots
        if j == 0:
            first, size = (BY_Y, slots - BY_Y) if over_x else (0, BY_Y)
        if over_x:
            return slab_copy(3, slab(1, c, j), 1, c, j, to_x, first, size)
        return slab_copy(3, slab(0, c_x, j), 1, c_x, j, to_y, first, size)

    def slab_wait(side, col, j):
        slab_copy(0, slab(side, col, j), side, col, j, to_core).wait_recv()

    def y_copy(m, tail):
        at, many = ((0, FIRST), (FIRST, OVER))[tail]
        return remote(y_out.at[span(m), pl.ds(at, many)], a_all.at[z, span(m), y, pl.ds(at, many)],
                      y_send.at[m, tail], y_recv.at[m, tail], to_y)

    def y_wait(m, tail):
        at, many = ((0, FIRST), (FIRST, OVER))[tail]
        remote(y_out.at[span(m), pl.ds(at, many)], a_all.at[z, span(m), 1 - y, pl.ds(at, many)],
               y_send.at[m, tail], y_recv.at[m, tail], to_y).wait_recv()

    def y_over(to):
        return remote(y_out.at[:, pl.ds(LIST, OVER)], a_all.at[z, :, to, pl.ds(LIST, OVER)],
                      over_y.at[0], over_y.at[1], to_y)

    def over_copy():
        return remote(over, over_in, o_send, o_recv, to_x)

    def z_first(way, m, side, tail):
        at, many = ((0, FIRST), (FIRST, OVER))[tail]
        piece = a_all.at[z, span(m), side, pl.ds(at, many)]
        return remote(piece, piece, z_send.at[way, z, m, 2 * side + tail], z_recv.at[z, m, tail],
                      (to_up, to_down)[way])

    def z_piece(rank, m, tail):
        return a_all.at[rank, span(m), :, (pl.ds(0, FIRST), pl.ds(FIRST, OVER))[tail]]

    def z_next(way, rank, m, tail):
        piece = z_piece(rank, m, tail)
        return remote(piece, piece, z_send.at[way, rank, m, tail], z_recv.at[rank, m, tail], (to_up, to_down)[way])

    def z_wait(rank, m, tail):
        piece = z_piece(rank, m, tail)
        remote(piece, piece, z_send.at[0, rank, m, tail], z_recv.at[rank, m, tail], to_y).wait_recv()

    def moved(step, act):
        @pl.when(step == 0)
        def _():
            act(0, 1)

        @pl.when(step + 1 < PARTS)
        def _():
            act(step + 1, 1)

        act(step, 0)

    def x_copy(rank, m):
        return remote(a_all.at[rank, span(m), :, pl.ds(FIRST, OVER)], a_all.at[rank, span(m), :, pl.ds(LIST, OVER)],
                      x_send.at[rank, m], x_recv.at[rank, m], to_x)

    def p_copy(rank, m, over_part):
        piece = (rank, span(m), slice(None), (pl.ds(0, FIRST), pl.ds(FIRST, 2 * OVER))[over_part])
        return remote(a_all.at[piece], a_par.at[piece], p_send.at[rank, m, over_part], p_recv.at[rank, m, over_part],
                      to_core)

    def c_copy(m):
        return remote(c_out.at[span(m)], c_in.at[span(m)], c_send.at[m, 0], c_recv.at[m, 0], to_y)

    def top_copy(m):
        return remote(top_out.at[m], top_in.at[m], c_send.at[m, 1], c_recv.at[m, 1], to_y)

    def sums_copy(d):
        row, col = near[d - 1]
        side = 0 if d < 4 else 1
        return remote(sums_out.at[side], sums_all.at[side, c], s_send.at[d], s_recv.at[d], {"row": row, "col": col})

    def both(m, side, tail, act):
        @pl.when(has_up)
        def _():
            act(z_first(0, m, side, tail))

        @pl.when(has_down)
        def _():
            act(z_first(1, m, side, tail))

    def start(copy):
        copy.start()

    def wait_send(copy):
        copy.wait_send()

    def rank_of(n):
        low = z < n_z // 2
        at = jnp.where(low, z, n_z - 1 - z)
        rank = n - 1 + jnp.where(n - 1 >= at, 1, 0)
        rank = jnp.where(low, rank, n_z - 1 - rank)
        return jnp.where(n == 0, z, rank)

    mine = [pltpu.make_async_copy(a_ref.at[t], cand.at[pl.ds(t * capacity, capacity)], local.at[0])]
    give_near().start()
    for n in range(capacity // 2):
        give_cand(n).start()
    mine[0].start()
    slab_own(2, 1, 0, 2).start()
    slab_own(1, 0, 0, 1).start()
    mine += [
        pltpu.make_async_copy(rows_ref, rows_all.at[r], local.at[1]),
        pltpu.make_async_copy(counts_ref, counts_all.at[r], local.at[2]),
        pltpu.make_async_copy(inner_ref, inner_all.at[0, c], local.at[3]),
        pltpu.make_async_copy(b_ref, b_all.at[0, c], local.at[4]),
    ]
    acc[...] = jnp.zeros_like(acc)
    sums_acc[...] = jnp.zeros_like(sums_acc)

    give_near().wait_recv()
    at_rank = lax.broadcasted_iota(jnp.int32, (1, 2), 1)
    near_count = jnp.max(jnp.where(at_rank == t, counts_near[...], 0))
    mine[0].wait()
    for n in range(capacity // 2):
        take_cand(n).wait_recv()

    own_count = counts_in[0, t]
    first_count = jnp.where(t == 0, own_count, near_count)
    total_count = own_count + near_count

    def place(p):
        return jnp.where(p < first_count, p, capacity + jnp.minimum(jnp.maximum(p - first_count, 0), capacity - 1))

    for p in range(OVER):
        over[p] = cand[place(LIST + p)]
    over_copy().start()

    def rows_at(side, m):
        return pl.ds(pl.multiple_of(side * half + m * GRAIN, GRAIN), GRAIN)

    def pack(p, carry):
        at = place(p)
        for g in range(grains):
            a_all[z, g, y, p] = cand[at, rows_at(y, g), :]
            y_out[g, p] = cand[at, rows_at(1 - y, g), :]
        return carry

    def pack_tail(p, carry):
        at = place(FIRST + p)
        keep = total_count > FIRST
        for g in range(grains):
            for side, there in ((y, True), (1 - y, False)):
                value = jnp.where(keep, cand[at, rows_at(side, g), :], over_in[p, rows_at(side, g), :])
                if there:
                    a_all[z, g, y, FIRST + p] = value
                else:
                    y_out[g, FIRST + p] = value
        return carry

    def pack_over(p, carry):
        for g in range(grains):
            a_all[z, g, y, LIST + p] = over[p, rows_at(y, g), :]
            y_out[g, LIST + p] = over[p, rows_at(1 - y, g), :]
        return carry

    lax.fori_loop(0, FIRST, pack, 0)
    def own_main(m):
        y_copy(m, 0).start()
        both(m, y, 0, start)

    def beside_main(m):
        y_wait(m, 0)
        both(m, 1 - y, 0, start)
        p_copy(z, m, 0).start()

    def own_tail(m):
        y_copy(m, 1).start()
        both(m, y, 1, start)

    def beside_tail(m):
        y_wait(m, 1)
        both(m, 1 - y, 1, start)

    parts(own_main)
    slab_own(1, 0, 1, slots - 1).start()
    for j in range(columns):
        slab_own(0, j).start()
    for d in range(1, 2 * n_z):
        for copy in metas(d):
            copy.start()
    for d in range(1, 8):
        inner_to(d).start()
    used_to().start()
    for copy in mine[1:]:
        copy.start()
    lax.fori_loop(0, OVER, pack_over, 0)
    parts(beside_main)
    over_copy().wait_recv()
    lax.fori_loop(0, OVER, pack_tail, 0)
    parts(own_tail)
    slab_own(1, 1).start()
    slab_own(2, 1, 2, slots - 2).start()
    parts(beside_tail)
    slab_own(2, 0).start()

    def relay(n, step):
        rank = rank_of(n)

        def act(m, tail):
            z_wait(rank, m, tail)

            @pl.when((rank < z) & has_up)
            def _():
                z_next(0, rank, m, tail).start()

            @pl.when((rank > z) & has_down)
            def _():
                z_next(1, rank, m, tail).start()

        moved(step, act)
        p_copy(rank, step, 0).start()

    def near_x(m):
        x_copy(rank_of(1), m).start()

        @pl.when(middle)
        def _():
            x_copy(rank_of(2), m).start()

    def near_relay(m):
        relay(1, m)

        @pl.when(middle)
        def _():
            relay(2, m)

    def far_relay(m):
        relay(jnp.where(middle, 3, 2), m)

    def far_x(m):
        x_copy(rank_of(jnp.where(middle, 3, 2)), m).start()

    def table(k, carry):
        rank = lax.div(k, 2)
        kk = lax.rem(k, 2)
        for side in range(2):
            for j in range(columns):
                limit = used_in[0, j] if side == 0 else used_s[0, j]
                q = jnp.int32(-1)
                for n in range(4 * slots):
                    found = (inner_s[side, n // slots, j, n % slots] == k) & (n < limit)
                    q = jnp.where(found, n, q)
                source_s[k, side * columns + j] = q
        base = jnp.where(t == 1, counts_par_s[rank, 0, kk], 0)
        live = counts_s[rank, 0, kk]
        for i in range(RB_DEV):
            p = jnp.int32(-1)
            for n in range(capacity):
                found = (rows_s[rank, kk, n] == i) & (n < live)
                p = jnp.where(found, n + base, p)
            slot_s[k, i] = p
        return carry

    def complete():
        for copy in mine[1:4]:
            copy.wait()
        for d in range(1, 2 * n_z):
            for copy in metas(d):
                copy.wait()
        par_counts().start()
        for d in range(1, 8):
            inner_to(d).wait()
        used_to().wait()
        par_counts().wait()
        for n, (src, dst) in enumerate((
                (rows_all, rows_s), (counts_all, counts_s), (counts_par, counts_par_s), (inner_all, inner_s),
                (used_all, used_s))):
            pltpu.make_async_copy(src, dst, ready.at[n]).start()
        for n, (src, dst) in enumerate((
                (rows_all, rows_s), (counts_all, counts_s), (counts_par, counts_par_s), (inner_all, inner_s),
                (used_all, used_s))):
            pltpu.make_async_copy(src, dst, ready.at[n]).wait()
        lax.fori_loop(0, 4 * n_z, table, 0)

    def give_core(rank, m):
        x_copy(rank, m).wait_recv()
        p_copy(rank, m, 1).start()

    def near_core(m):
        give_core(rank_of(1), m)

        @pl.when(middle)
        def _():
            give_core(rank_of(2), m)

    def slab_next(side, col, j):
        slab_wait(side, col, j)
        slab_core(side, col, j).start()

    def forward(m):
        near_x(m)
        far_x(m)

    slab_next(0, c_x, 0)
    slab_diag(0, False).start()
    parts(near_relay)
    slab_next(1, c, 1)
    slab_diag(1, True).start()
    slab_next(0, c_x, 1)
    complete()
    quarter(far_relay, 0)
    slab_next(1, c, 0)
    slab_diag(0, True).start()
    y_over(y).start()
    quarter(far_relay, 1)
    slab_next(1, c_x, 1)
    quarter(forward, 0)
    slab_next(1, c_x, 0)
    quarter(forward, 1)
    quarter(far_relay, 2)

    mine[4].wait()
    for j in range(columns):
        for side in range(2):
            for col in (c_t, 2 * (1 - x) + 1 - t):
                slab_wait(side, col, j)

    def gather_right(n, carry):
        rank = lax.div(n, 4)
        side = lax.rem(lax.div(n, 2), 2)
        u = lax.rem(n, 2)
        k = 2 * (2 * rank + side) + jnp.where(u == 0, t, 1 - t)
        rows = pl.ds(pl.multiple_of(lax.rem(n, 4) * block, block), block)
        for s in range(2):
            for j in range(columns):
                q = source_s[k, s * columns + j]
                at = jnp.maximum(q, 0)
                value = b_all[s, lax.div(at, slots), j, lax.rem(at, slots)]
                to = (s * columns + j) * block
                right[rank, rows, to:to + block] = jnp.where(q >= 0, value, jnp.zeros_like(value))
        return carry

    lax.fori_loop(0, 4 * n_z, gather_right, 0)

    tall = RB_DEV * GRAIN

    def multiply(rank, m):
        p_copy(rank, m, 0).wait_recv()
        p_copy(rank, m, 1).wait_recv()
        for g in range(size):
            for u, source in enumerate((a_all, a_par)):
                for side in range(2):
                    stage[u, side, g] = source[rank, m * size + g, side]
        for side in range(2):
            for u in range(2):
                k = 2 * (2 * rank + side) + (t if u == 0 else 1 - t)
                at = (2 * side + u) * block
                for i in range(RB_DEV):
                    p = slot_s[k, i]
                    for g in range(size):
                        value = stage[u, side, g, jnp.maximum(p, 0)]
                        to = g * tall + i * GRAIN
                        lhs[to:to + GRAIN, at:at + block] = jnp.where(p >= 0, value, jnp.zeros_like(value))
        for n in range(2):
            cols = slice(n * wide, (n + 1) * wide)
            product = jnp.dot(lhs[...], right[rank, :, cols], preferred_element_type=jnp.float32)
            acc[span(m), :, cols] += product.reshape(size, tall, wide)

    def cores(m):
        near_core(m)
        give_core(rank_of(jnp.where(middle, 3, 2)), m)

    def last_relay(m):
        rank = rank_of(3)

        def act(n, tail):
            z_wait(rank, n, tail)
            if tail:
                x_copy(rank, n).start()

        moved(m, act)
        p_copy(rank, m, 0).start()
        give_core(rank, m)

    def finish_part(m):
        for n in range(2):
            value = acc[span(m), :, n * wide:(n + 1) * wide]
            squared = value * value
            sums_acc[n] += jnp.sum(squared.reshape(-1, 8, wide), axis=0)

        @pl.when(m + 1 == PARTS)
        def _():
            for n in range(2):
                sums_out[n] = jnp.sum(sums_acc[n], axis=0, keepdims=True)
            for d in range(1, 8):
                sums_copy(d).start()

        value = acc[span(m), :, wide:].reshape(-1, wide)
        top = jnp.maximum(jnp.max(value, axis=0, keepdims=True), 1e-30)
        scaled = value * (LEVELS / top) + 0.5
        coded = jnp.minimum(scaled, LEVELS).astype(jnp.int32)
        word = lax.shift_left(coded[:, :block], jnp.int32(16)) | coded[:, block:]
        c_out[span(m)] = word.reshape(size, tall, block)
        top_out[m] = jnp.broadcast_to(top, (8, wide))
        c_copy(m).start()
        top_copy(m).start()

    quarter(forward, 2)
    quarter(far_relay, 3)
    quarter(forward, 3)
    y_over(1 - y).wait_recv()
    parts(lambda m: p_copy(z, m, 1).start())
    cores(0)

    def drain_start():
        give_near().wait_send()
        for n in range(capacity // 2):
            give_cand(n).wait_send()
        over_copy().wait_send()
        y_over(y).wait_send()
        for way in range(3):
            for j in range(columns):
                slab_own(way, j).wait_send()
        for j in range(columns):
            slab_diag(j, True).wait_send()
            if j == 0:
                slab_diag(j, False).wait_send()
            for side, col in ((0, c_x), (1, c), (1, c_x)):
                slab_core(side, col, j).wait_send()

    def drain_rank(rank, m):
        p_copy(rank, m, 0).wait_send()
        p_copy(rank, m, 1).wait_send()

        @pl.when(rank != z)
        def _():
            x_copy(rank, m).wait_send()

    def drain_part(m):
        for tail in range(2):
            y_copy(m, tail).wait_send()
            both(m, 0, tail, wait_send)
            both(m, 1, tail, wait_send)

        def one(n, carry):
            drain_rank(rank_of(n), m)
            return carry

        lax.fori_loop(0, 3, one, 0)

    def drain_last(m):
        drain_rank(rank_of(3), m)
        c_copy(m).wait_send()
        top_copy(m).wait_send()

        @pl.when(middle)
        def _():
            def one(rank, carry):
                for tail in range(2):
                    @pl.when((rank < z) & has_up)
                    def _():
                        z_next(0, rank, m, tail).wait_send()

                    @pl.when((rank > z) & has_down)
                    def _():
                        z_next(1, rank, m, tail).wait_send()
                return carry

            lax.fori_loop(0, n_z, one, 0)

    def one_part(m):
        @pl.when(m + 1 < PARTS)
        def _():
            cores(m + 1)

        def one_rank(n, carry):
            @pl.when((n == 3) & end)
            def _():
                last_relay(m)

            multiply(rank_of(jnp.where(n == 3, 3, lax.rem(n + 1, 3))), m)
            return carry

        lax.fori_loop(0, 4, one_rank, 0)
        finish_part(m)

        @pl.when(m + 1 < PARTS)
        def _():
            @pl.when(m == 0)
            def _():
                drain_start()

            drain_part(m)

    parts(one_part)
    drain_part(PARTS - 1)

    for d in range(1, 8):
        sums_copy(d).wait()
    sums = sums_out[0]
    for d in range(1, 8):
        sums = sums + sums_all[0 if d < 4 else 1, near[d - 1][1]]
    factor = float(RB_DEV * 4 * block) / sums

    def store(value, g, side):
        value = value.astype(jnp.bfloat16)
        for i in range(RB_DEV):
            for j in range(columns):
                result[j, i, rows_at(side, g), :] = value[i * GRAIN:(i + 1) * GRAIN, j * block:(j + 1) * block]

    def scale_own(g, carry):
        value = acc[g, :, :wide]
        store(value * value * factor, g, y)
        return carry

    def out_half(side):
        rows = pl.ds(pl.multiple_of(side * half, half), half)
        return pltpu.make_async_copy(
            result.at[:, :, rows], out_ref.at[:, :, rows], local.at[6 + side])

    lax.fori_loop(0, grains, scale_own, 0)
    out_half(y).start()
    def scale_other(m):
        c_copy(m).wait_recv()
        top_copy(m).wait_recv()
        step = top_in[m][0:1, :] * (1.0 / LEVELS)

        def one(g, carry):
            word = c_in[g]
            upper = lax.shift_right_logical(word, jnp.int32(16)).astype(jnp.float32)
            lower = (word & jnp.int32(65535)).astype(jnp.float32)
            value = jnp.concatenate([upper, lower], axis=1) * step
            store(value * value * factor, g, 1 - y)
            return carry

        lax.fori_loop(m * size, (m + 1) * size, one, 0)

    parts(scale_other)
    out_half(1 - y).start()
    parts(drain_last)
    out_half(0).wait()
    out_half(1).wait()


def paired(n_z, matrix_blocks, matrix_rows, matrix_counts, slab_blocks, slab_inner, slab_counts):
    capacity, block = matrix_blocks.shape[1], matrix_blocks.shape[2]
    columns, slots = slab_blocks.shape[0], slab_blocks.shape[1]
    grains = block // 2 // GRAIN
    counts = matrix_counts.reshape(1, 2)
    used = slab_counts.reshape(1, columns)
    hbm = pl.BlockSpec(memory_space=pltpu.HBM)
    smem = pl.BlockSpec(memory_space=pltpu.SMEM)
    dma = pltpu.SemaphoreType.DMA
    half_word, full = jnp.bfloat16, jnp.float32
    rows_shape, counts_shape, inner_shape = (2 * n_z, 2, capacity), (2 * n_z, 1, 2), (2, 4) + slab_inner.shape
    lists = (n_z, grains, 2, SLOTS, GRAIN, block)
    parts, most = PARTS, grains // PARTS
    vmem = [
        ((2 * capacity, block, block), half_word),
        ((OVER, block, block), half_word),
        ((OVER, block, block), half_word),
        ((grains, SLOTS, GRAIN, block), half_word),
        (lists, half_word),
        (lists, half_word),
        ((2, 4) + slab_blocks.shape, half_word),
        ((n_z, 4 * block, 2 * columns * block), half_word),
        ((2, 2, most, SLOTS, GRAIN, block), half_word),
        ((most * RB_DEV * GRAIN, 4 * block), half_word),
        ((grains, RB_DEV * GRAIN, 2 * columns * block), full),
        ((columns, RB_DEV, block, block), half_word),
        ((2, 8, columns * block), full),
        ((2, 1, columns * block), full),
        ((2, 4, 1, columns * block), full),
        ((grains, RB_DEV * GRAIN, block), jnp.int32),
        ((grains, RB_DEV * GRAIN, block), jnp.int32),
        ((parts, 8, columns * block), full),
        ((parts, 8, columns * block), full),
        (rows_shape, jnp.int32), (counts_shape, jnp.int32), (counts_shape, jnp.int32), ((1, 2), jnp.int32),
        (inner_shape, jnp.int32), ((1, columns), jnp.int32),
    ]
    words = [rows_shape, counts_shape, counts_shape, inner_shape, (1, columns),
             (4 * n_z, RB_DEV), (4 * n_z, 2 * columns)]
    sems = [(8,), (5,), (2, capacity // 2), (2, capacity // 2), (2, n_z, parts, 4), (n_z, parts, 2), (parts, 2), (parts, 2), None, None, (2,),
            (n_z, parts), (n_z, parts), (n_z, parts, 2), (n_z, parts, 2), (4, 2, 4, columns), (2, 4, columns),
            (4, 2 * n_z), (4, 2 * n_z), (parts, 2), (parts, 2), (8,), (8,)]
    return pl.pallas_call(
        functools.partial(pair_kernel, n_z, (columns, slots, capacity, block)),
        out_shape=jax.ShapeDtypeStruct((columns, RB_DEV, block, block), jnp.bfloat16),
        in_specs=[hbm] * 6 + [smem] * 2,
        out_specs=pl.BlockSpec(memory_space=pl.ANY),
        scratch_shapes=[pltpu.VMEM(s, d) for s, d in vmem] + [pltpu.SMEM(s, jnp.int32) for s in words]
        + [dma if s is None else dma(s) for s in sems],
        compiler_params=pltpu.CompilerParams(
            collective_id=1, has_side_effects=True, vmem_limit_bytes=44 << 20),
        name="packed_pair_multiply",
    )(*[pltpu.with_memory_space_constraint(v, pltpu.HBM) for v in (
        matrix_blocks, slab_blocks, matrix_rows, counts, slab_inner, used)], counts, used)


def choose(n_row, n_col, *args):
    if n_row == 8 and n_col == 4 and args[0].shape[0] == 2 and args[0].shape[1] == SLOTS // 2:
        return paired(n_row // 2, *args)
    return on_device(n_row, n_col, *args)


def solution(mesh):
    return jax.shard_map(
        functools.partial(choose, mesh.shape["row"], mesh.shape["col"]),
        mesh=mesh,
        in_specs=(
            P("row", "col", None, None),
            P("row", "col"),
            P("row", "col"),
            P("row", "col", None, None),
            P("row", "col"),
            P("row"),
        ),
        out_specs=P("row", "col", None, None),
        check_vma=False,
    )
```

```python
import functools

import jax
import jax.numpy as jnp
from jax import lax
from jax.experimental import pallas as pl
from jax.experimental.pallas import tpu as pltpu
from jax.sharding import PartitionSpec as P

RB_DEV = 8
MESH = pl.DeviceIdType.MESH
CHUNKS = 6
PLAIN = CHUNKS - 1
UP, DOWN, SIDE = 0, 1, 2


def step_kernel(n_row, n_col, shape, a_ref, b_ref, rows_ref, counts_ref, inner_ref, slab_counts, out_ref,
                a_all, b_all, rows_all, counts_all, inner_all, rows_s, counts_s, inner_s,
                slot_s, source_s, stage, right, acc, sums_all, result,
                send, recv, b_send, b_recv, m_send, m_recv, s_send, s_recv, local, done):
    columns, slots, per_rank, capacity, block = shape
    each = CHUNKS // per_rank
    size = capacity // each
    n_z = n_row // 2
    r = lax.axis_index("row")
    c = lax.axis_index("col")
    z = lax.div(r, 2)
    y = lax.rem(r, 2)
    other = 1 - y
    beside = 2 * z + other
    has_up = z < n_z - 1
    has_down = z > 0

    barrier = pltpu.get_barrier_semaphore()
    for d in range(1, n_row):
        pl.semaphore_signal(barrier, inc=1, device_id={"row": lax.rem(r + d, n_row)}, device_id_type=MESH)
    for d in range(1, n_col):
        pl.semaphore_signal(barrier, inc=1, device_id={"col": lax.rem(c + d, n_col)}, device_id_type=MESH)
    pl.semaphore_wait(barrier, n_row + n_col - 2)

    def chunk(way, rank, ch, own=False):
        target = {UP: r + 2, DOWN: r - 2, SIDE: beside}[way]
        src = a_ref.at[ch] if own else a_all.at[rank, ch]
        return pltpu.make_async_remote_copy(
            src_ref=src, dst_ref=a_all.at[rank, ch], send_sem=send.at[way, rank, ch],
            recv_sem=recv.at[rank, ch], device_id={"row": target}, device_id_type=MESH)

    def arrived(rank, ch):
        pltpu.make_async_remote_copy(
            src_ref=a_all.at[rank, ch], dst_ref=a_all.at[rank, ch], send_sem=send.at[SIDE, rank, ch],
            recv_sem=recv.at[rank, ch], device_id={"row": beside}, device_id_type=MESH).wait_recv()

    def small(d):
        target = {"row": lax.rem(r + d, n_row)}
        return [
            pltpu.make_async_remote_copy(
                src_ref=src, dst_ref=dst.at[r], send_sem=m_send.at[n, d], recv_sem=m_recv.at[n, d],
                device_id=target, device_id_type=MESH)
            for n, (src, dst) in enumerate(((rows_ref, rows_all), (counts_ref, counts_all)))
        ]

    def slab(d):
        target = {"col": lax.rem(c + d, n_col)}
        return [
            pltpu.make_async_remote_copy(
                src_ref=inner_ref, dst_ref=inner_all.at[c], send_sem=b_send.at[1, d], recv_sem=b_recv.at[1, d],
                device_id=target, device_id_type=MESH),
            pltpu.make_async_remote_copy(
                src_ref=b_ref, dst_ref=b_all.at[c], send_sem=b_send.at[0, d], recv_sem=b_recv.at[0, d],
                device_id=target, device_id_type=MESH),
        ]

    def share(d):
        return pltpu.make_async_remote_copy(
            src_ref=sums_all.at[c], dst_ref=sums_all.at[c], send_sem=s_send.at[d], recv_sem=s_recv.at[d],
            device_id={"col": lax.rem(c + d, n_col)}, device_id_type=MESH)

    for ch in [PLAIN] + list(range(PLAIN)):
        chunk(SIDE, r, ch, True).start()
    for ch in range(CHUNKS):
        @pl.when(has_up)
        def _():
            chunk(UP, r, ch, True).start()

        @pl.when(has_down)
        def _():
            chunk(DOWN, r, ch, True).start()

    for d in range(1, n_row):
        for copy in small(d):
            copy.start()
    for d in range(1, n_col):
        for copy in slab(d):
            copy.start()
    mine = (
        pltpu.make_async_copy(a_ref, a_all.at[r], local.at[0]),
        pltpu.make_async_copy(b_ref, b_all.at[c], local.at[1]),
        pltpu.make_async_copy(rows_ref, rows_all.at[r], local.at[2]),
        pltpu.make_async_copy(counts_ref, counts_all.at[r], local.at[3]),
        pltpu.make_async_copy(inner_ref, inner_all.at[c], local.at[4]),
    )
    for copy in mine:
        copy.start()
    acc[...] = jnp.zeros_like(acc)

    arrived(beside, PLAIN)

    @pl.when(has_up)
    def _():
        chunk(UP, beside, PLAIN).start()

    @pl.when(has_down)
    def _():
        chunk(DOWN, beside, PLAIN).start()

    steps = [(0, ch, True) for ch in range(PLAIN)] + [(0, PLAIN, False), (1, PLAIN, False)]

    def sides(d, work):
        def one(side, carry):
            at = z + d * (2 * side - 1)

            @pl.when((at >= 0) & (at < n_z))
            def _():
                work(at)
            return carry

        lax.fori_loop(0, 2, one, 0)

    def relay(d, extra):
        for n, (flip, ch, cross) in enumerate(steps):
            column = other if flip else y

            @pl.when(z >= d)
            def _():
                rank = 2 * (z - d) + column
                arrived(rank, ch)

                @pl.when(has_up)
                def _():
                    chunk(UP, rank, ch).start()

                if cross:
                    chunk(SIDE, rank, ch).start()

            @pl.when(z + d < n_z)
            def _():
                rank = 2 * (z + d) + column
                arrived(rank, ch)

                @pl.when(has_down)
                def _():
                    chunk(DOWN, rank, ch).start()

                if cross:
                    chunk(SIDE, rank, ch).start()

            for work in extra.get(n, ()):
                work()

    def half(rank, kk):
        k = rank * per_rank + kk
        copy = pltpu.make_async_copy(a_all.at[rank, pl.ds(kk * each, each)], stage, local.at[0])
        copy.start()
        for j in range(columns):
            q = source_s[k, j]
            at = jnp.maximum(q, 0)
            value = b_all[lax.div(at, slots), j * slots + lax.rem(at, slots)]
            right[:, j * block:(j + 1) * block] = jnp.where(q >= 0, value, jnp.zeros_like(value))
        copy.wait()

        def block_row(i, carry):
            t = slot_s[k, i]
            at = jnp.maximum(t, 0)
            value = stage[lax.div(at, size), lax.rem(at, size)]
            left = jnp.where(t >= 0, value, jnp.zeros_like(value))
            rows = pl.ds(pl.multiple_of(i * block, block), block)
            acc[rows, :] += jnp.dot(left, right[...], preferred_element_type=jnp.float32)
            return carry

        lax.fori_loop(0, RB_DEV, block_row, 0, unroll=2)

    def whole(rank):
        def one(kk, carry):
            half(rank, kk)
            return carry

        lax.fori_loop(0, per_rank, one, 0)

    def await_side(rank, first, end):
        for ch in range(first, end):
            arrived(rank, ch)

    def own_whole(at):
        whole(2 * at + y)

    def side_whole(at):
        await_side(2 * at + other, 0, PLAIN)
        whole(2 * at + other)

    def own_half(kk):
        def work(at):
            half(2 * at + y, kk)
        return work

    def side_half(kk):
        def work(at):
            await_side(2 * at + other, kk * each, min(kk * each + each, PLAIN))
            half(2 * at + other, kk)
        return work

    relay(1, {})

    def complete():
        for copy in mine:
            copy.wait()
        for d in range(1, n_row):
            for copy in small(d):
                copy.wait()
        for d in range(1, n_col):
            for copy in slab(d):
                copy.wait()
        for n, (src, dst) in enumerate(((rows_all, rows_s), (counts_all, counts_s), (inner_all, inner_s))):
            copy = pltpu.make_async_copy(src, dst, local.at[5 + n])
            copy.start()
            copy.wait()
        lax.fori_loop(0, n_row, table, 0)

    def table(rank, carry):
        for kk in range(per_rank):
            k = rank * per_rank + kk
            for j in range(columns):
                q = jnp.int32(-1)
                for n in range(n_col * slots):
                    found = (inner_s[n // slots, j, n % slots] == k) & (n < slab_counts[j])
                    q = jnp.where(found, n, q)
                source_s[k, j] = q
            for i in range(RB_DEV):
                t = jnp.int32(-1)
                for n in range(capacity):
                    found = (rows_s[rank, kk, n] == i) & (n < counts_s[rank, 0, kk])
                    t = jnp.where(found, n, t)
                slot_s[k, i] = t
        return carry

    def side_here():
        await_side(beside, 0, PLAIN)
        whole(beside)

    relay(2, {
        0: (complete,),
        1: (lambda: whole(r),),
        2: (side_here,),
        3: (lambda: sides(1, own_whole),),
    })
    sides(1, side_whole)
    sides(2, own_whole)

    def later(d, carry):
        relay(d, {})
        sides(d - 1, side_whole)
        sides(d, own_whole)
        return carry

    lax.fori_loop(3, n_z - 1, later, 0)
    far = n_z - 1

    def side_halves(at):
        side_half(0)(at)
        side_half(1)(at)

    relay(far, {
        each - 1: (lambda: sides(far, own_half(0)), lambda: sides(far - 1, side_halves)),
        CHUNKS - 1: (lambda: sides(far, own_half(1)), lambda: sides(far, side_half(0))),
        CHUNKS: (lambda: sides(far, side_half(1)),),
    })

    def square(i, total):
        rows = pl.ds(pl.multiple_of(i * block, block), block)
        value = acc[rows, :]
        value = value * value
        return total + jnp.sum(value.reshape(block // 8, 8, columns * block), axis=0)

    total = lax.fori_loop(0, RB_DEV, square, jnp.zeros((8, columns * block), jnp.float32))
    sums_all[c] = total
    for d in range(1, n_col):
        share(d).start()

    for ch in range(CHUNKS):
        chunk(SIDE, r, ch, True).wait_send()

        @pl.when(has_up)
        def _():
            chunk(UP, r, ch, True).wait_send()

        @pl.when(has_down)
        def _():
            chunk(DOWN, r, ch, True).wait_send()

    @pl.when(has_up)
    def _():
        chunk(UP, beside, PLAIN).wait_send()

    @pl.when(has_down)
    def _():
        chunk(DOWN, beside, PLAIN).wait_send()

    def drain(d, carry):
        for flip, ch, cross in steps:
            column = other if flip else y

            @pl.when(z >= d)
            def _():
                rank = 2 * (z - d) + column

                @pl.when(has_up)
                def _():
                    chunk(UP, rank, ch).wait_send()

                if cross:
                    chunk(SIDE, rank, ch).wait_send()

            @pl.when(z + d < n_z)
            def _():
                rank = 2 * (z + d) + column

                @pl.when(has_down)
                def _():
                    chunk(DOWN, rank, ch).wait_send()

                if cross:
                    chunk(SIDE, rank, ch).wait_send()
        return carry

    lax.fori_loop(1, n_z, drain, 0)

    for d in range(1, n_col):
        share(d).wait()
    sums = jnp.sum(jnp.sum(sums_all[...], axis=0), axis=0, keepdims=True)
    factor = float(RB_DEV * n_col * block) / sums

    def scale(i, carry):
        rows = pl.ds(pl.multiple_of(i * block, block), block)
        value = acc[rows, :]
        value = (value * value * factor).astype(jnp.bfloat16)
        for j in range(columns):
            result[j, i] = value[:, j * block:(j + 1) * block]
            pltpu.make_async_copy(result.at[j, i], out_ref.at[j, i], done.at[j, i]).start()
        return carry

    lax.fori_loop(0, RB_DEV, scale, 0)

    def finish(i, carry):
        for j in range(columns):
            pltpu.make_async_copy(result.at[j, i], out_ref.at[j, i], done.at[j, i]).wait()
        return carry

    lax.fori_loop(0, RB_DEV, finish, 0)


def on_device(n_row, n_col, matrix_blocks, matrix_rows, matrix_counts, slab_blocks, slab_inner, slab_counts):
    per_rank, capacity, block = matrix_blocks.shape[0], matrix_blocks.shape[1], matrix_blocks.shape[2]
    columns, slots = slab_blocks.shape[0], slab_blocks.shape[1]
    held = per_rank * capacity
    size = held // CHUNKS
    a = matrix_blocks.reshape(CHUNKS, size, block, block)
    b = slab_blocks.reshape(columns * slots, block, block)
    matrix_counts = matrix_counts.reshape(1, per_rank)
    hbm = pl.BlockSpec(memory_space=pltpu.HBM)
    dma = pltpu.SemaphoreType.DMA
    rows_shape, counts_shape, inner_shape = (
        (n_row,) + matrix_rows.shape, (n_row,) + matrix_counts.shape, (n_col,) + slab_inner.shape)
    return pl.pallas_call(
        functools.partial(step_kernel, n_row, n_col, (columns, slots, per_rank, capacity, block)),
        out_shape=jax.ShapeDtypeStruct((columns, RB_DEV, block, block), jnp.bfloat16),
        in_specs=[hbm, hbm, hbm, hbm, hbm, pl.BlockSpec(memory_space=pltpu.SMEM)],
        out_specs=hbm,
        scratch_shapes=[
            pltpu.VMEM((n_row,) + a.shape, a.dtype),
            pltpu.VMEM((n_col,) + b.shape, b.dtype),
            pltpu.VMEM(rows_shape, jnp.int32),
            pltpu.VMEM(counts_shape, jnp.int32),
            pltpu.VMEM(inner_shape, jnp.int32),
            pltpu.SMEM(rows_shape, jnp.int32),
            pltpu.SMEM(counts_shape, jnp.int32),
            pltpu.SMEM(inner_shape, jnp.int32),
            pltpu.SMEM((n_row * per_rank, RB_DEV), jnp.int32),
            pltpu.SMEM((n_row * per_rank, columns), jnp.int32),
            pltpu.VMEM((CHUNKS // per_rank, size, block, block), a.dtype),
            pltpu.VMEM((block, columns * block), b.dtype),
            pltpu.VMEM((RB_DEV * block, columns * block), jnp.float32),
            pltpu.VMEM((n_col, 8, columns * block), jnp.float32),
            pltpu.VMEM((columns, RB_DEV, block, block), jnp.bfloat16),
            dma((3, n_row, CHUNKS)), dma((n_row, CHUNKS)),
            dma((2, n_col)), dma((2, n_col)), dma((2, n_row)), dma((2, n_row)), dma((n_col,)), dma((n_col,)),
            dma((8,)), dma((columns, RB_DEV)),
        ],
        compiler_params=pltpu.CompilerParams(
            collective_id=0, has_side_effects=True, vmem_limit_bytes=63 << 20),
        name="gather_multiply_normalize",
    )(a, b, matrix_rows, matrix_counts, slab_inner, slab_counts)


LIST = 9
OVER = 3
FIRST = LIST - OVER
SLOTS = LIST + OVER
GRAIN = 16
PARTS = 4
BY_Y = 3
LEVELS = 65535.0


def pair_kernel(n_z, shape, a_ref, b_ref, rows_ref, counts_ref, inner_ref, used_ref, counts_in, used_in, out_ref,
                cand, over, over_in, y_out, a_all, a_par, b_all, right, stage, lhs, acc, result,
                sums_acc, sums_out, sums_all, c_out, c_in, top_out, top_in,
                rows_all, counts_all, counts_par, counts_near, inner_all, used_all,
                rows_s, counts_s, counts_par_s, inner_s, used_s, slot_s, source_s,
                local, ready, near_send, near_recv, z_send, z_recv, y_send, y_recv, o_send, o_recv,
                over_y, x_send, x_recv, p_send, p_recv, b_send, b_recv, m_send, m_recv, c_send, c_recv, s_send, s_recv):
    columns, slots, capacity, block = shape
    half = block // 2
    size = half // GRAIN // PARTS
    grains = half // GRAIN
    wide = columns * block
    r = lax.axis_index("row")
    c = lax.axis_index("col")
    z = lax.div(r, 2)
    y = lax.rem(r, 2)
    x = lax.div(c, 2)
    t = lax.rem(c, 2)
    has_up = z < n_z - 1
    has_down = z > 0
    middle = has_up & has_down
    end = jnp.logical_not(middle)
    c_x = 2 * (1 - x) + t
    c_t = 2 * x + 1 - t
    to_up = {"row": r + 2, "col": c}
    to_down = {"row": r - 2, "col": c}
    to_y = {"row": 2 * z + 1 - y, "col": c}
    to_x = {"row": r, "col": c_x}
    to_core = {"row": r, "col": c_t}

    def span(m):
        return pl.ds(m * size, size)

    def parts(work, first=0, end_at=PARTS):
        def one(m, carry):
            work(m)
            return carry

        lax.fori_loop(first, end_at, one, 0)

    def quarter(work, n):
        parts(work, n * PARTS // 4, (n + 1) * PARTS // 4)

    def remote(src, dst, send_sem, recv_sem, target):
        return pltpu.make_async_remote_copy(
            src_ref=src, dst_ref=dst, send_sem=send_sem, recv_sem=recv_sem,
            device_id=target, device_id_type=MESH)

    near = [(2 * z + (y if d < 4 else 1 - y), lax.rem(c + d, 4)) for d in range(1, 8)]

    barrier = pltpu.get_barrier_semaphore()
    for d in range(1, 2 * n_z):
        pl.semaphore_signal(
            barrier, inc=1, device_id={"row": lax.rem(r + d, 2 * n_z), "col": c}, device_id_type=MESH)
    for d, (row, col) in enumerate(near, 1):
        if d != 4:
            pl.semaphore_signal(barrier, inc=1, device_id={"row": row, "col": col}, device_id_type=MESH)
    pl.semaphore_wait(barrier, 2 * n_z - 1 + 6)

    def give_cand(n):
        return remote(a_ref.at[1 - t, pl.ds(2 * n, 2)], cand.at[pl.ds(t * capacity + 2 * n, 2)],
                      near_send.at[0, n], near_recv.at[0, n], to_core)

    def take_cand(n):
        return remote(a_ref.at[1 - t, pl.ds(2 * n, 2)], cand.at[pl.ds((1 - t) * capacity + 2 * n, 2)],
                      near_send.at[0, n], near_recv.at[0, n], to_core)

    def give_near():
        return remote(counts_ref, counts_near, near_send.at[1, 0], near_recv.at[1, 0], to_core)

    def metas(d):
        target = {"row": lax.rem(r + d, 2 * n_z), "col": c}
        return [remote(rows_ref, rows_all.at[r], m_send.at[0, d], m_recv.at[0, d], target),
                remote(counts_ref, counts_all.at[r], m_send.at[1, d], m_recv.at[1, d], target)]

    def inner_to(d):
        side = 0 if d < 4 else 1
        row, col = near[d - 1]
        return remote(inner_ref, inner_all.at[side, c], m_send.at[2, d], m_recv.at[2, d], {"row": row, "col": col})

    def used_to():
        return remote(used_ref, used_all, m_send.at[3, 0], m_recv.at[3, 0], to_y)

    def par_counts():
        return remote(counts_all, counts_par, m_send.at[3, 1], m_recv.at[3, 1], to_core)

    def slab(side, col, j):
        return b_all.at[side, col, j]

    def slab_copy(way, src, side, col, j, target, first=0, size=slots):
        piece = pl.ds(first, size)
        return remote(src.at[piece], b_all.at[side, col, j, piece], b_send.at[way, side, col, j],
                      b_recv.at[side, col, j], target)

    def slab_own(way, j, first=0, size=slots):
        side, target = {0: (0, to_core), 1: (0, to_x), 2: (1, to_y)}[way]
        return slab_copy(way, b_ref.at[j], side, c, j, target, first, size)

    def slab_core(side, col, j):
        return slab_copy(0, slab(side, col, j), side, col, j, to_core)

    def slab_diag(j, over_x):
        first, size = 0, slots
        if j == 0:
            first, size = (BY_Y, slots - BY_Y) if over_x else (0, BY_Y)
        if over_x:
            return slab_copy(3, slab(1, c, j), 1, c, j, to_x, first, size)
        return slab_copy(3, slab(0, c_x, j), 1, c_x, j, to_y, first, size)

    def slab_wait(side, col, j):
        slab_copy(0, slab(side, col, j), side, col, j, to_core).wait_recv()

    def y_copy(m, tail):
        at, many = ((0, FIRST), (FIRST, OVER))[tail]
        return remote(y_out.at[span(m), pl.ds(at, many)], a_all.at[z, span(m), y, pl.ds(at, many)],
                      y_send.at[m, tail], y_recv.at[m, tail], to_y)

    def y_wait(m, tail):
        at, many = ((0, FIRST), (FIRST, OVER))[tail]
        remote(y_out.at[span(m), pl.ds(at, many)], a_all.at[z, span(m), 1 - y, pl.ds(at, many)],
               y_send.at[m, tail], y_recv.at[m, tail], to_y).wait_recv()

    def y_over(to):
        return remote(y_out.at[:, pl.ds(LIST, OVER)], a_all.at[z, :, to, pl.ds(LIST, OVER)],
                      over_y.at[0], over_y.at[1], to_y)

    def over_copy():
        return remote(over, over_in, o_send, o_recv, to_x)

    def z_first(way, m, side, tail):
        at, many = ((0, FIRST), (FIRST, OVER))[tail]
        piece = a_all.at[z, span(m), side, pl.ds(at, many)]
        return remote(piece, piece, z_send.at[way, z, m, 2 * side + tail], z_recv.at[z, m, tail],
                      (to_up, to_down)[way])

    def z_piece(rank, m, tail):
        return a_all.at[rank, span(m), :, (pl.ds(0, FIRST), pl.ds(FIRST, OVER))[tail]]

    def z_next(way, rank, m, tail):
        piece = z_piece(rank, m, tail)
        return remote(piece, piece, z_send.at[way, rank, m, tail], z_recv.at[rank, m, tail], (to_up, to_down)[way])

    def z_wait(rank, m, tail):
        piece = z_piece(rank, m, tail)
        remote(piece, piece, z_send.at[0, rank, m, tail], z_recv.at[rank, m, tail], to_y).wait_recv()

    def moved(step, act):
        @pl.when(step == 0)
        def _():
            act(0, 1)

        @pl.when(step + 1 < PARTS)
        def _():
            act(step + 1, 1)

        act(step, 0)

    def x_copy(rank, m):
        return remote(a_all.at[rank, span(m), :, pl.ds(FIRST, OVER)], a_all.at[rank, span(m), :, pl.ds(LIST, OVER)],
                      x_send.at[rank, m], x_recv.at[rank, m], to_x)

    def p_copy(rank, m, over_part):
        piece = (rank, span(m), slice(None), (pl.ds(0, FIRST), pl.ds(FIRST, 2 * OVER))[over_part])
        return remote(a_all.at[piece], a_par.at[piece], p_send.at[rank, m, over_part], p_recv.at[rank, m, over_part],
                      to_core)

    def c_copy(m):
        return remote(c_out.at[span(m)], c_in.at[span(m)], c_send.at[m, 0], c_recv.at[m, 0], to_y)

    def top_copy(m):
        return remote(top_out.at[m], top_in.at[m], c_send.at[m, 1], c_recv.at[m, 1], to_y)

    def sums_copy(d):
        row, col = near[d - 1]
        side = 0 if d < 4 else 1
        return remote(sums_out.at[side], sums_all.at[side, c], s_send.at[d], s_recv.at[d], {"row": row, "col": col})

    def both(m, side, tail, act):
        @pl.when(has_up)
        def _():
            act(z_first(0, m, side, tail))

        @pl.when(has_down)
        def _():
            act(z_first(1, m, side, tail))

    def start(copy):
        copy.start()

    def wait_send(copy):
        copy.wait_send()

    def rank_of(n):
        low = z < n_z // 2
        at = jnp.where(low, z, n_z - 1 - z)
        rank = n - 1 + jnp.where(n - 1 >= at, 1, 0)
        rank = jnp.where(low, rank, n_z - 1 - rank)
        return jnp.where(n == 0, z, rank)

    mine = [pltpu.make_async_copy(a_ref.at[t], cand.at[pl.ds(t * capacity, capacity)], local.at[0])]
    give_near().start()
    for n in range(capacity // 2):
        give_cand(n).start()
    mine[0].start()
    slab_own(2, 1, 0, 2).start()
    slab_own(1, 0, 0, 1).start()
    mine += [
        pltpu.make_async_copy(rows_ref, rows_all.at[r], local.at[1]),
        pltpu.make_async_copy(counts_ref, counts_all.at[r], local.at[2]),
        pltpu.make_async_copy(inner_ref, inner_all.at[0, c], local.at[3]),
        pltpu.make_async_copy(b_ref, b_all.at[0, c], local.at[4]),
    ]
    acc[...] = jnp.zeros_like(acc)
    sums_acc[...] = jnp.zeros_like(sums_acc)

    give_near().wait_recv()
    at_rank = lax.broadcasted_iota(jnp.int32, (1, 2), 1)
    near_count = jnp.max(jnp.where(at_rank == t, counts_near[...], 0))
    mine[0].wait()
    for n in range(capacity // 2):
        take_cand(n).wait_recv()

    own_count = counts_in[0, t]
    first_count = jnp.where(t == 0, own_count, near_count)
    total_count = own_count + near_count

    def place(p):
        return jnp.where(p < first_count, p, capacity + jnp.minimum(jnp.maximum(p - first_count, 0), capacity - 1))

    for p in range(OVER):
        over[p] = cand[place(LIST + p)]
    over_copy().start()

    def rows_at(side, m):
        return pl.ds(pl.multiple_of(side * half + m * GRAIN, GRAIN), GRAIN)

    def pack(p, carry):
        at = place(p)
        for g in range(grains):
            a_all[z, g, y, p] = cand[at, rows_at(y, g), :]
            y_out[g, p] = cand[at, rows_at(1 - y, g), :]
        return carry

    def pack_tail(p, carry):
        at = place(FIRST + p)
        keep = total_count > FIRST
        for g in range(grains):
            for side, there in ((y, True), (1 - y, False)):
                value = jnp.where(keep, cand[at, rows_at(side, g), :], over_in[p, rows_at(side, g), :])
                if there:
                    a_all[z, g, y, FIRST + p] = value
                else:
                    y_out[g, FIRST + p] = value
        return carry

    def pack_over(p, carry):
        for g in range(grains):
            a_all[z, g, y, LIST + p] = over[p, rows_at(y, g), :]
            y_out[g, LIST + p] = over[p, rows_at(1 - y, g), :]
        return carry

    lax.fori_loop(0, FIRST, pack, 0)
    def own_main(m):
        y_copy(m, 0).start()
        both(m, y, 0, start)

    def beside_main(m):
        y_wait(m, 0)
        both(m, 1 - y, 0, start)
        p_copy(z, m, 0).start()

    def own_tail(m):
        y_copy(m, 1).start()
        both(m, y, 1, start)

    def beside_tail(m):
        y_wait(m, 1)
        both(m, 1 - y, 1, start)

    parts(own_main)
    slab_own(1, 0, 1, slots - 1).start()
    for j in range(columns):
        slab_own(0, j).start()
    for d in range(1, 2 * n_z):
        for copy in metas(d):
            copy.start()
    for d in range(1, 8):
        inner_to(d).start()
    used_to().start()
    for copy in mine[1:]:
        copy.start()
    lax.fori_loop(0, OVER, pack_over, 0)
    parts(beside_main)
    over_copy().wait_recv()
    lax.fori_loop(0, OVER, pack_tail, 0)
    parts(own_tail)
    slab_own(1, 1).start()
    slab_own(2, 1, 2, slots - 2).start()
    parts(beside_tail)
    slab_own(2, 0).start()

    def relay(n, step):
        rank = rank_of(n)

        def act(m, tail):
            z_wait(rank, m, tail)

            @pl.when((rank < z) & has_up)
            def _():
                z_next(0, rank, m, tail).start()

            @pl.when((rank > z) & has_down)
            def _():
                z_next(1, rank, m, tail).start()

        moved(step, act)
        p_copy(rank, step, 0).start()

    def near_x(m):
        x_copy(rank_of(1), m).start()

        @pl.when(middle)
        def _():
            x_copy(rank_of(2), m).start()

    def near_relay(m):
        relay(1, m)

        @pl.when(middle)
        def _():
            relay(2, m)

    def far_relay(m):
        relay(jnp.where(middle, 3, 2), m)

    def far_x(m):
        x_copy(rank_of(jnp.where(middle, 3, 2)), m).start()

    def table(k, carry):
        rank = lax.div(k, 2)
        kk = lax.rem(k, 2)
        for side in range(2):
            for j in range(columns):
                limit = used_in[0, j] if side == 0 else used_s[0, j]
                q = jnp.int32(-1)
                for n in range(4 * slots):
                    found = (inner_s[side, n // slots, j, n % slots] == k) & (n < limit)
                    q = jnp.where(found, n, q)
                source_s[k, side * columns + j] = q
        base = jnp.where(t == 1, counts_par_s[rank, 0, kk], 0)
        live = counts_s[rank, 0, kk]
        for i in range(RB_DEV):
            p = jnp.int32(-1)
            for n in range(capacity):
                found = (rows_s[rank, kk, n] == i) & (n < live)
                p = jnp.where(found, n + base, p)
            slot_s[k, i] = p
        return carry

    def complete():
        for copy in mine[1:4]:
            copy.wait()
        for d in range(1, 2 * n_z):
            for copy in metas(d):
                copy.wait()
        par_counts().start()
        for d in range(1, 8):
            inner_to(d).wait()
        used_to().wait()
        par_counts().wait()
        for n, (src, dst) in enumerate((
                (rows_all, rows_s), (counts_all, counts_s), (counts_par, counts_par_s), (inner_all, inner_s),
                (used_all, used_s))):
            pltpu.make_async_copy(src, dst, ready.at[n]).start()
        for n, (src, dst) in enumerate((
                (rows_all, rows_s), (counts_all, counts_s), (counts_par, counts_par_s), (inner_all, inner_s),
                (used_all, used_s))):
            pltpu.make_async_copy(src, dst, ready.at[n]).wait()
        lax.fori_loop(0, 4 * n_z, table, 0)

    def give_core(rank, m):
        x_copy(rank, m).wait_recv()
        p_copy(rank, m, 1).start()

    def near_core(m):
        give_core(rank_of(1), m)

        @pl.when(middle)
        def _():
            give_core(rank_of(2), m)

    def slab_next(side, col, j):
        slab_wait(side, col, j)
        slab_core(side, col, j).start()

    def forward(m):
        near_x(m)
        far_x(m)

    slab_next(0, c_x, 0)
    slab_diag(0, False).start()
    parts(near_relay)
    slab_next(1, c, 1)
    slab_diag(1, True).start()
    slab_next(0, c_x, 1)
    complete()
    quarter(far_relay, 0)
    slab_next(1, c, 0)
    slab_diag(0, True).start()
    y_over(y).start()
    quarter(far_relay, 1)
    slab_next(1, c_x, 1)
    quarter(forward, 0)
    slab_next(1, c_x, 0)
    quarter(forward, 1)
    quarter(far_relay, 2)

    mine[4].wait()
    for j in range(columns):
        for side in range(2):
            for col in (c_t, 2 * (1 - x) + 1 - t):
                slab_wait(side, col, j)

    def gather_right(n, carry):
        rank = lax.div(n, 4)
        side = lax.rem(lax.div(n, 2), 2)
        u = lax.rem(n, 2)
        k = 2 * (2 * rank + side) + jnp.where(u == 0, t, 1 - t)
        rows = pl.ds(pl.multiple_of(lax.rem(n, 4) * block, block), block)
        for s in range(2):
            for j in range(columns):
                q = source_s[k, s * columns + j]
                at = jnp.maximum(q, 0)
                value = b_all[s, lax.div(at, slots), j, lax.rem(at, slots)]
                to = (s * columns + j) * block
                right[rank, rows, to:to + block] = jnp.where(q >= 0, value, jnp.zeros_like(value))
        return carry

    lax.fori_loop(0, 4 * n_z, gather_right, 0)

    tall = RB_DEV * GRAIN

    def multiply(rank, m):
        p_copy(rank, m, 0).wait_recv()
        p_copy(rank, m, 1).wait_recv()
        for g in range(size):
            for u, source in enumerate((a_all, a_par)):
                for side in range(2):
                    stage[u, side, g] = source[rank, m * size + g, side]
        for side in range(2):
            for u in range(2):
                k = 2 * (2 * rank + side) + (t if u == 0 else 1 - t)
                at = (2 * side + u) * block
                for i in range(RB_DEV):
                    p = slot_s[k, i]
                    for g in range(size):
                        value = stage[u, side, g, jnp.maximum(p, 0)]
                        to = g * tall + i * GRAIN
                        lhs[to:to + GRAIN, at:at + block] = jnp.where(p >= 0, value, jnp.zeros_like(value))
        for n in range(2):
            cols = slice(n * wide, (n + 1) * wide)
            product = jnp.dot(lhs[...], right[rank, :, cols], preferred_element_type=jnp.float32)
            acc[span(m), :, cols] += product.reshape(size, tall, wide)

    def cores(m):
        near_core(m)
        give_core(rank_of(jnp.where(middle, 3, 2)), m)

    def last_relay(m):
        rank = rank_of(3)

        def act(n, tail):
            z_wait(rank, n, tail)
            if tail:
                x_copy(rank, n).start()

        moved(m, act)
        p_copy(rank, m, 0).start()
        give_core(rank, m)

    def finish_part(m):
        for n in range(2):
            value = acc[span(m), :, n * wide:(n + 1) * wide]
            squared = value * value
            sums_acc[n] += jnp.sum(squared.reshape(-1, 8, wide), axis=0)

        @pl.when(m + 1 == PARTS)
        def _():
            for n in range(2):
                sums_out[n] = jnp.sum(sums_acc[n], axis=0, keepdims=True)
            for d in range(1, 8):
                sums_copy(d).start()

        value = acc[span(m), :, wide:].reshape(-1, wide)
        top = jnp.maximum(jnp.max(value, axis=0, keepdims=True), 1e-30)
        scaled = value * (LEVELS / top) + 0.5
        coded = jnp.minimum(scaled, LEVELS).astype(jnp.int32)
        word = lax.shift_left(coded[:, :block], jnp.int32(16)) | coded[:, block:]
        c_out[span(m)] = word.reshape(size, tall, block)
        top_out[m] = top
        top_copy(m).start()
        c_copy(m).start()

    quarter(forward, 2)
    quarter(far_relay, 3)
    quarter(forward, 3)
    y_over(1 - y).wait_recv()
    parts(lambda m: p_copy(z, m, 1).start())
    cores(0)

    def drain_start():
        give_near().wait_send()
        for n in range(capacity // 2):
            give_cand(n).wait_send()
        over_copy().wait_send()
        y_over(y).wait_send()
        for way in range(3):
            for j in range(columns):
                slab_own(way, j).wait_send()
        for j in range(columns):
            slab_diag(j, True).wait_send()
            if j == 0:
                slab_diag(j, False).wait_send()
            for side, col in ((0, c_x), (1, c), (1, c_x)):
                slab_core(side, col, j).wait_send()

    def drain_rank(rank, m):
        p_copy(rank, m, 0).wait_send()
        p_copy(rank, m, 1).wait_send()

        @pl.when(rank != z)
        def _():
            x_copy(rank, m).wait_send()

    def drain_part(m):
        for tail in range(2):
            y_copy(m, tail).wait_send()
            both(m, 0, tail, wait_send)
            both(m, 1, tail, wait_send)

        def one(n, carry):
            drain_rank(rank_of(n), m)
            return carry

        lax.fori_loop(0, 3, one, 0)

    def drain_last(m):
        drain_rank(rank_of(3), m)
        c_copy(m).wait_send()
        top_copy(m).wait_send()

        @pl.when(middle)
        def _():
            def one(rank, carry):
                for tail in range(2):
                    @pl.when((rank < z) & has_up)
                    def _():
                        z_next(0, rank, m, tail).wait_send()

                    @pl.when((rank > z) & has_down)
                    def _():
                        z_next(1, rank, m, tail).wait_send()
                return carry

            lax.fori_loop(0, n_z, one, 0)

    def one_part(m):
        @pl.when(m + 1 < PARTS)
        def _():
            cores(m + 1)

        def one_rank(n, carry):
            @pl.when((n == 3) & end)
            def _():
                last_relay(m)

            multiply(rank_of(jnp.where(n == 3, 3, lax.rem(n + 1, 3))), m)
            return carry

        lax.fori_loop(0, 4, one_rank, 0)
        finish_part(m)

        @pl.when(m + 1 < PARTS)
        def _():
            @pl.when(m == 0)
            def _():
                drain_start()

            drain_part(m)

    parts(one_part)
    drain_part(PARTS - 1)

    for d in range(1, 8):
        sums_copy(d).wait()
    sums = sums_out[0]
    for d in range(1, 8):
        sums = sums + sums_all[0 if d < 4 else 1, near[d - 1][1]]
    factor = float(RB_DEV * 4 * block) / sums

    def store(value, g, side):
        value = value.astype(jnp.bfloat16)
        for i in range(RB_DEV):
            for j in range(columns):
                result[j, i, rows_at(side, g), :] = value[i * GRAIN:(i + 1) * GRAIN, j * block:(j + 1) * block]

    def scale_own(g, carry):
        value = acc[g, :, :wide]
        store(value * value * factor, g, y)
        return carry

    def out_half():
        rows = pl.ds(pl.multiple_of(y * half, half), half)
        return pltpu.make_async_copy(result.at[:, :, rows], out_ref.at[:, :, rows], local.at[6])

    def out_part(m):
        rows = pl.ds(pl.multiple_of((1 - y) * half + m * size * GRAIN, GRAIN), size * GRAIN)
        return pltpu.make_async_copy(result.at[:, :, rows], out_ref.at[:, :, rows], local.at[7 + m])

    lax.fori_loop(0, grains, scale_own, 0)
    out_half().start()
    def scale_other(m):
        c_copy(m).wait_recv()
        top_copy(m).wait_recv()
        step = top_in[m] * (1.0 / LEVELS)

        def one(g, carry):
            word = c_in[g]
            upper = lax.shift_right_logical(word, jnp.int32(16)).astype(jnp.float32)
            lower = (word & jnp.int32(65535)).astype(jnp.float32)
            value = jnp.concatenate([upper, lower], axis=1) * step
            store(value * value * factor, g, 1 - y)
            return carry

        lax.fori_loop(m * size, (m + 1) * size, one, 0)
        out_part(m).start()

    parts(scale_other)
    parts(drain_last)
    out_half().wait()
    parts(lambda m: out_part(m).wait())


def paired(n_z, matrix_blocks, matrix_rows, matrix_counts, slab_blocks, slab_inner, slab_counts):
    capacity, block = matrix_blocks.shape[1], matrix_blocks.shape[2]
    columns, slots = slab_blocks.shape[0], slab_blocks.shape[1]
    grains = block // 2 // GRAIN
    counts = matrix_counts.reshape(1, 2)
    used = slab_counts.reshape(1, columns)
    hbm = pl.BlockSpec(memory_space=pltpu.HBM)
    smem = pl.BlockSpec(memory_space=pltpu.SMEM)
    dma = pltpu.SemaphoreType.DMA
    half_word, full = jnp.bfloat16, jnp.float32
    rows_shape, counts_shape, inner_shape = (2 * n_z, 2, capacity), (2 * n_z, 1, 2), (2, 4) + slab_inner.shape
    lists = (n_z, grains, 2, SLOTS, GRAIN, block)
    parts, most = PARTS, grains // PARTS
    vmem = [
        ((2 * capacity, block, block), half_word),
        ((OVER, block, block), half_word),
        ((OVER, block, block), half_word),
        ((grains, SLOTS, GRAIN, block), half_word),
        (lists, half_word),
        (lists, half_word),
        ((2, 4) + slab_blocks.shape, half_word),
        ((n_z, 4 * block, 2 * columns * block), half_word),
        ((2, 2, most, SLOTS, GRAIN, block), half_word),
        ((most * RB_DEV * GRAIN, 4 * block), half_word),
        ((grains, RB_DEV * GRAIN, 2 * columns * block), full),
        ((columns, RB_DEV, block, block), half_word),
        ((2, 8, columns * block), full),
        ((2, 1, columns * block), full),
        ((2, 4, 1, columns * block), full),
        ((grains, RB_DEV * GRAIN, block), jnp.int32),
        ((grains, RB_DEV * GRAIN, block), jnp.int32),
        ((parts, 1, columns * block), full),
        ((parts, 1, columns * block), full),
        (rows_shape, jnp.int32), (counts_shape, jnp.int32), (counts_shape, jnp.int32), ((1, 2), jnp.int32),
        (inner_shape, jnp.int32), ((1, columns), jnp.int32),
    ]
    words = [rows_shape, counts_shape, counts_shape, inner_shape, (1, columns),
             (4 * n_z, RB_DEV), (4 * n_z, 2 * columns)]
    sems = [(7 + parts,), (5,), (2, capacity // 2), (2, capacity // 2), (2, n_z, parts, 4), (n_z, parts, 2), (parts, 2), (parts, 2), None, None, (2,),
            (n_z, parts), (n_z, parts), (n_z, parts, 2), (n_z, parts, 2), (4, 2, 4, columns), (2, 4, columns),
            (4, 2 * n_z), (4, 2 * n_z), (parts, 2), (parts, 2), (8,), (8,)]
    return pl.pallas_call(
        functools.partial(pair_kernel, n_z, (columns, slots, capacity, block)),
        out_shape=jax.ShapeDtypeStruct((columns, RB_DEV, block, block), jnp.bfloat16),
        in_specs=[hbm] * 6 + [smem] * 2,
        out_specs=pl.BlockSpec(memory_space=pl.ANY),
        scratch_shapes=[pltpu.VMEM(s, d) for s, d in vmem] + [pltpu.SMEM(s, jnp.int32) for s in words]
        + [dma if s is None else dma(s) for s in sems],
        compiler_params=pltpu.CompilerParams(
            collective_id=1, has_side_effects=True, vmem_limit_bytes=44 << 20),
        name="packed_pair_multiply",
    )(*[pltpu.with_memory_space_constraint(v, pltpu.HBM) for v in (
        matrix_blocks, slab_blocks, matrix_rows, counts, slab_inner, used)], counts, used)


def choose(n_row, n_col, *args):
    if n_row == 8 and n_col == 4 and args[0].shape[0] == 2 and args[0].shape[1] == SLOTS // 2:
        return paired(n_row // 2, *args)
    return on_device(n_row, n_col, *args)


def solution(mesh):
    return jax.shard_map(
        functools.partial(choose, mesh.shape["row"], mesh.shape["col"]),
        mesh=mesh,
        in_specs=(
            P("row", "col", None, None),
            P("row", "col"),
            P("row", "col"),
            P("row", "col", None, None),
            P("row", "col"),
            P("row"),
        ),
        out_specs=P("row", "col", None, None),
        check_vma=False,
    )
```
